32 devices in a mesh: tm: 8 (over y, x, core), rows: 4 (over z).
Axes of the slice: x: 2, y: 2, z: 4, core: 2. Of those that a mesh axis runs over, the one named last changes fastest.
Arguments:
- event_slices: bfloat16 [8, 32, 160, 256], P('tm', 'rows'), may hold values from -6 to 6
- frame_features: bfloat16 [8, 32, 160, 256], P('tm', 'rows'), may hold values from -6 to 6
- exposure_start: int32 [8], P('tm'), may hold values from 0 to 7, as said below
- exposure_end: int32 [8], P('tm'), may hold values from 0 to 7, as said below
- intersection_us: int32 [8, 5], P('tm'), may hold values from 1 to 1000
- conv_first: bfloat16 [3, 3, 256, 256], replicated, may hold values from -0.125 to 0.125
- conv_second: bfloat16 [3, 3, 256, 256], replicated, may hold values from -0.125 to 0.125
- conv_frame: bfloat16 [3, 3, 256, 256], replicated, may hold values from -0.125 to 0.125
Outputs:
- frame_out: bfloat16 [8, 32, 160, 256], P('tm', 'rows')
The draws below stay inside these ranges and needn't reach their ends.
Inputs may be any that keep to these rules, and one draw needn't show every extreme that they name: exposure_start[f] lies between f - 2 and f. exposure_end[f] lies between f and f + 2.
All inputs are finite; a program needn't handle non-finite values.
Results may differ from the reference program's by a relative error of at most 0.014.
Values may be sent and summed in bfloat16 or wider, within the bound.
No kernel may reach another device: no remote copies, remote signals or barrier semaphores. Data moves between devices by JAX's collectives and lax.ppermute only.
A program may use at most 128 MiB of HBM per device.

```python
import jax
import jax.numpy as jnp
from jax import lax

C = 256
COLS = 160
RADIUS = 2
SPAN = 5
SLICES = 8
FRAMES = 8
HEIGHT = 32


def draw_exposure_start(key, part):
    offsets = jax.random.randint(jax.random.fold_in(key, 11), (FRAMES,), 0, RADIUS + 1)
    offsets = offsets.at[FRAMES // 2].set(RADIUS)
    offsets = offsets.at[FRAMES - 1].set(0)
    return jnp.maximum(jnp.arange(FRAMES, dtype=jnp.int32) - offsets, 0).astype(jnp.int32)


def draw_exposure_end(key, part):
    offsets = jax.random.randint(jax.random.fold_in(key, 23), (FRAMES,), 0, RADIUS + 1)
    offsets = offsets.at[FRAMES // 2].set(RADIUS)
    offsets = offsets.at[0].set(0)
    return jnp.minimum(jnp.arange(FRAMES, dtype=jnp.int32) + offsets, FRAMES - 1).astype(jnp.int32)


def plant(result, rng, low, high):
    extent = result.shape
    index_at = [jax.random.randint(jax.random.fold_in(rng, axis), (), 0, extent[axis]) for axis in range(len(extent))]
    result = result.at[tuple(index_at)].set(low)
    longest = extent.index(max(extent))
    index_at[longest] = (index_at[longest] + 1) % extent[longest]
    return result.at[tuple(index_at)].set(high)


def steps_of(stream_key, dims, split, low, high):
    def one(position, blocks):
        draws = jax.random.uniform(jax.random.fold_in(jax.random.fold_in(stream_key, 6), position), (blocks,), jnp.float32, low / len(split), high / len(split))
        return jnp.repeat(jnp.exp(draws), dims[position] // blocks).reshape((-1,) + (1,) * (len(dims) - position - 1))

    loudness = one(*split[0])
    for cut in split[1:]:
        loudness = loudness * one(*cut)
    return loudness


def noise(stream_key, dims, spread, bound, cuts=(), kind=jnp.bfloat16):
    loudness = steps_of(stream_key, dims, cuts, -0.22, 0.18) if cuts else 1.0
    entries = jax.random.normal(stream_key, dims, jnp.float32) * spread * loudness
    return jnp.minimum(jnp.maximum(entries, -bound), bound).astype(kind)


def setup_inputs(seed: int = 0) -> dict:
    seeds = jax.random.split(jax.random.key(seed), 9)
    return {
        "event_slices": noise(seeds[0], (SLICES, HEIGHT, COLS, C), 1.0, 6.0, ((0, 8), (1, 4))),
        "frame_features": noise(seeds[1], (FRAMES, HEIGHT, COLS, C), 1.0, 6.0, ((0, 8), (1, 4))),
        "exposure_start": draw_exposure_start(jax.random.fold_in(seeds[8], 71), 0),
        "exposure_end": draw_exposure_end(jax.random.fold_in(seeds[8], 71), 0),
        "intersection_us": plant(jax.random.randint(seeds[4], (FRAMES, SPAN), 1, 1001), jax.random.fold_in(seeds[4], 1), 1, 1000).astype(jnp.int32),
        "conv_first": noise(seeds[5], (3, 3, C, C), (9 * C) ** -0.5, 0.125),
        "conv_second": noise(seeds[6], (3, 3, C, C), (9 * C) ** -0.5, 0.125),
        "conv_frame": noise(seeds[7], (3, 3, C, C), (9 * C) ** -0.5, 0.125),
    }


def conv_same(image, kernel):
    return lax.conv_general_dilated(image[None].astype(jnp.float32), kernel.astype(jnp.float32), (1, 1), ((1, 1), (1, 1)), dimension_numbers=("NHWC", "HWIO", "NHWC"), precision=lax.Precision.HIGHEST)[0]


def reference(event_slices, frame_features, exposure_start, exposure_end, intersection_us, conv_first, conv_second, conv_frame):
    def slice_layers(image):
        first_layer = jax.nn.gelu(conv_same(image, conv_first), approximate=True).astype(jnp.bfloat16)
        return jax.nn.gelu(conv_same(first_layer, conv_second), approximate=True).astype(jnp.bfloat16)

    features = lax.map(slice_layers, event_slices)
    frame_ids = jnp.arange(FRAMES, dtype=jnp.int32)
    slice_index = frame_ids[:, None] + jnp.arange(SPAN, dtype=jnp.int32)[None, :] - RADIUS
    valid = (slice_index >= exposure_start[:, None]) & (slice_index <= exposure_end[:, None])
    weights = jnp.where(valid, intersection_us.astype(jnp.float32), jnp.float32(0.0))
    totals = jnp.sum(weights, axis=1)

    def frame_mix(packed):
        frame_index, weight_row, weight_total, feature = packed
        summed = jnp.zeros(feature.shape, jnp.float32)
        for offset in range(SPAN):
            source = jnp.clip(frame_index + offset - RADIUS, 0, SLICES - 1).astype(jnp.int32)
            picked = lax.dynamic_index_in_dim(features, source, 0, keepdims=False)
            summed = summed + weight_row[offset] * picked.astype(jnp.float32)
        mixed_frame = (summed / weight_total * feature.astype(jnp.float32)).astype(jnp.bfloat16)
        return conv_same(mixed_frame, conv_frame).astype(jnp.bfloat16)

    return lax.map(frame_mix, (frame_ids, weights, totals, frame_features))
```

```python
import jax
import jax.numpy as jnp
from jax import lax
from jax.sharding import PartitionSpec as P


def shifted(value, axis, steps):
    count = lax.axis_size(axis)
    initial, last = (max(0, -steps), min(count, count - steps))
    pairs = [(source, source + steps) for source in range(initial, last)]
    if not pairs:
        return jnp.zeros_like(value)
    return lax.ppermute(value, axis, pairs)


def local_conv(padded, kernel):
    return lax.conv_general_dilated(
        padded[None],
        kernel,
        (1, 1),
        ((0, 0), (1, 1)),
        dimension_numbers=("NHWC", "HWIO", "NHWC"),
        preferred_element_type=jnp.float32,
    )[0]


def inside_rows(count, first_row, height):
    rows = first_row + jnp.arange(count, dtype=jnp.int32)
    return ((rows >= 0) & (rows < height))[:, None, None]


def shards(
    event_slices,
    frame_features,
    exposure_start,
    exposure_end,
    intersection_us,
    conv_first,
    conv_second,
    conv_frame,
):
    image = event_slices[0]
    frame = frame_features[0]
    block = image.shape[0]
    height = block * lax.axis_size("rows")
    row0 = lax.axis_index("rows") * block

    down = jnp.concatenate([image[block - 3 :], frame[block - 1 :]], axis=0)
    up = jnp.concatenate([image[:3], frame[:1]], axis=0)
    from_above = shifted(down, "rows", 1)
    from_below = shifted(up, "rows", -1)
    image_ext = jnp.concatenate([from_above[:3], image, from_below[:3]], axis=0)
    frame_ext = jnp.concatenate([from_above[3:], frame, from_below[3:]], axis=0)

    first = jax.nn.gelu(local_conv(image_ext, conv_first), approximate=True)
    first = jnp.where(inside_rows(block + 4, row0 - 2, height), first, 0.0).astype(jnp.bfloat16)
    second = jax.nn.gelu(local_conv(first, conv_second), approximate=True).astype(jnp.bfloat16)

    frame_index = lax.axis_index("tm")
    intersection = intersection_us[0].astype(jnp.float32)
    window = intersection.shape[0]
    radius = (window - 1) // 2
    slice_index = frame_index + jnp.arange(window, dtype=jnp.int32) - radius
    valid = (slice_index >= exposure_start[0]) & (slice_index <= exposure_end[0])
    frame_weights = jnp.where(valid, intersection, jnp.float32(0.0))
    scaled = frame_weights / jnp.sum(frame_weights)

    summed = scaled[radius] * second.astype(jnp.float32)
    for offset in range(window):
        if offset != radius:
            arrived = shifted(second, "tm", radius - offset)
            summed = summed + scaled[offset] * arrived.astype(jnp.float32)
    mixed = (summed * frame_ext.astype(jnp.float32)).astype(jnp.bfloat16)
    result = local_conv(mixed, conv_frame).astype(jnp.bfloat16)
    return result[None]


def solution(mesh):
    return jax.shard_map(
        shards,
        mesh=mesh,
        in_specs=(
            P("tm", "rows", None, None),
            P("tm", "rows", None, None),
            P("tm"),
            P("tm"),
            P("tm", None),
            P(),
            P(),
            P(),
        ),
        out_specs=P("tm", "rows", None, None),
        check_vma=False,
    )
```

```python
import jax
import jax.numpy as jnp
from jax import lax
from jax.sharding import PartitionSpec as P


def shifted(value, axis, steps):
    count = lax.axis_size(axis)
    initial, last = (max(0, -steps), min(count, count - steps))
    pairs = [(source, source + steps) for source in range(initial, last)]
    if not pairs:
        return jnp.zeros_like(value)
    return lax.ppermute(value, axis, pairs)


def local_conv(padded, kernel):
    return lax.conv_general_dilated(
        padded[None],
        kernel,
        (1, 1),
        ((0, 0), (1, 1)),
        dimension_numbers=("NHWC", "HWIO", "NHWC"),
        preferred_element_type=jnp.float32,
    )[0]


def inside_rows(count, first_row, height):
    rows = first_row + jnp.arange(count, dtype=jnp.int32)
    return ((rows >= 0) & (rows < height))[:, None, None]


def shards(
    event_slices,
    frame_features,
    exposure_start,
    exposure_end,
    intersection_us,
    conv_first,
    conv_second,
    conv_frame,
):
    image = event_slices[0]
    frame = frame_features[0]
    block = image.shape[0]
    height = block * lax.axis_size("rows")
    row0 = lax.axis_index("rows") * block

    down = jnp.concatenate([image[block - 3 :], frame[block - 1 :]], axis=0)
    up = jnp.concatenate([image[:3], frame[:1]], axis=0)
    from_above = shifted(down, "rows", 1)
    from_below = shifted(up, "rows", -1)
    image_ext = jnp.concatenate([from_above[:3], image, from_below[:3]], axis=0)
    frame_ext = jnp.concatenate([from_above[3:], frame, from_below[3:]], axis=0)

    first = jax.nn.gelu(local_conv(image_ext, conv_first), approximate=True)
    first = jnp.where(inside_rows(block + 4, row0 - 2, height), first, 0.0).astype(jnp.bfloat16)
    second = jax.nn.gelu(local_conv(first, conv_second), approximate=True).astype(jnp.bfloat16)

    count = lax.axis_size("tm")
    t = lax.axis_index("tm")
    window = intersection_us.shape[1]
    radius = (window - 1) // 2
    frames = jnp.arange(count, dtype=jnp.int32)[:, None]
    slice_index = frames + jnp.arange(window, dtype=jnp.int32)[None, :] - radius
    valid = (slice_index >= exposure_start[:, None]) & (slice_index <= exposure_end[:, None])
    weights = jnp.where(valid, intersection_us.astype(jnp.float32), jnp.float32(0.0))
    weights = weights / jnp.sum(weights, axis=1, keepdims=True)

    partner = lax.ppermute(second, "tm", [(i, i ^ 1) for i in range(count)])
    odd = (t % 2).astype(jnp.float32)
    even = 1.0 - odd
    own32 = second.astype(jnp.float32)
    partner32 = partner.astype(jnp.float32)
    ahead = weights[jnp.minimum(t + 2, count - 1)]
    behind = weights[jnp.maximum(t - 2, 0)]
    to_ahead = (ahead[0] * own32 + (even * ahead[1]) * partner32).astype(jnp.bfloat16)
    to_behind = (behind[4] * own32 + (odd * behind[3]) * partner32).astype(jnp.bfloat16)
    from_behind = shifted(to_ahead, "tm", 2)
    from_ahead = shifted(to_behind, "tm", -2)
    mine = weights[t]
    partner_weight = odd * mine[1] + even * mine[3]
    summed = (
        mine[2] * own32
        + partner_weight * partner32
        + from_behind.astype(jnp.float32)
        + from_ahead.astype(jnp.float32)
    )
    mixed = (summed * frame_ext.astype(jnp.float32)).astype(jnp.bfloat16)
    result = local_conv(mixed, conv_frame).astype(jnp.bfloat16)
    return result[None]


def solution(mesh):
    return jax.shard_map(
        shards,
        mesh=mesh,
        in_specs=(
            P("tm", "rows", None, None),
            P("tm", "rows", None, None),
            P(),
            P(),
            P(),
            P(),
            P(),
            P(),
        ),
        out_specs=P("tm", "rows", None, None),
        check_vma=False,
    )
```

```python
import jax
import jax.numpy as jnp
from jax import lax
from jax.sharding import PartitionSpec as P


def shifted(value, axis, steps):
    count = lax.axis_size(axis)
    initial, last = (max(0, -steps), min(count, count - steps))
    pairs = [(source, source + steps) for source in range(initial, last)]
    if not pairs:
        return jnp.zeros_like(value)
    return lax.ppermute(value, axis, pairs)


def local_conv(padded, kernel):
    return lax.conv_general_dilated(
        padded[None],
        kernel,
        (1, 1),
        ((0, 0), (1, 1)),
        dimension_numbers=("NHWC", "HWIO", "NHWC"),
        preferred_element_type=jnp.float32,
    )[0]


def inside_rows(count, first_row, height):
    rows = first_row + jnp.arange(count, dtype=jnp.int32)
    return ((rows >= 0) & (rows < height))[:, None, None]


def shards(
    event_slices,
    frame_features,
    exposure_start,
    exposure_end,
    intersection_us,
    conv_first,
    conv_second,
    conv_frame,
):
    image = event_slices[0]
    frame = frame_features[0]
    block = image.shape[0]
    height = block * lax.axis_size("rows")
    row0 = lax.axis_index("rows") * block

    down = jnp.concatenate([image[block - 3 :], frame[block - 1 :]], axis=0)
    up = jnp.concatenate([image[:3], frame[:1]], axis=0)
    from_above = shifted(down, "rows", 1)
    from_below = shifted(up, "rows", -1)
    image_ext = jnp.concatenate([from_above[:3], image, from_below[:3]], axis=0)
    frame_ext = jnp.concatenate([from_above[3:], frame, from_below[3:]], axis=0)

    first = jax.nn.gelu(local_conv(image_ext, conv_first), approximate=True)
    first = jnp.where(inside_rows(block + 4, row0 - 2, height), first, 0.0).astype(jnp.bfloat16)
    second = jax.nn.gelu(local_conv(first, conv_second), approximate=True).astype(jnp.bfloat16)

    count = lax.axis_size("tm")
    t = lax.axis_index("tm")
    intersection = intersection_us[0].astype(jnp.float32)
    window = intersection.shape[0]
    radius = (window - 1) // 2
    slice_index = t + jnp.arange(window, dtype=jnp.int32) - radius
    valid = (slice_index >= exposure_start[0]) & (slice_index <= exposure_end[0])
    weights = jnp.where(valid, intersection, jnp.float32(0.0))
    weights = weights / jnp.sum(weights)

    swap = [(i, i ^ 1) for i in range(count)]
    partner = lax.ppermute(second, "tm", swap)
    from_behind = shifted(second, "tm", 2)
    from_ahead = shifted(second, "tm", -2)
    odd = t % 2
    forward = jnp.where(odd == 1, from_behind, from_ahead)
    relayed = lax.ppermute(forward, "tm", swap)
    even_f = (1 - odd).astype(jnp.float32)
    odd_f = odd.astype(jnp.float32)
    summed = (
        weights[0] * from_behind.astype(jnp.float32)
        + (even_f * weights[1] + odd_f * weights[3]) * relayed.astype(jnp.float32)
        + weights[2] * second.astype(jnp.float32)
        + (even_f * weights[3] + odd_f * weights[1]) * partner.astype(jnp.float32)
        + weights[4] * from_ahead.astype(jnp.float32)
    )
    mixed = (summed * frame_ext.astype(jnp.float32)).astype(jnp.bfloat16)
    result = local_conv(mixed, conv_frame).astype(jnp.bfloat16)
    return result[None]


def solution(mesh):
    return jax.shard_map(
        shards,
        mesh=mesh,
        in_specs=(
            P("tm", "rows", None, None),
            P("tm", "rows", None, None),
            P("tm"),
            P("tm"),
            P("tm", None),
            P(),
            P(),
            P(),
        ),
        out_specs=P("tm", "rows", None, None),
        check_vma=False,
    )
```

```python
import numpy as np
import jax
import jax.numpy as jnp
from jax import lax
from jax.experimental import pallas as pl
from jax.experimental.pallas import tpu as pltpu
from jax.sharding import PartitionSpec as P


def shifted(value, axis, steps):
    count = lax.axis_size(axis)
    initial, last = (max(0, -steps), min(count, count - steps))
    pairs = [(source, source + steps) for source in range(initial, last)]
    if not pairs:
        return jnp.zeros_like(value)
    return lax.ppermute(value, axis, pairs)


def gelu(v):
    c = np.float32(np.sqrt(2 / np.pi))
    return v * (0.5 * (1.0 + jnp.tanh(c * (v + 0.044715 * (v * v * v)))))


def conv_rows(x, w_ref, rows_out):
    cols, cin = x.shape[1], x.shape[2]
    cout = w_ref.shape[3]
    m = rows_out * cols
    taps = []
    for b in range(3):
        acc = None
        for a in range(3):
            d = jnp.dot(x[a : a + rows_out].reshape(m, cin), w_ref[a, b],
                        preferred_element_type=jnp.float32)
            acc = d if acc is None else acc + d
        taps.append(acc)
    col = lax.broadcasted_iota(jnp.int32, (rows_out, cols, cout), 1).reshape(m, cout)
    left = pltpu.roll(taps[0], shift=1, axis=0)
    right = pltpu.roll(taps[2], shift=m - 1, axis=0)
    out = taps[1] + jnp.where(col == 0, 0.0, left) + jnp.where(col == cols - 1, 0.0, right)
    return out.reshape(rows_out, cols, cout)


def layers_kernel(bounds_ref, above_ref, image_ref, below_ref, w1_ref, w2_ref, out_ref, xbuf):
    halo = below_ref.shape[0] - 1
    block = image_ref.shape[0]
    xbuf[0:halo] = above_ref[0:halo]
    xbuf[halo : halo + block] = image_ref[...]
    xbuf[halo + block :] = below_ref[0:halo]
    rows1 = block + 2 * halo - 2
    first = gelu(conv_rows(xbuf[...], w1_ref, rows1))
    row = lax.broadcasted_iota(jnp.int32, first.shape, 0)
    inside = (row >= bounds_ref[0]) & (row < bounds_ref[1])
    first = jnp.where(inside, first, 0.0).astype(jnp.bfloat16)
    out_ref[...] = gelu(conv_rows(first, w2_ref, rows1 - 2)).astype(jnp.bfloat16)


def mix_kernel(coef_ref, fb_ref, rel_ref, own_ref, par_ref, fa_ref, above_ref, frame_ref,
               below_ref, w3_ref, out_ref, fbuf):
    halo = below_ref.shape[0] - 1
    block = frame_ref.shape[0]
    fbuf[0:1] = above_ref[halo : halo + 1]
    fbuf[1 : block + 1] = frame_ref[...]
    fbuf[block + 1 :] = below_ref[halo : halo + 1]
    f32 = jnp.float32
    summed = (
        coef_ref[0] * fb_ref[...].astype(f32)
        + coef_ref[1] * rel_ref[...].astype(f32)
        + coef_ref[2] * own_ref[...].astype(f32)
        + coef_ref[3] * par_ref[...].astype(f32)
        + coef_ref[4] * fa_ref[...].astype(f32)
    )
    mixed = (summed * fbuf[...].astype(f32)).astype(jnp.bfloat16)
    out_ref[...] = conv_rows(mixed, w3_ref, block).astype(jnp.bfloat16)


def vmem():
    return pl.BlockSpec(memory_space=pltpu.VMEM)


def smem():
    return pl.BlockSpec(memory_space=pltpu.SMEM)


def layers(bounds, above, image, below, w1, w2):
    block, cols, c = image.shape
    halo = below.shape[0] - 1
    rows = block + 2 * halo
    flops = 2 * 9 * c * c * cols * (2 * rows - 6)
    return pl.pallas_call(
        layers_kernel,
        out_shape=jax.ShapeDtypeStruct((rows - 4, cols, c), jnp.bfloat16),
        in_specs=[smem()] + [vmem()] * 5,
        out_specs=vmem(),
        scratch_shapes=[pltpu.VMEM((rows, cols, c), jnp.bfloat16)],
        cost_estimate=pl.CostEstimate(flops=flops, transcendentals=2 * rows * cols * c,
                                      bytes_accessed=4 * rows * cols * c + 4 * 9 * c * c),
    )(bounds, above, image, below, w1, w2)


def mix(coef, fb, rel, own, par, fa, above, frame, below, w3):
    block, cols, c = frame.shape
    flops = 2 * 9 * c * c * cols * block
    return pl.pallas_call(
        mix_kernel,
        out_shape=jax.ShapeDtypeStruct((block, cols, c), jnp.bfloat16),
        in_specs=[smem()] + [vmem()] * 9,
        out_specs=vmem(),
        scratch_shapes=[pltpu.VMEM((block + 2, cols, c), jnp.bfloat16)],
        cost_estimate=pl.CostEstimate(flops=flops, transcendentals=0,
                                      bytes_accessed=14 * (block + 2) * cols * c + 2 * 9 * c * c),
    )(coef, fb, rel, own, par, fa, above, frame, below, w3)


def shards(
    event_slices,
    frame_features,
    exposure_start,
    exposure_end,
    intersection_us,
    conv_first,
    conv_second,
    conv_frame,
):
    image = event_slices[0]
    frame = frame_features[0]
    block = image.shape[0]
    height = block * lax.axis_size("rows")
    row0 = lax.axis_index("rows") * block

    down = jnp.concatenate([image[block - 3 :], frame[block - 1 :]], axis=0)
    up = jnp.concatenate([image[:3], frame[:1]], axis=0)
    from_above = shifted(down, "rows", 1)
    from_below = shifted(up, "rows", -1)

    bounds = jnp.stack([2 - row0, height - row0 + 2]).astype(jnp.int32)
    second = layers(bounds, from_above, image, from_below, conv_first, conv_second)

    count = lax.axis_size("tm")
    t = lax.axis_index("tm")
    intersection = intersection_us[0].astype(jnp.float32)
    window = intersection.shape[0]
    radius = (window - 1) // 2
    slice_index = t + jnp.arange(window, dtype=jnp.int32) - radius
    valid = (slice_index >= exposure_start[0]) & (slice_index <= exposure_end[0])
    weights = jnp.where(valid, intersection, jnp.float32(0.0))
    weights = weights / jnp.sum(weights)

    swap = [(i, i ^ 1) for i in range(count)]
    partner = lax.ppermute(second, "tm", swap)
    from_behind = shifted(second, "tm", 2)
    from_ahead = shifted(second, "tm", -2)
    odd = t % 2
    forward = jnp.where(odd == 1, from_behind, from_ahead)
    relayed = lax.ppermute(forward, "tm", swap)
    is_odd = odd == 1
    coef = jnp.stack([
        weights[0],
        jnp.where(is_odd, weights[3], weights[1]),
        weights[2],
        jnp.where(is_odd, weights[1], weights[3]),
        weights[4],
    ])
    result = mix(coef, from_behind, relayed, second, partner, from_ahead,
                 from_above, frame, from_below, conv_frame)
    return result[None]


def solution(mesh):
    return jax.shard_map(
        shards,
        mesh=mesh,
        in_specs=(
            P("tm", "rows", None, None),
            P("tm", "rows", None, None),
            P("tm"),
            P("tm"),
            P("tm", None),
            P(),
            P(),
            P(),
        ),
        out_specs=P("tm", "rows", None, None),
        check_vma=False,
    )
```

```python
import numpy as np
import jax
import jax.numpy as jnp
from jax import lax
from jax.experimental import pallas as pl
from jax.experimental.pallas import tpu as pltpu
from jax.sharding import PartitionSpec as P


def shifted(value, axis, steps):
    count = lax.axis_size(axis)
    initial, last = (max(0, -steps), min(count, count - steps))
    pairs = [(source, source + steps) for source in range(initial, last)]
    if not pairs:
        return jnp.zeros_like(value)
    return lax.ppermute(value, axis, pairs)


def gelu(v):
    c = np.float32(np.sqrt(2 / np.pi))
    return v * (0.5 * (1.0 + jnp.tanh(c * (v + 0.044715 * (v * v * v)))))


def conv_rows(x, w_ref, rows_out):
    cols, cin = x.shape[1], x.shape[2]
    cout = w_ref.shape[3]
    m = rows_out * cols
    taps = []
    for b in range(3):
        acc = None
        for a in range(3):
            d = jnp.dot(x[a : a + rows_out].reshape(m, cin), w_ref[a, b],
                        preferred_element_type=jnp.float32)
            acc = d if acc is None else acc + d
        taps.append(acc)
    col = lax.broadcasted_iota(jnp.int32, (rows_out, cols, cout), 1).reshape(m, cout)
    left = pltpu.roll(taps[0], shift=1, axis=0)
    right = pltpu.roll(taps[2], shift=m - 1, axis=0)
    out = taps[1] + jnp.where(col == 0, 0.0, left) + jnp.where(col == cols - 1, 0.0, right)
    return out.reshape(rows_out, cols, cout)


def layers_kernel(bounds_ref, above_ref, image_ref, below_ref, w1_ref, w2_ref, out_ref, xbuf):
    halo = below_ref.shape[0] - 1
    block = image_ref.shape[0]
    xbuf[0:halo] = above_ref[0:halo]
    xbuf[halo : halo + block] = image_ref[...]
    xbuf[halo + block :] = below_ref[0:halo]
    rows1 = block + 2 * halo - 2
    first = gelu(conv_rows(xbuf[...], w1_ref, rows1))
    row = lax.broadcasted_iota(jnp.int32, first.shape, 0)
    inside = (row >= bounds_ref[0]) & (row < bounds_ref[1])
    first = jnp.where(inside, first, 0.0).astype(jnp.bfloat16)
    out_ref[...] = gelu(conv_rows(first, w2_ref, rows1 - 2)).astype(jnp.bfloat16)


def mix_kernel(coef_ref, fb_ref, rb_ref, own_ref, par_ref, ra_ref, fa_ref, above_ref, frame_ref,
               below_ref, w3_ref, out_ref, fbuf):
    halo = below_ref.shape[0] - 1
    block = frame_ref.shape[0]
    fbuf[0:1] = above_ref[halo : halo + 1]
    fbuf[1 : block + 1] = frame_ref[...]
    fbuf[block + 1 :] = below_ref[halo : halo + 1]
    f32 = jnp.float32
    summed = (
        coef_ref[0] * fb_ref[...].astype(f32)
        + coef_ref[1] * rb_ref[...].astype(f32)
        + coef_ref[2] * own_ref[...].astype(f32)
        + coef_ref[3] * par_ref[...].astype(f32)
        + coef_ref[4] * ra_ref[...].astype(f32)
        + coef_ref[5] * fa_ref[...].astype(f32)
    )
    mixed = (summed * fbuf[...].astype(f32)).astype(jnp.bfloat16)
    out_ref[...] = conv_rows(mixed, w3_ref, block).astype(jnp.bfloat16)


def vmem():
    return pl.BlockSpec(memory_space=pltpu.VMEM)


def smem():
    return pl.BlockSpec(memory_space=pltpu.SMEM)


def layers(bounds, above, image, below, w1, w2):
    block, cols, c = image.shape
    halo = below.shape[0] - 1
    rows = block + 2 * halo
    flops = 2 * 9 * c * c * cols * (2 * rows - 6)
    return pl.pallas_call(
        layers_kernel,
        out_shape=jax.ShapeDtypeStruct((rows - 4, cols, c), jnp.bfloat16),
        in_specs=[smem()] + [vmem()] * 5,
        out_specs=vmem(),
        scratch_shapes=[pltpu.VMEM((rows, cols, c), jnp.bfloat16)],
        cost_estimate=pl.CostEstimate(flops=flops, transcendentals=2 * rows * cols * c,
                                      bytes_accessed=4 * rows * cols * c + 4 * 9 * c * c),
    )(bounds, above, image, below, w1, w2)


def mix(coef, fb, rb, own, par, ra, fa, above, frame, below, w3):
    block, cols, c = frame.shape
    flops = 2 * 9 * c * c * cols * block
    return pl.pallas_call(
        mix_kernel,
        out_shape=jax.ShapeDtypeStruct((block, cols, c), jnp.bfloat16),
        in_specs=[smem()] + [vmem()] * 10,
        out_specs=vmem(),
        scratch_shapes=[pltpu.VMEM((block + 2, cols, c), jnp.bfloat16)],
        cost_estimate=pl.CostEstimate(flops=flops, transcendentals=0,
                                      bytes_accessed=16 * (block + 2) * cols * c + 2 * 9 * c * c),
    )(coef, fb, rb, own, par, ra, fa, above, frame, below, w3)


def shards(
    event_slices,
    frame_features,
    exposure_start,
    exposure_end,
    intersection_us,
    conv_first,
    conv_second,
    conv_frame,
):
    image = event_slices[0]
    frame = frame_features[0]
    block = image.shape[0]
    height = block * lax.axis_size("rows")
    row0 = lax.axis_index("rows") * block

    down = jnp.concatenate([image[block - 3 :], frame[block - 1 :]], axis=0)
    up = jnp.concatenate([image[:3], frame[:1]], axis=0)
    from_above = shifted(down, "rows", 1)
    from_below = shifted(up, "rows", -1)

    count = lax.axis_size("tm")
    t = lax.axis_index("tm")
    intersection = intersection_us[0].astype(jnp.float32)
    window = intersection.shape[0]
    radius = (window - 1) // 2
    slice_index = t + jnp.arange(window, dtype=jnp.int32) - radius
    valid = (slice_index >= exposure_start[0]) & (slice_index <= exposure_end[0])
    weights = jnp.where(valid, intersection, jnp.float32(0.0))
    weights = weights / jnp.sum(weights)
    is_odd = (t % 2) == 1
    partner_weight = jnp.where(is_odd, weights[1], weights[3])
    coef = jnp.concatenate([weights[:3], partner_weight[None], weights[3:]])
    bounds = jnp.stack([2 - row0, height - row0 + 2]).astype(jnp.int32)
    coef, bounds, image = lax.optimization_barrier((coef, bounds, image))

    second = layers(bounds, from_above, image, from_below, conv_first, conv_second)

    partner = lax.ppermute(second, "tm", [(i, i ^ 1) for i in range(count)])
    from_behind = shifted(second, "tm", 2)
    from_ahead = shifted(second, "tm", -2)
    relay_behind = lax.ppermute(from_behind, "tm", [(i + 1, i) for i in range(0, count, 2)])
    relay_ahead = lax.ppermute(from_ahead, "tm", [(i, i + 1) for i in range(0, count, 2)])
    result = mix(coef, from_behind, relay_behind, second, partner, relay_ahead, from_ahead,
                 from_above, frame, from_below, conv_frame)
    return result[None]


def solution(mesh):
    return jax.shard_map(
        shards,
        mesh=mesh,
        in_specs=(
            P("tm", "rows", None, None),
            P("tm", "rows", None, None),
            P("tm"),
            P("tm"),
            P("tm", None),
            P(),
            P(),
            P(),
        ),
        out_specs=P("tm", "rows", None, None),
        check_vma=False,
    )
```

```python
import numpy as np
import jax
import jax.numpy as jnp
from jax import lax
from jax.experimental import pallas as pl
from jax.experimental.pallas import tpu as pltpu
from jax.sharding import PartitionSpec as P


def shifted(value, axis, steps):
    count = lax.axis_size(axis)
    initial, last = (max(0, -steps), min(count, count - steps))
    pairs = [(source, source + steps) for source in range(initial, last)]
    if not pairs:
        return jnp.zeros_like(value)
    return lax.ppermute(value, axis, pairs)


def gelu(v):
    c = np.float32(np.sqrt(2 / np.pi))
    return v * (0.5 * (1.0 + jnp.tanh(c * (v + 0.044715 * (v * v * v)))))


def conv_rows(x, w_ref, stack, rows_out):
    cols, cin = x.shape[1], x.shape[2]
    cout = w_ref.shape[3]
    m = rows_out * cols
    for a in range(3):
        stack[0:rows_out, :, a * cin : (a + 1) * cin] = x[a : a + rows_out]
    lhs = stack[0:rows_out].reshape(m, 3 * cin)
    taps = [
        jnp.dot(lhs, w_ref[:, b].reshape(3 * cin, cout), preferred_element_type=jnp.float32)
        for b in range(3)
    ]
    col = lax.broadcasted_iota(jnp.int32, (rows_out, cols, cout), 1).reshape(m, cout)
    left = pltpu.roll(taps[0], shift=1, axis=0)
    right = pltpu.roll(taps[2], shift=m - 1, axis=0)
    out = taps[1] + jnp.where(col == 0, 0.0, left) + jnp.where(col == cols - 1, 0.0, right)
    return out.reshape(rows_out, cols, cout)


def layers_kernel(bounds_ref, above_ref, image_ref, below_ref, w1_ref, w2_ref, out_ref, xbuf, stack):
    halo = below_ref.shape[0] - 1
    block = image_ref.shape[0]
    xbuf[0:halo] = above_ref[0:halo]
    xbuf[halo : halo + block] = image_ref[...]
    xbuf[halo + block :] = below_ref[0:halo]
    rows1 = block + 2 * halo - 2
    first = gelu(conv_rows(xbuf[...], w1_ref, stack, rows1))
    row = lax.broadcasted_iota(jnp.int32, first.shape, 0)
    inside = (row >= bounds_ref[0]) & (row < bounds_ref[1])
    first = jnp.where(inside, first, 0.0).astype(jnp.bfloat16)
    out_ref[...] = gelu(conv_rows(first, w2_ref, stack, rows1 - 2)).astype(jnp.bfloat16)


def mix_kernel(coef_ref, fb_ref, rb_ref, own_ref, par_ref, ra_ref, fa_ref, above_ref, frame_ref,
               below_ref, w3_ref, out_ref, fbuf, stack):
    halo = below_ref.shape[0] - 1
    block = frame_ref.shape[0]
    fbuf[0:1] = above_ref[halo : halo + 1]
    fbuf[1 : block + 1] = frame_ref[...]
    fbuf[block + 1 :] = below_ref[halo : halo + 1]
    f32 = jnp.float32
    summed = (
        coef_ref[0] * fb_ref[...].astype(f32)
        + coef_ref[1] * rb_ref[...].astype(f32)
        + coef_ref[2] * own_ref[...].astype(f32)
        + coef_ref[3] * par_ref[...].astype(f32)
        + coef_ref[4] * ra_ref[...].astype(f32)
        + coef_ref[5] * fa_ref[...].astype(f32)
    )
    mixed = (summed * fbuf[...].astype(f32)).astype(jnp.bfloat16)
    out_ref[...] = conv_rows(mixed, w3_ref, stack, block).astype(jnp.bfloat16)


def vmem():
    return pl.BlockSpec(memory_space=pltpu.VMEM)


def smem():
    return pl.BlockSpec(memory_space=pltpu.SMEM)


def layers(bounds, above, image, below, w1, w2):
    block, cols, c = image.shape
    halo = below.shape[0] - 1
    rows = block + 2 * halo
    flops = 2 * 9 * c * c * cols * (2 * rows - 6)
    return pl.pallas_call(
        layers_kernel,
        out_shape=jax.ShapeDtypeStruct((rows - 4, cols, c), jnp.bfloat16),
        in_specs=[smem()] + [vmem()] * 5,
        out_specs=vmem(),
        scratch_shapes=[pltpu.VMEM((rows, cols, c), jnp.bfloat16),
                        pltpu.VMEM((rows - 2, cols, 3 * c), jnp.bfloat16)],
        cost_estimate=pl.CostEstimate(flops=flops, transcendentals=2 * rows * cols * c,
                                      bytes_accessed=4 * rows * cols * c + 4 * 9 * c * c),
    )(bounds, above, image, below, w1, w2)


def mix(coef, fb, rb, own, par, ra, fa, above, frame, below, w3):
    block, cols, c = frame.shape
    flops = 2 * 9 * c * c * cols * block
    return pl.pallas_call(
        mix_kernel,
        out_shape=jax.ShapeDtypeStruct((block, cols, c), jnp.bfloat16),
        in_specs=[smem()] + [vmem()] * 10,
        out_specs=vmem(),
        scratch_shapes=[pltpu.VMEM((block + 2, cols, c), jnp.bfloat16),
                        pltpu.VMEM((block, cols, 3 * c), jnp.bfloat16)],
        cost_estimate=pl.CostEstimate(flops=flops, transcendentals=0,
                                      bytes_accessed=16 * (block + 2) * cols * c + 2 * 9 * c * c),
    )(coef, fb, rb, own, par, ra, fa, above, frame, below, w3)


def shards(
    event_slices,
    frame_features,
    exposure_start,
    exposure_end,
    intersection_us,
    conv_first,
    conv_second,
    conv_frame,
):
    image = event_slices[0]
    frame = frame_features[0]
    block = image.shape[0]
    height = block * lax.axis_size("rows")
    row0 = lax.axis_index("rows") * block

    down = jnp.concatenate([image[block - 3 :], frame[block - 1 :]], axis=0)
    up = jnp.concatenate([image[:3], frame[:1]], axis=0)
    from_above = shifted(down, "rows", 1)
    from_below = shifted(up, "rows", -1)

    count = lax.axis_size("tm")
    t = lax.axis_index("tm")
    intersection = intersection_us[0].astype(jnp.float32)
    window = intersection.shape[0]
    radius = (window - 1) // 2
    slice_index = t + jnp.arange(window, dtype=jnp.int32) - radius
    valid = (slice_index >= exposure_start[0]) & (slice_index <= exposure_end[0])
    weights = jnp.where(valid, intersection, jnp.float32(0.0))
    weights = weights / jnp.sum(weights)
    is_odd = (t % 2) == 1
    partner_weight = jnp.where(is_odd, weights[1], weights[3])
    coef = jnp.concatenate([weights[:3], partner_weight[None], weights[3:]])
    bounds = jnp.stack([2 - row0, height - row0 + 2]).astype(jnp.int32)
    coef, bounds, image = lax.optimization_barrier((coef, bounds, image))

    second = layers(bounds, from_above, image, from_below, conv_first, conv_second)

    partner = lax.ppermute(second, "tm", [(i, i ^ 1) for i in range(count)])
    from_behind = shifted(second, "tm", 2)
    from_ahead = shifted(second, "tm", -2)
    relay_behind = lax.ppermute(from_behind, "tm", [(i + 1, i) for i in range(0, count, 2)])
    relay_ahead = lax.ppermute(from_ahead, "tm", [(i, i + 1) for i in range(0, count, 2)])
    result = mix(coef, from_behind, relay_behind, second, partner, relay_ahead, from_ahead,
                 from_above, frame, from_below, conv_frame)
    return result[None]


def solution(mesh):
    return jax.shard_map(
        shards,
        mesh=mesh,
        in_specs=(
            P("tm", "rows", None, None),
            P("tm", "rows", None, None),
            P("tm"),
            P("tm"),
            P("tm", None),
            P(),
            P(),
            P(),
        ),
        out_specs=P("tm", "rows", None, None),
        check_vma=False,
    )
```

```python
import numpy as np
import jax
import jax.numpy as jnp
from jax import lax
from jax.experimental import pallas as pl
from jax.experimental.pallas import tpu as pltpu
from jax.sharding import PartitionSpec as P


def shifted(value, axis, steps):
    count = lax.axis_size(axis)
    initial, last = (max(0, -steps), min(count, count - steps))
    pairs = [(source, source + steps) for source in range(initial, last)]
    if not pairs:
        return jnp.zeros_like(value)
    return lax.ppermute(value, axis, pairs)


def gelu(v):
    c = np.float32(np.sqrt(2 / np.pi))
    return v * (0.5 * (1.0 + jnp.tanh(c * (v + 0.044715 * (v * v * v)))))


def conv_rows(x, w_ref, stack, rows_out):
    cols, cin = x.shape[1], x.shape[2]
    cout = w_ref.shape[3]
    m = rows_out * cols
    for a in range(3):
        stack[0:rows_out, :, a * cin : (a + 1) * cin] = x[a : a + rows_out]
    lhs = stack[0:rows_out].reshape(m, 3 * cin)
    taps = [
        jnp.dot(lhs, w_ref[:, b].reshape(3 * cin, cout), preferred_element_type=jnp.float32)
        for b in range(3)
    ]
    col = lax.broadcasted_iota(jnp.int32, (rows_out, cols, cout), 1).reshape(m, cout)
    left = pltpu.roll(taps[0], shift=1, axis=0)
    right = pltpu.roll(taps[2], shift=m - 1, axis=0)
    out = taps[1] + jnp.where(col == 0, 0.0, left) + jnp.where(col == cols - 1, 0.0, right)
    return out.reshape(rows_out, cols, cout)


def layers_kernel(bounds_ref, above_ref, image_ref, below_ref, w1_ref, w2_ref, out_ref, xbuf, stack):
    halo = below_ref.shape[0] - 1
    block = image_ref.shape[0]
    xbuf[0:halo] = above_ref[0:halo]
    xbuf[halo : halo + block] = image_ref[...]
    xbuf[halo + block :] = below_ref[0:halo]
    rows1 = block + 2 * halo - 2
    first = gelu(conv_rows(xbuf[...], w1_ref, stack, rows1))
    row = lax.broadcasted_iota(jnp.int32, first.shape, 0)
    inside = (row >= bounds_ref[0]) & (row < bounds_ref[1])
    first = jnp.where(inside, first, 0.0).astype(jnp.bfloat16)
    out_ref[...] = gelu(conv_rows(first, w2_ref, stack, rows1 - 2)).astype(jnp.bfloat16)


def mix_kernel(coef_ref, fb_ref, fb2_ref, rb_ref, own_ref, par_ref, ra_ref, fa2_ref, fa_ref,
               above_ref, frame_ref, below_ref, w3_ref, out_ref, fbuf, stack):
    halo = below_ref.shape[0] - 1
    block = frame_ref.shape[0]
    fbuf[0:1] = above_ref[halo : halo + 1]
    fbuf[1 : block + 1] = frame_ref[...]
    fbuf[block + 1 :] = below_ref[halo : halo + 1]
    f32 = jnp.float32
    summed = (
        coef_ref[0] * (fb_ref[...].astype(f32) + fb2_ref[...].astype(f32))
        + coef_ref[1] * rb_ref[...].astype(f32)
        + coef_ref[2] * own_ref[...].astype(f32)
        + coef_ref[3] * par_ref[...].astype(f32)
        + coef_ref[4] * ra_ref[...].astype(f32)
        + coef_ref[5] * (fa_ref[...].astype(f32) + fa2_ref[...].astype(f32))
    )
    mixed = (summed * fbuf[...].astype(f32)).astype(jnp.bfloat16)
    out_ref[...] = conv_rows(mixed, w3_ref, stack, block).astype(jnp.bfloat16)


def vmem():
    return pl.BlockSpec(memory_space=pltpu.VMEM)


def smem():
    return pl.BlockSpec(memory_space=pltpu.SMEM)


def layers(bounds, above, image, below, w1, w2):
    block, cols, c = image.shape
    halo = below.shape[0] - 1
    rows = block + 2 * halo
    flops = 2 * 9 * c * c * cols * (2 * rows - 6)
    return pl.pallas_call(
        layers_kernel,
        out_shape=jax.ShapeDtypeStruct((rows - 4, cols, c), jnp.bfloat16),
        in_specs=[smem()] + [vmem()] * 5,
        out_specs=vmem(),
        scratch_shapes=[pltpu.VMEM((rows, cols, c), jnp.bfloat16),
                        pltpu.VMEM((rows - 2, cols, 3 * c), jnp.bfloat16)],
        cost_estimate=pl.CostEstimate(flops=flops, transcendentals=2 * rows * cols * c,
                                      bytes_accessed=4 * rows * cols * c + 4 * 9 * c * c),
    )(bounds, above, image, below, w1, w2)


def mix(coef, fb, fb2, rb, own, par, ra, fa2, fa, above, frame, below, w3):
    block, cols, c = frame.shape
    flops = 2 * 9 * c * c * cols * block
    return pl.pallas_call(
        mix_kernel,
        out_shape=jax.ShapeDtypeStruct((block, cols, c), jnp.bfloat16),
        in_specs=[smem()] + [vmem()] * 12,
        out_specs=vmem(),
        scratch_shapes=[pltpu.VMEM((block + 2, cols, c), jnp.bfloat16),
                        pltpu.VMEM((block, cols, 3 * c), jnp.bfloat16)],
        cost_estimate=pl.CostEstimate(flops=flops, transcendentals=0,
                                      bytes_accessed=20 * (block + 2) * cols * c + 2 * 9 * c * c),
    )(coef, fb, fb2, rb, own, par, ra, fa2, fa, above, frame, below, w3)


def shards(
    event_slices,
    frame_features,
    exposure_start,
    exposure_end,
    intersection_us,
    conv_first,
    conv_second,
    conv_frame,
):
    image = event_slices[0]
    frame = frame_features[0]
    block = image.shape[0]
    height = block * lax.axis_size("rows")
    row0 = lax.axis_index("rows") * block

    down = jnp.concatenate([image[block - 3 :], frame[block - 1 :]], axis=0)
    up = jnp.concatenate([image[:3], frame[:1]], axis=0)
    from_above = shifted(down, "rows", 1)
    from_below = shifted(up, "rows", -1)

    count = lax.axis_size("tm")
    t = lax.axis_index("tm")
    intersection = intersection_us[0].astype(jnp.float32)
    window = intersection.shape[0]
    radius = (window - 1) // 2
    slice_index = t + jnp.arange(window, dtype=jnp.int32) - radius
    valid = (slice_index >= exposure_start[0]) & (slice_index <= exposure_end[0])
    weights = jnp.where(valid, intersection, jnp.float32(0.0))
    weights = weights / jnp.sum(weights)
    is_odd = (t % 2) == 1
    partner_weight = jnp.where(is_odd, weights[1], weights[3])
    coef = jnp.concatenate([weights[:3], partner_weight[None], weights[3:]])
    bounds = jnp.stack([2 - row0, height - row0 + 2]).astype(jnp.int32)
    coef, bounds, image = lax.optimization_barrier((coef, bounds, image))

    second = layers(bounds, from_above, image, from_below, conv_first, conv_second)

    partner = lax.ppermute(second, "tm", [(i, i ^ 1) for i in range(count)])
    if count == 8:
        from_behind = lax.ppermute(second, "tm", [(0, 2), (1, 3), (3, 5), (4, 6), (5, 7)])
        from_ahead = lax.ppermute(second, "tm", [(2, 0), (3, 1), (4, 2), (6, 4), (7, 5)])
        hop = lax.ppermute(second, "tm", [(5, 1)])
        behind_routed = lax.ppermute(from_ahead, "tm", [(0, 4)])
        ahead_routed = lax.ppermute(hop, "tm", [(1, 3)])
    else:
        from_behind = shifted(second, "tm", 2)
        from_ahead = shifted(second, "tm", -2)
        behind_routed = jnp.zeros_like(second)
        ahead_routed = jnp.zeros_like(second)
    relay_behind = lax.ppermute(from_behind, "tm", [(i + 1, i) for i in range(0, count, 2)])
    relay_ahead = lax.ppermute(from_ahead, "tm", [(i, i + 1) for i in range(0, count, 2)])
    result = mix(coef, from_behind, behind_routed, relay_behind, second, partner, relay_ahead,
                 ahead_routed, from_ahead, from_above, frame, from_below, conv_frame)
    return result[None]


def solution(mesh):
    return jax.shard_map(
        shards,
        mesh=mesh,
        in_specs=(
            P("tm", "rows", None, None),
            P("tm", "rows", None, None),
            P("tm"),
            P("tm"),
            P("tm", None),
            P(),
            P(),
            P(),
        ),
        out_specs=P("tm", "rows", None, None),
        check_vma=False,
    )
```

```python
import numpy as np
import jax
import jax.numpy as jnp
from jax import lax
from jax.experimental import pallas as pl
from jax.experimental.pallas import tpu as pltpu
from jax.sharding import PartitionSpec as P


def shifted(value, axis, steps):
    count = lax.axis_size(axis)
    initial, last = (max(0, -steps), min(count, count - steps))
    pairs = [(source, source + steps) for source in range(initial, last)]
    if not pairs:
        return jnp.zeros_like(value)
    return lax.ppermute(value, axis, pairs)


def gelu(v):
    c = np.float32(np.sqrt(2 / np.pi))
    return v * (0.5 * (1.0 + jnp.tanh(c * (v + 0.044715 * (v * v * v)))))


def conv_rows(x, w_ref, stack, rows_out):
    cols, cin = x.shape[1], x.shape[2]
    cout = w_ref.shape[3]
    m = rows_out * cols
    for a in range(3):
        stack[0:rows_out, :, a * cin : (a + 1) * cin] = x[a : a + rows_out]
    lhs = stack[0:rows_out].reshape(m, 3 * cin)
    taps = [
        jnp.dot(lhs, w_ref[:, b].reshape(3 * cin, cout), preferred_element_type=jnp.float32)
        for b in range(3)
    ]
    col = lax.broadcasted_iota(jnp.int32, (rows_out, cols, cout), 1).reshape(m, cout)
    left = pltpu.roll(taps[0], shift=1, axis=0)
    right = pltpu.roll(taps[2], shift=m - 1, axis=0)
    out = taps[1] + jnp.where(col == 0, 0.0, left) + jnp.where(col == cols - 1, 0.0, right)
    return out.reshape(rows_out, cols, cout)


def layers_kernel(bounds_ref, above_ref, image_ref, below_ref, w1_ref, w2_ref, out_ref, xbuf, stack):
    halo = below_ref.shape[0] - 1
    block = image_ref.shape[0]
    xbuf[0:halo] = above_ref[0:halo]
    xbuf[halo : halo + block] = image_ref[...]
    xbuf[halo + block :] = below_ref[0:halo]
    rows1 = block + 2 * halo - 2
    first = gelu(conv_rows(xbuf[...], w1_ref, stack, rows1))
    row = lax.broadcasted_iota(jnp.int32, first.shape, 0)
    inside = (row >= bounds_ref[0]) & (row < bounds_ref[1])
    first = jnp.where(inside, first, 0.0).astype(jnp.bfloat16)
    out_ref[...] = gelu(conv_rows(first, w2_ref, stack, rows1 - 2)).astype(jnp.bfloat16)


def mix_kernel(coef_ref, fb_ref, rb_ref, own_ref, par_ref, ra_ref, fa_ref, routed_ref,
               above_ref, frame_ref, below_ref, w3_ref, out_ref, fbuf, stack):
    halo = below_ref.shape[0] - 1
    block = frame_ref.shape[0]
    fbuf[0:1] = above_ref[halo : halo + 1]
    fbuf[1 : block + 1] = frame_ref[...]
    fbuf[block + 1 :] = below_ref[halo : halo + 1]
    f32 = jnp.float32
    summed = (
        coef_ref[0] * fb_ref[...].astype(f32)
        + coef_ref[1] * rb_ref[...].astype(f32)
        + coef_ref[2] * own_ref[...].astype(f32)
        + coef_ref[3] * par_ref[...].astype(f32)
        + coef_ref[4] * ra_ref[...].astype(f32)
        + coef_ref[5] * fa_ref[...].astype(f32)
        + coef_ref[6] * routed_ref[...].astype(f32)
    )
    mixed = (summed * fbuf[...].astype(f32)).astype(jnp.bfloat16)
    out_ref[...] = conv_rows(mixed, w3_ref, stack, block).astype(jnp.bfloat16)


def vmem():
    return pl.BlockSpec(memory_space=pltpu.VMEM)


def smem():
    return pl.BlockSpec(memory_space=pltpu.SMEM)


def layers(bounds, above, image, below, w1, w2):
    block, cols, c = image.shape
    halo = below.shape[0] - 1
    rows = block + 2 * halo
    flops = 2 * 9 * c * c * cols * (2 * rows - 6)
    return pl.pallas_call(
        layers_kernel,
        out_shape=jax.ShapeDtypeStruct((rows - 4, cols, c), jnp.bfloat16),
        in_specs=[smem()] + [vmem()] * 5,
        out_specs=vmem(),
        scratch_shapes=[pltpu.VMEM((rows, cols, c), jnp.bfloat16),
                        pltpu.VMEM((rows - 2, cols, 3 * c), jnp.bfloat16)],
        cost_estimate=pl.CostEstimate(flops=flops, transcendentals=2 * rows * cols * c,
                                      bytes_accessed=4 * rows * cols * c + 4 * 9 * c * c),
    )(bounds, above, image, below, w1, w2)


def mix(coef, fb, rb, own, par, ra, fa, routed, above, frame, below, w3):
    block, cols, c = frame.shape
    flops = 2 * 9 * c * c * cols * block
    return pl.pallas_call(
        mix_kernel,
        out_shape=jax.ShapeDtypeStruct((block, cols, c), jnp.bfloat16),
        in_specs=[smem()] + [vmem()] * 11,
        out_specs=vmem(),
        scratch_shapes=[pltpu.VMEM((block + 2, cols, c), jnp.bfloat16),
                        pltpu.VMEM((block, cols, 3 * c), jnp.bfloat16)],
        cost_estimate=pl.CostEstimate(flops=flops, transcendentals=0,
                                      bytes_accessed=18 * (block + 2) * cols * c + 2 * 9 * c * c),
    )(coef, fb, rb, own, par, ra, fa, routed, above, frame, below, w3)


def shards(
    event_slices,
    frame_features,
    exposure_start,
    exposure_end,
    intersection_us,
    conv_first,
    conv_second,
    conv_frame,
):
    image = event_slices[0]
    frame = frame_features[0]
    block = image.shape[0]
    height = block * lax.axis_size("rows")
    row0 = lax.axis_index("rows") * block

    down = jnp.concatenate([image[block - 3 :], frame[block - 1 :]], axis=0)
    up = jnp.concatenate([image[:3], frame[:1]], axis=0)
    from_above = shifted(down, "rows", 1)
    from_below = shifted(up, "rows", -1)

    count = lax.axis_size("tm")
    t = lax.axis_index("tm")
    intersection = intersection_us[0].astype(jnp.float32)
    window = intersection.shape[0]
    radius = (window - 1) // 2
    slice_index = t + jnp.arange(window, dtype=jnp.int32) - radius
    valid = (slice_index >= exposure_start[0]) & (slice_index <= exposure_end[0])
    weights = jnp.where(valid, intersection, jnp.float32(0.0))
    weights = weights / jnp.sum(weights)
    is_odd = (t % 2) == 1
    partner_weight = jnp.where(is_odd, weights[1], weights[3])
    routed_weight = jnp.where(is_odd, weights[4], weights[0])
    coef = jnp.concatenate([weights[:3], partner_weight[None], weights[3:], routed_weight[None]])
    bounds = jnp.stack([2 - row0, height - row0 + 2]).astype(jnp.int32)
    coef, bounds, image = lax.optimization_barrier((coef, bounds, image))

    second = layers(bounds, from_above, image, from_below, conv_first, conv_second)

    partner = lax.ppermute(second, "tm", [(i, i ^ 1) for i in range(count)])
    if count == 8:
        from_behind = lax.ppermute(second, "tm", [(0, 2), (1, 3), (3, 5), (4, 6), (5, 7)])
        from_ahead = lax.ppermute(second, "tm", [(2, 0), (3, 1), (4, 2), (6, 4), (7, 5)])
        hop = lax.ppermute(second, "tm", [(2, 6), (5, 1)])
        routed = lax.ppermute(hop, "tm", [(6, 4), (1, 3)])
    else:
        from_behind = shifted(second, "tm", 2)
        from_ahead = shifted(second, "tm", -2)
        routed = jnp.zeros_like(second)
    relay_behind = lax.ppermute(from_behind, "tm", [(i + 1, i) for i in range(0, count, 2)])
    relay_ahead = lax.ppermute(from_ahead, "tm", [(i, i + 1) for i in range(0, count, 2)])
    result = mix(coef, from_behind, relay_behind, second, partner, relay_ahead, from_ahead, routed,
                 from_above, frame, from_below, conv_frame)
    return result[None]


def solution(mesh):
    return jax.shard_map(
        shards,
        mesh=mesh,
        in_specs=(
            P("tm", "rows", None, None),
            P("tm", "rows", None, None),
            P("tm"),
            P("tm"),
            P("tm", None),
            P(),
            P(),
            P(),
        ),
        out_specs=P("tm", "rows", None, None),
        check_vma=False,
    )
```

```python
import numpy as np
import jax
import jax.numpy as jnp
from jax import lax
from jax.experimental import pallas as pl
from jax.experimental.pallas import tpu as pltpu
from jax.sharding import PartitionSpec as P


def shifted(value, axis, steps):
    count = lax.axis_size(axis)
    initial, last = (max(0, -steps), min(count, count - steps))
    pairs = [(source, source + steps) for source in range(initial, last)]
    if not pairs:
        return jnp.zeros_like(value)
    return lax.ppermute(value, axis, pairs)


def gelu(v):
    c = np.float32(np.sqrt(2 / np.pi))
    return v * (0.5 * (1.0 + jnp.tanh(c * (v + 0.044715 * (v * v * v)))))


def conv_rows(x, w_ref, stack, rows_out):
    cols, cin = x.shape[1], x.shape[2]
    cout = w_ref.shape[3]
    m = rows_out * cols
    for a in range(3):
        stack[0:rows_out, :, a * cin : (a + 1) * cin] = x[a : a + rows_out]
    lhs = stack[0:rows_out].reshape(m, 3 * cin)
    taps = [
        jnp.dot(lhs, w_ref[:, b].reshape(3 * cin, cout), preferred_element_type=jnp.float32)
        for b in range(3)
    ]
    col = lax.broadcasted_iota(jnp.int32, (rows_out, cols, cout), 1).reshape(m, cout)
    left = pltpu.roll(taps[0], shift=1, axis=0)
    right = pltpu.roll(taps[2], shift=m - 1, axis=0)
    out = taps[1] + jnp.where(col == 0, 0.0, left) + jnp.where(col == cols - 1, 0.0, right)
    return out.reshape(rows_out, cols, cout)


def interior_kernel(image_ref, w1_ref, w2_ref, first_ref, second_ref, stack):
    block = image_ref.shape[0]
    first = gelu(conv_rows(image_ref[...], w1_ref, stack, block - 2)).astype(jnp.bfloat16)
    first_ref[...] = first
    second_ref[...] = gelu(conv_rows(first, w2_ref, stack, block - 4)).astype(jnp.bfloat16)


def edges_kernel(bounds_ref, above_ref, image_ref, below_ref, first_in_ref, second_in_ref, w1_ref,
                 w2_ref, out_ref, xbuf, first_buf, stack):
    halo = below_ref.shape[0] - 1
    block = image_ref.shape[0]
    rows1 = block + 2 * halo - 2
    edge = halo + 2
    row = lax.broadcasted_iota(jnp.int32, (halo, image_ref.shape[1], image_ref.shape[2]), 0)
    xbuf[0:halo] = above_ref[0:halo]
    xbuf[halo:edge] = image_ref[0:2]
    top = gelu(conv_rows(xbuf[...], w1_ref, stack, halo))
    top = jnp.where((row >= bounds_ref[0]) & (row < bounds_ref[1]), top, 0.0)
    first_buf[0:halo] = top.astype(jnp.bfloat16)
    xbuf[0:2] = image_ref[block - 2 :]
    xbuf[2:edge] = below_ref[0:halo]
    bottom = gelu(conv_rows(xbuf[...], w1_ref, stack, halo))
    low = rows1 - halo
    bottom = jnp.where((row + low >= bounds_ref[0]) & (row + low < bounds_ref[1]), bottom, 0.0)
    first_buf[low:] = bottom.astype(jnp.bfloat16)
    first_buf[halo:low] = first_in_ref[...]
    top2 = gelu(conv_rows(first_buf[0 : halo + 2], w2_ref, stack, halo))
    bottom2 = gelu(conv_rows(first_buf[low - 2 :], w2_ref, stack, halo))
    rows2 = rows1 - 2
    out_ref[0:halo] = top2.astype(jnp.bfloat16)
    out_ref[halo : rows2 - halo] = second_in_ref[...]
    out_ref[rows2 - halo :] = bottom2.astype(jnp.bfloat16)


def mix_kernel(coef_ref, fb_ref, rb_ref, own_ref, par_ref, ra_ref, fa_ref, routed_ref,
               above_ref, frame_ref, below_ref, w3_ref, out_ref, fbuf, stack):
    halo = below_ref.shape[0] - 1
    block = frame_ref.shape[0]
    fbuf[0:1] = above_ref[halo : halo + 1]
    fbuf[1 : block + 1] = frame_ref[...]
    fbuf[block + 1 :] = below_ref[halo : halo + 1]
    f32 = jnp.float32
    summed = (
        coef_ref[0] * fb_ref[...].astype(f32)
        + coef_ref[1] * rb_ref[...].astype(f32)
        + coef_ref[2] * own_ref[...].astype(f32)
        + coef_ref[3] * par_ref[...].astype(f32)
        + coef_ref[4] * ra_ref[...].astype(f32)
        + coef_ref[5] * fa_ref[...].astype(f32)
        + coef_ref[6] * routed_ref[...].astype(f32)
    )
    mixed = (summed * fbuf[...].astype(f32)).astype(jnp.bfloat16)
    out_ref[...] = conv_rows(mixed, w3_ref, stack, block).astype(jnp.bfloat16)


def vmem():
    return pl.BlockSpec(memory_space=pltpu.VMEM)


def smem():
    return pl.BlockSpec(memory_space=pltpu.SMEM)


def layers(bounds, above, image, below, w1, w2):
    block, cols, c = image.shape
    halo = below.shape[0] - 1
    rows = block + 2 * halo
    inner_flops = 2 * 9 * c * c * cols * (2 * block - 6)
    first_in, second_in = pl.pallas_call(
        interior_kernel,
        out_shape=(jax.ShapeDtypeStruct((block - 2, cols, c), jnp.bfloat16),
                   jax.ShapeDtypeStruct((block - 4, cols, c), jnp.bfloat16)),
        in_specs=[vmem()] * 3,
        out_specs=(vmem(), vmem()),
        scratch_shapes=[pltpu.VMEM((block - 2, cols, 3 * c), jnp.bfloat16)],
        cost_estimate=pl.CostEstimate(flops=inner_flops, transcendentals=2 * block * cols * c,
                                      bytes_accessed=4 * block * cols * c + 4 * 9 * c * c),
    )(image, w1, w2)
    edge_flops = 2 * 9 * c * c * cols * 4 * halo
    return pl.pallas_call(
        edges_kernel,
        out_shape=jax.ShapeDtypeStruct((rows - 4, cols, c), jnp.bfloat16),
        in_specs=[smem()] + [vmem()] * 7,
        out_specs=vmem(),
        scratch_shapes=[pltpu.VMEM((halo + 2, cols, c), jnp.bfloat16),
                        pltpu.VMEM((rows - 2, cols, c), jnp.bfloat16),
                        pltpu.VMEM((halo, cols, 3 * c), jnp.bfloat16)],
        cost_estimate=pl.CostEstimate(flops=edge_flops, transcendentals=4 * halo * cols * c,
                                      bytes_accessed=6 * rows * cols * c + 4 * 9 * c * c),
    )(bounds, above, image, below, first_in, second_in, w1, w2)


def mix(coef, fb, rb, own, par, ra, fa, routed, above, frame, below, w3):
    block, cols, c = frame.shape
    flops = 2 * 9 * c * c * cols * block
    return pl.pallas_call(
        mix_kernel,
        out_shape=jax.ShapeDtypeStruct((block, cols, c), jnp.bfloat16),
        in_specs=[smem()] + [vmem()] * 11,
        out_specs=vmem(),
        scratch_shapes=[pltpu.VMEM((block + 2, cols, c), jnp.bfloat16),
                        pltpu.VMEM((block, cols, 3 * c), jnp.bfloat16)],
        cost_estimate=pl.CostEstimate(flops=flops, transcendentals=0,
                                      bytes_accessed=18 * (block + 2) * cols * c + 2 * 9 * c * c),
    )(coef, fb, rb, own, par, ra, fa, routed, above, frame, below, w3)


def shards(
    event_slices,
    frame_features,
    exposure_start,
    exposure_end,
    intersection_us,
    conv_first,
    conv_second,
    conv_frame,
):
    image = event_slices[0]
    frame = frame_features[0]
    block = image.shape[0]
    height = block * lax.axis_size("rows")
    row0 = lax.axis_index("rows") * block

    down = jnp.concatenate([image[block - 3 :], frame[block - 1 :]], axis=0)
    up = jnp.concatenate([image[:3], frame[:1]], axis=0)
    from_above = shifted(down, "rows", 1)
    from_below = shifted(up, "rows", -1)

    count = lax.axis_size("tm")
    t = lax.axis_index("tm")
    intersection = intersection_us[0].astype(jnp.float32)
    window = intersection.shape[0]
    radius = (window - 1) // 2
    slice_index = t + jnp.arange(window, dtype=jnp.int32) - radius
    valid = (slice_index >= exposure_start[0]) & (slice_index <= exposure_end[0])
    weights = jnp.where(valid, intersection, jnp.float32(0.0))
    weights = weights / jnp.sum(weights)
    is_odd = (t % 2) == 1
    partner_weight = jnp.where(is_odd, weights[1], weights[3])
    routed_weight = jnp.where(is_odd, weights[4], weights[0])
    coef = jnp.concatenate([weights[:3], partner_weight[None], weights[3:], routed_weight[None]])
    bounds = jnp.stack([2 - row0, height - row0 + 2]).astype(jnp.int32)
    coef, bounds, image = lax.optimization_barrier((coef, bounds, image))

    second = layers(bounds, from_above, image, from_below, conv_first, conv_second)

    partner = lax.ppermute(second, "tm", [(i, i ^ 1) for i in range(count)])
    if count == 8:
        from_behind = lax.ppermute(second, "tm", [(0, 2), (1, 3), (3, 5), (4, 6), (5, 7)])
        from_ahead = lax.ppermute(second, "tm", [(2, 0), (3, 1), (4, 2), (6, 4), (7, 5)])
        hop = lax.ppermute(second, "tm", [(2, 6), (5, 1)])
        routed = lax.ppermute(hop, "tm", [(6, 4), (1, 3)])
    else:
        from_behind = shifted(second, "tm", 2)
        from_ahead = shifted(second, "tm", -2)
        routed = jnp.zeros_like(second)
    relay_behind = lax.ppermute(from_behind, "tm", [(i + 1, i) for i in range(0, count, 2)])
    relay_ahead = lax.ppermute(from_ahead, "tm", [(i, i + 1) for i in range(0, count, 2)])
    result = mix(coef, from_behind, relay_behind, second, partner, relay_ahead, from_ahead, routed,
                 from_above, frame, from_below, conv_frame)
    return result[None]


def solution(mesh):
    return jax.shard_map(
        shards,
        mesh=mesh,
        in_specs=(
            P("tm", "rows", None, None),
            P("tm", "rows", None, None),
            P("tm"),
            P("tm"),
            P("tm", None),
            P(),
            P(),
            P(),
        ),
        out_specs=P("tm", "rows", None, None),
        check_vma=False,
    )
```

```python
import numpy as np
import jax
import jax.numpy as jnp
from jax import lax
from jax.experimental import pallas as pl
from jax.experimental.pallas import tpu as pltpu
from jax.sharding import PartitionSpec as P


def shifted(value, axis, steps):
    count = lax.axis_size(axis)
    initial, last = (max(0, -steps), min(count, count - steps))
    pairs = [(source, source + steps) for source in range(initial, last)]
    if not pairs:
        return jnp.zeros_like(value)
    return lax.ppermute(value, axis, pairs)


def gelu(v):
    c = np.float32(np.sqrt(2 / np.pi))
    return v * (0.5 * (1.0 + jnp.tanh(c * (v + 0.044715 * (v * v * v)))))


def conv_rows(x, w_ref, stack, rows_out):
    cols, cin = x.shape[1], x.shape[2]
    cout = w_ref.shape[3]
    m = rows_out * cols
    for a in range(3):
        stack[0:rows_out, :, a * cin : (a + 1) * cin] = x[a : a + rows_out]
    lhs = stack[0:rows_out].reshape(m, 3 * cin)
    taps = [
        jnp.dot(lhs, w_ref[:, b].reshape(3 * cin, cout), preferred_element_type=jnp.float32)
        for b in range(3)
    ]
    col = lax.broadcasted_iota(jnp.int32, (rows_out, cols, cout), 1).reshape(m, cout)
    left = pltpu.roll(taps[0], shift=1, axis=0)
    right = pltpu.roll(taps[2], shift=m - 1, axis=0)
    out = taps[1] + jnp.where(col == 0, 0.0, left) + jnp.where(col == cols - 1, 0.0, right)
    return out.reshape(rows_out, cols, cout)


def layers_kernel(bounds_ref, above_ref, image_ref, below_ref, w1_ref, w2_ref, out_ref, xbuf, stack):
    halo = below_ref.shape[0] - 1
    block = image_ref.shape[0]
    xbuf[0:halo] = above_ref[0:halo]
    xbuf[halo : halo + block] = image_ref[...]
    xbuf[halo + block :] = below_ref[0:halo]
    rows1 = block + 2 * halo - 2
    first = gelu(conv_rows(xbuf[...], w1_ref, stack, rows1))
    row = lax.broadcasted_iota(jnp.int32, first.shape, 0)
    inside = (row >= bounds_ref[0]) & (row < bounds_ref[1])
    first = jnp.where(inside, first, 0.0).astype(jnp.bfloat16)
    out_ref[...] = gelu(conv_rows(first, w2_ref, stack, rows1 - 2)).astype(jnp.bfloat16)


def mix_kernel(coef_ref, fb_ref, rb_ref, own_ref, par_ref, ra_ref, fa_ref, routed_ref, frame_ref,
               w3_ref, out_ref, stack):
    f32 = jnp.float32
    summed = (
        coef_ref[0] * fb_ref[...].astype(f32)
        + coef_ref[1] * rb_ref[...].astype(f32)
        + coef_ref[2] * own_ref[...].astype(f32)
        + coef_ref[3] * par_ref[...].astype(f32)
        + coef_ref[4] * ra_ref[...].astype(f32)
        + coef_ref[5] * fa_ref[...].astype(f32)
        + coef_ref[6] * routed_ref[...].astype(f32)
    )
    mixed = (summed * frame_ref[...].astype(f32)).astype(jnp.bfloat16)
    out_ref[...] = conv_rows(mixed, w3_ref, stack, out_ref.shape[0]).astype(jnp.bfloat16)


def vmem():
    return pl.BlockSpec(memory_space=pltpu.VMEM)


def smem():
    return pl.BlockSpec(memory_space=pltpu.SMEM)


def layers(bounds, above, image, below, w1, w2):
    block, cols, c = image.shape
    halo = below.shape[0] - 1
    rows = block + 2 * halo
    flops = 2 * 9 * c * c * cols * (2 * rows - 6)
    return pl.pallas_call(
        layers_kernel,
        out_shape=jax.ShapeDtypeStruct((rows - 4, cols, c), jnp.bfloat16),
        in_specs=[smem()] + [vmem()] * 5,
        out_specs=vmem(),
        scratch_shapes=[pltpu.VMEM((rows, cols, c), jnp.bfloat16),
                        pltpu.VMEM((rows - 2, cols, 3 * c), jnp.bfloat16)],
        cost_estimate=pl.CostEstimate(flops=flops, transcendentals=2 * rows * cols * c,
                                      bytes_accessed=4 * rows * cols * c + 4 * 9 * c * c),
    )(bounds, above, image, below, w1, w2)


def mix(coef, fb, rb, own, par, ra, fa, routed, frame_ext, w3):
    rows, cols, c = frame_ext.shape
    block = rows - 2
    half = block // 2
    window = pl.BlockSpec((pl.Element(half + 2), pl.Element(cols), pl.Element(c)),
                          lambda i: (i * half, 0, 0))
    flops = 2 * 9 * c * c * cols * block
    return pl.pallas_call(
        mix_kernel,
        grid=(2,),
        out_shape=jax.ShapeDtypeStruct((block, cols, c), jnp.bfloat16),
        in_specs=[smem()] + [window] * 8 + [pl.BlockSpec(w3.shape, lambda i: (0, 0, 0, 0))],
        out_specs=pl.BlockSpec((half, cols, c), lambda i: (i, 0, 0)),
        scratch_shapes=[pltpu.VMEM((half, cols, 3 * c), jnp.bfloat16)],
        cost_estimate=pl.CostEstimate(flops=flops, transcendentals=0,
                                      bytes_accessed=18 * rows * cols * c + 2 * 9 * c * c),
    )(coef, fb, rb, own, par, ra, fa, routed, frame_ext, w3)


def shards(
    event_slices,
    frame_features,
    exposure_start,
    exposure_end,
    intersection_us,
    conv_first,
    conv_second,
    conv_frame,
):
    image = event_slices[0]
    frame = frame_features[0]
    block = image.shape[0]
    height = block * lax.axis_size("rows")
    row0 = lax.axis_index("rows") * block

    down = jnp.concatenate([image[block - 3 :], frame[block - 1 :]], axis=0)
    up = jnp.concatenate([image[:3], frame[:1]], axis=0)
    from_above = shifted(down, "rows", 1)
    from_below = shifted(up, "rows", -1)

    count = lax.axis_size("tm")
    t = lax.axis_index("tm")
    intersection = intersection_us[0].astype(jnp.float32)
    window = intersection.shape[0]
    radius = (window - 1) // 2
    slice_index = t + jnp.arange(window, dtype=jnp.int32) - radius
    valid = (slice_index >= exposure_start[0]) & (slice_index <= exposure_end[0])
    weights = jnp.where(valid, intersection, jnp.float32(0.0))
    weights = weights / jnp.sum(weights)
    is_odd = (t % 2) == 1
    partner_weight = jnp.where(is_odd, weights[1], weights[3])
    routed_weight = jnp.where(is_odd, weights[4], weights[0])
    coef = jnp.concatenate([weights[:3], partner_weight[None], weights[3:], routed_weight[None]])
    bounds = jnp.stack([2 - row0, height - row0 + 2]).astype(jnp.int32)
    coef, bounds, image = lax.optimization_barrier((coef, bounds, image))

    second = layers(bounds, from_above, image, from_below, conv_first, conv_second)

    partner = lax.ppermute(second, "tm", [(i, i ^ 1) for i in range(count)])
    if count == 8:
        from_behind = lax.ppermute(second, "tm", [(0, 2), (1, 3), (3, 5), (4, 6), (5, 7)])
        from_ahead = lax.ppermute(second, "tm", [(2, 0), (3, 1), (4, 2), (6, 4), (7, 5)])
        hop = lax.ppermute(second, "tm", [(2, 6), (5, 1)])
        routed = lax.ppermute(hop, "tm", [(6, 4), (1, 3)])
    else:
        from_behind = shifted(second, "tm", 2)
        from_ahead = shifted(second, "tm", -2)
        routed = jnp.zeros_like(second)
    relay_behind = lax.ppermute(from_behind, "tm", [(i + 1, i) for i in range(2, count, 2)])
    relay_ahead = lax.ppermute(from_ahead, "tm", [(i, i + 1) for i in range(0, count - 2, 2)])
    frame_ext = jnp.concatenate([from_above[3:], frame, from_below[3:]], axis=0)
    result = mix(coef, from_behind, relay_behind, second, partner, relay_ahead, from_ahead, routed,
                 frame_ext, conv_frame)
    return result[None]


def solution(mesh):
    return jax.shard_map(
        shards,
        mesh=mesh,
        in_specs=(
            P("tm", "rows", None, None),
            P("tm", "rows", None, None),
            P("tm"),
            P("tm"),
            P("tm", None),
            P(),
            P(),
            P(),
        ),
        out_specs=P("tm", "rows", None, None),
        check_vma=False,
    )
```

```python
import numpy as np
import jax
import jax.numpy as jnp
from jax import lax
from jax.experimental import pallas as pl
from jax.experimental.pallas import tpu as pltpu
from jax.sharding import PartitionSpec as P


def shifted(value, axis, steps):
    count = lax.axis_size(axis)
    initial, last = (max(0, -steps), min(count, count - steps))
    pairs = [(source, source + steps) for source in range(initial, last)]
    if not pairs:
        return jnp.zeros_like(value)
    return lax.ppermute(value, axis, pairs)


def gelu(v):
    c = np.float32(np.sqrt(2 / np.pi))
    return v * (0.5 * (1.0 + jnp.tanh(c * (v + 0.044715 * (v * v * v)))))


def conv_rows(src_ref, w_ref, stack, rows_out, emit):
    chunk = stack.shape[0]
    cols, cin = src_ref.shape[1], src_ref.shape[2]
    cout = w_ref.shape[3]
    r0 = 0
    while r0 < rows_out:
        n = min(chunk, rows_out - r0)
        m = n * cols
        for a in range(3):
            stack[0:n, :, a * cin : (a + 1) * cin] = src_ref[r0 + a : r0 + a + n]
        lhs = stack[0:n].reshape(m, 3 * cin)
        taps = [
            jnp.dot(lhs, w_ref[:, b].reshape(3 * cin, cout), preferred_element_type=jnp.float32)
            for b in range(3)
        ]
        col = lax.broadcasted_iota(jnp.int32, (n, cols, cout), 1).reshape(m, cout)
        left = pltpu.roll(taps[0], shift=1, axis=0)
        right = pltpu.roll(taps[2], shift=m - 1, axis=0)
        out = taps[1] + jnp.where(col == 0, 0.0, left) + jnp.where(col == cols - 1, 0.0, right)
        emit(r0, n, out.reshape(n, cols, cout))
        r0 += n


def layers_kernel(bounds_ref, above_ref, image_ref, below_ref, w1_ref, w2_ref, out_ref, xbuf,
                  first_buf, stack):
    halo = below_ref.shape[0] - 1
    block = image_ref.shape[0]
    xbuf[0:halo] = above_ref[0:halo]
    xbuf[halo : halo + block] = image_ref[...]
    xbuf[halo + block :] = below_ref[0:halo]
    rows1 = block + 2 * halo - 2

    def emit_first(r0, n, value):
        value = gelu(value)
        row = lax.broadcasted_iota(jnp.int32, value.shape, 0) + r0
        inside = (row >= bounds_ref[0]) & (row < bounds_ref[1])
        first_buf[r0 : r0 + n] = jnp.where(inside, value, 0.0).astype(jnp.bfloat16)

    def emit_second(r0, n, value):
        out_ref[r0 : r0 + n] = gelu(value).astype(jnp.bfloat16)

    conv_rows(xbuf, w1_ref, stack, rows1, emit_first)
    conv_rows(first_buf, w2_ref, stack, rows1 - 2, emit_second)


def mix_kernel(coef_ref, fb_ref, rb_ref, own_ref, par_ref, ra_ref, fa_ref, routed_ref,
               above_ref, frame_ref, below_ref, w3_ref, out_ref, fbuf, mixed_buf, stack):
    halo = below_ref.shape[0] - 1
    block = frame_ref.shape[0]
    fbuf[0:1] = above_ref[halo : halo + 1]
    fbuf[1 : block + 1] = frame_ref[...]
    fbuf[block + 1 :] = below_ref[halo : halo + 1]
    f32 = jnp.float32
    step = stack.shape[0]
    for r0 in range(0, block + 2, step):
        rows = pl.ds(r0, min(step, block + 2 - r0))
        summed = (
            coef_ref[0] * fb_ref[rows].astype(f32)
            + coef_ref[1] * rb_ref[rows].astype(f32)
            + coef_ref[2] * own_ref[rows].astype(f32)
            + coef_ref[3] * par_ref[rows].astype(f32)
            + coef_ref[4] * ra_ref[rows].astype(f32)
            + coef_ref[5] * fa_ref[rows].astype(f32)
            + coef_ref[6] * routed_ref[rows].astype(f32)
        )
        mixed_buf[rows] = (summed * fbuf[rows].astype(f32)).astype(jnp.bfloat16)

    def emit(r0, n, value):
        out_ref[r0 : r0 + n] = value.astype(jnp.bfloat16)

    conv_rows(mixed_buf, w3_ref, stack, block, emit)


def vmem():
    return pl.BlockSpec(memory_space=pltpu.VMEM)


def smem():
    return pl.BlockSpec(memory_space=pltpu.SMEM)


CHUNK = 2


def layers(bounds, above, image, below, w1, w2):
    block, cols, c = image.shape
    halo = below.shape[0] - 1
    rows = block + 2 * halo
    flops = 2 * 9 * c * c * cols * (2 * rows - 6)
    return pl.pallas_call(
        layers_kernel,
        out_shape=jax.ShapeDtypeStruct((rows - 4, cols, c), jnp.bfloat16),
        in_specs=[smem()] + [vmem()] * 5,
        out_specs=vmem(),
        scratch_shapes=[pltpu.VMEM((rows, cols, c), jnp.bfloat16),
                        pltpu.VMEM((rows - 2, cols, c), jnp.bfloat16),
                        pltpu.VMEM((CHUNK, cols, 3 * c), jnp.bfloat16)],
        cost_estimate=pl.CostEstimate(flops=flops, transcendentals=2 * rows * cols * c,
                                      bytes_accessed=4 * rows * cols * c + 4 * 9 * c * c),
    )(bounds, above, image, below, w1, w2)


def mix(coef, fb, rb, own, par, ra, fa, routed, above, frame, below, w3):
    block, cols, c = frame.shape
    flops = 2 * 9 * c * c * cols * block
    return pl.pallas_call(
        mix_kernel,
        out_shape=jax.ShapeDtypeStruct((block, cols, c), jnp.bfloat16),
        in_specs=[smem()] + [vmem()] * 11,
        out_specs=vmem(),
        scratch_shapes=[pltpu.VMEM((block + 2, cols, c), jnp.bfloat16),
                        pltpu.VMEM((block + 2, cols, c), jnp.bfloat16),
                        pltpu.VMEM((CHUNK, cols, 3 * c), jnp.bfloat16)],
        cost_estimate=pl.CostEstimate(flops=flops, transcendentals=0,
                                      bytes_accessed=18 * (block + 2) * cols * c + 2 * 9 * c * c),
    )(coef, fb, rb, own, par, ra, fa, routed, above, frame, below, w3)


def shards(
    event_slices,
    frame_features,
    exposure_start,
    exposure_end,
    intersection_us,
    conv_first,
    conv_second,
    conv_frame,
):
    image = event_slices[0]
    frame = frame_features[0]
    block = image.shape[0]
    height = block * lax.axis_size("rows")
    row0 = lax.axis_index("rows") * block

    down = jnp.concatenate([image[block - 3 :], frame[block - 1 :]], axis=0)
    up = jnp.concatenate([image[:3], frame[:1]], axis=0)
    from_above = shifted(down, "rows", 1)
    from_below = shifted(up, "rows", -1)

    count = lax.axis_size("tm")
    t = lax.axis_index("tm")
    intersection = intersection_us[0].astype(jnp.float32)
    window = intersection.shape[0]
    radius = (window - 1) // 2
    slice_index = t + jnp.arange(window, dtype=jnp.int32) - radius
    valid = (slice_index >= exposure_start[0]) & (slice_index <= exposure_end[0])
    weights = jnp.where(valid, intersection, jnp.float32(0.0))
    weights = weights / jnp.sum(weights)
    is_odd = (t % 2) == 1
    partner_weight = jnp.where(is_odd, weights[1], weights[3])
    routed_weight = jnp.where(is_odd, weights[4], weights[0])
    coef = jnp.concatenate([weights[:3], partner_weight[None], weights[3:], routed_weight[None]])
    bounds = jnp.stack([2 - row0, height - row0 + 2]).astype(jnp.int32)
    coef, bounds, image = lax.optimization_barrier((coef, bounds, image))

    second = layers(bounds, from_above, image, from_below, conv_first, conv_second)

    partner = lax.ppermute(second, "tm", [(i, i ^ 1) for i in range(count)])
    if count == 8:
        from_behind = lax.ppermute(second, "tm", [(0, 2), (1, 3), (3, 5), (4, 6), (5, 7)])
        from_ahead = lax.ppermute(second, "tm", [(2, 0), (3, 1), (4, 2), (6, 4), (7, 5)])
        hop = lax.ppermute(second, "tm", [(2, 6), (5, 1)])
        routed = lax.ppermute(hop, "tm", [(6, 4), (1, 3)])
    else:
        from_behind = shifted(second, "tm", 2)
        from_ahead = shifted(second, "tm", -2)
        routed = jnp.zeros_like(second)
    relay_behind = lax.ppermute(from_behind, "tm", [(i + 1, i) for i in range(2, count, 2)])
    relay_ahead = lax.ppermute(from_ahead, "tm", [(i, i + 1) for i in range(0, count - 2, 2)])
    result = mix(coef, from_behind, relay_behind, second, partner, relay_ahead, from_ahead, routed,
                 from_above, frame, from_below, conv_frame)
    return result[None]


def solution(mesh):
    return jax.shard_map(
        shards,
        mesh=mesh,
        in_specs=(
            P("tm", "rows", None, None),
            P("tm", "rows", None, None),
            P("tm"),
            P("tm"),
            P("tm", None),
            P(),
            P(),
            P(),
        ),
        out_specs=P("tm", "rows", None, None),
        check_vma=False,
    )
```

```python
import numpy as np
import jax
import jax.numpy as jnp
from jax import lax
from jax.experimental import pallas as pl
from jax.experimental.pallas import tpu as pltpu
from jax.sharding import PartitionSpec as P


def shifted(value, axis, steps):
    count = lax.axis_size(axis)
    initial, last = (max(0, -steps), min(count, count - steps))
    pairs = [(source, source + steps) for source in range(initial, last)]
    if not pairs:
        return jnp.zeros_like(value)
    return lax.ppermute(value, axis, pairs)


def gelu(v):
    c = np.float32(np.sqrt(2 / np.pi))
    return v * (0.5 * (1.0 + jnp.tanh(c * (v + 0.044715 * (v * v * v)))))


def conv_rows(src_ref, w_ref, stack, rows_out, emit):
    chunk = stack.shape[0]
    cols, cin = src_ref.shape[1], src_ref.shape[2]
    cout = w_ref.shape[3]
    r0 = 0
    while r0 < rows_out:
        n = min(chunk, rows_out - r0)
        m = n * cols
        for a in range(3):
            stack[0:n, :, a * cin : (a + 1) * cin] = src_ref[r0 + a : r0 + a + n]
        lhs = stack[0:n].reshape(m, 3 * cin)
        taps = [
            jnp.dot(lhs, w_ref[:, b].reshape(3 * cin, cout), preferred_element_type=jnp.float32)
            for b in range(3)
        ]
        col = lax.broadcasted_iota(jnp.int32, (n, cols, cout), 1).reshape(m, cout)
        left = pltpu.roll(taps[0], shift=1, axis=0)
        right = pltpu.roll(taps[2], shift=m - 1, axis=0)
        out = taps[1] + jnp.where(col == 0, 0.0, left) + jnp.where(col == cols - 1, 0.0, right)
        emit(r0, n, out.reshape(n, cols, cout))
        r0 += n


def layers_kernel(bounds_ref, above_ref, image_ref, below_ref, w1_ref, w2_ref, out_ref, xbuf,
                  first_buf, stack):
    halo = below_ref.shape[0] - 1
    block = image_ref.shape[0]
    xbuf[0:halo] = above_ref[0:halo]
    xbuf[halo : halo + block] = image_ref[...]
    xbuf[halo + block :] = below_ref[0:halo]
    rows1 = block + 2 * halo - 2

    def emit_first(r0, n, value):
        value = gelu(value)
        row = lax.broadcasted_iota(jnp.int32, value.shape, 0) + r0
        inside = (row >= bounds_ref[0]) & (row < bounds_ref[1])
        first_buf[r0 : r0 + n] = jnp.where(inside, value, 0.0).astype(jnp.bfloat16)

    def emit_second(r0, n, value):
        out_ref[r0 : r0 + n] = gelu(value).astype(jnp.bfloat16)

    conv_rows(xbuf, w1_ref, stack, rows1, emit_first)
    conv_rows(first_buf, w2_ref, stack, rows1 - 2, emit_second)


def mix_kernel(coef_ref, fbe_ref, fbo_ref, rb_ref, own_ref, par_ref, ra_ref, fae_ref, fao_ref,
               routed_ref, above_ref, frame_ref, below_ref, w3_ref, out_ref, fbuf, mixed_buf, stack):
    halo = below_ref.shape[0] - 1
    block = frame_ref.shape[0]
    fbuf[0:1] = above_ref[halo : halo + 1]
    fbuf[1 : block + 1] = frame_ref[...]
    fbuf[block + 1 :] = below_ref[halo : halo + 1]
    f32 = jnp.float32
    step = stack.shape[0]
    odd = coef_ref[7] > 0.5
    for r0 in range(0, block + 2, step):
        rows = pl.ds(r0, min(step, block + 2 - r0))

        def even_terms():
            return (
                coef_ref[0] * fbe_ref[rows].astype(f32)
                + coef_ref[1] * rb_ref[rows].astype(f32)
                + coef_ref[5] * fae_ref[rows].astype(f32)
            )

        def odd_terms():
            return (
                coef_ref[0] * fbo_ref[rows].astype(f32)
                + coef_ref[4] * ra_ref[rows].astype(f32)
                + coef_ref[5] * fao_ref[rows].astype(f32)
            )

        summed = lax.cond(odd, odd_terms, even_terms) + (
            coef_ref[2] * own_ref[rows].astype(f32)
            + coef_ref[3] * par_ref[rows].astype(f32)
            + coef_ref[6] * routed_ref[rows].astype(f32)
        )
        mixed_buf[rows] = (summed * fbuf[rows].astype(f32)).astype(jnp.bfloat16)

    def emit(r0, n, value):
        out_ref[r0 : r0 + n] = value.astype(jnp.bfloat16)

    conv_rows(mixed_buf, w3_ref, stack, block, emit)


def vmem():
    return pl.BlockSpec(memory_space=pltpu.VMEM)


def smem():
    return pl.BlockSpec(memory_space=pltpu.SMEM)


CHUNK = 2


def layers(bounds, above, image, below, w1, w2):
    block, cols, c = image.shape
    halo = below.shape[0] - 1
    rows = block + 2 * halo
    flops = 2 * 9 * c * c * cols * (2 * rows - 6)
    return pl.pallas_call(
        layers_kernel,
        out_shape=jax.ShapeDtypeStruct((rows - 4, cols, c), jnp.bfloat16),
        in_specs=[smem()] + [vmem()] * 5,
        out_specs=vmem(),
        scratch_shapes=[pltpu.VMEM((rows, cols, c), jnp.bfloat16),
                        pltpu.VMEM((rows - 2, cols, c), jnp.bfloat16),
                        pltpu.VMEM((CHUNK, cols, 3 * c), jnp.bfloat16)],
        cost_estimate=pl.CostEstimate(flops=flops, transcendentals=2 * rows * cols * c,
                                      bytes_accessed=4 * rows * cols * c + 4 * 9 * c * c),
    )(bounds, above, image, below, w1, w2)


def mix(coef, fbe, fbo, rb, own, par, ra, fae, fao, routed, above, frame, below, w3):
    block, cols, c = frame.shape
    flops = 2 * 9 * c * c * cols * block
    return pl.pallas_call(
        mix_kernel,
        out_shape=jax.ShapeDtypeStruct((block, cols, c), jnp.bfloat16),
        in_specs=[smem()] + [vmem()] * 13,
        out_specs=vmem(),
        scratch_shapes=[pltpu.VMEM((block + 2, cols, c), jnp.bfloat16),
                        pltpu.VMEM((block + 2, cols, c), jnp.bfloat16),
                        pltpu.VMEM((CHUNK, cols, 3 * c), jnp.bfloat16)],
        cost_estimate=pl.CostEstimate(flops=flops, transcendentals=0,
                                      bytes_accessed=18 * (block + 2) * cols * c + 2 * 9 * c * c),
    )(coef, fbe, fbo, rb, own, par, ra, fae, fao, routed, above, frame, below, w3)


def shards(
    event_slices,
    frame_features,
    exposure_start,
    exposure_end,
    intersection_us,
    conv_first,
    conv_second,
    conv_frame,
):
    image = event_slices[0]
    frame = frame_features[0]
    block = image.shape[0]
    height = block * lax.axis_size("rows")
    row0 = lax.axis_index("rows") * block

    down = jnp.concatenate([image[block - 3 :], frame[block - 1 :]], axis=0)
    up = jnp.concatenate([image[:3], frame[:1]], axis=0)
    from_above = shifted(down, "rows", 1)
    from_below = shifted(up, "rows", -1)

    count = lax.axis_size("tm")
    t = lax.axis_index("tm")
    intersection = intersection_us[0].astype(jnp.float32)
    window = intersection.shape[0]
    radius = (window - 1) // 2
    slice_index = t + jnp.arange(window, dtype=jnp.int32) - radius
    valid = (slice_index >= exposure_start[0]) & (slice_index <= exposure_end[0])
    weights = jnp.where(valid, intersection, jnp.float32(0.0))
    weights = weights / jnp.sum(weights)
    is_odd = (t % 2) == 1
    partner_weight = jnp.where(is_odd, weights[1], weights[3])
    routed_weight = jnp.where(is_odd, weights[4], weights[0])
    coef = jnp.concatenate([weights[:3], partner_weight[None], weights[3:], routed_weight[None],
                            is_odd.astype(jnp.float32)[None]])
    bounds = jnp.stack([2 - row0, height - row0 + 2]).astype(jnp.int32)
    coef, bounds, image = lax.optimization_barrier((coef, bounds, image))

    second = layers(bounds, from_above, image, from_below, conv_first, conv_second)

    partner = lax.ppermute(second, "tm", [(i, i ^ 1) for i in range(count)])
    if count == 8:
        behind_pairs = [(0, 2), (1, 3), (3, 5), (4, 6), (5, 7)]
        ahead_pairs = [(2, 0), (3, 1), (4, 2), (6, 4), (7, 5)]
        hop = lax.ppermute(second, "tm", [(2, 6), (5, 1)])
        routed = lax.ppermute(hop, "tm", [(6, 4), (1, 3)])
    else:
        behind_pairs = [(i, i + 2) for i in range(count - 2)]
        ahead_pairs = [(i + 2, i) for i in range(count - 2)]
        routed = jnp.zeros_like(second)
    def by_parity(pairs, parity):
        chosen = [(a, b) for a, b in pairs if b % 2 == parity]
        return lax.ppermute(second, "tm", chosen) if chosen else jnp.zeros_like(second)

    behind_even = by_parity(behind_pairs, 0)
    behind_odd = by_parity(behind_pairs, 1)
    ahead_even = by_parity(ahead_pairs, 0)
    ahead_odd = by_parity(ahead_pairs, 1)
    relay_behind = lax.ppermute(behind_odd, "tm", [(i + 1, i) for i in range(2, count, 2)])
    relay_ahead = lax.ppermute(ahead_even, "tm", [(i, i + 1) for i in range(0, count - 2, 2)])
    result = mix(coef, behind_even, behind_odd, relay_behind, second, partner, relay_ahead,
                 ahead_even, ahead_odd, routed, from_above, frame, from_below, conv_frame)
    return result[None]


def solution(mesh):
    return jax.shard_map(
        shards,
        mesh=mesh,
        in_specs=(
            P("tm", "rows", None, None),
            P("tm", "rows", None, None),
            P("tm"),
            P("tm"),
            P("tm", None),
            P(),
            P(),
            P(),
        ),
        out_specs=P("tm", "rows", None, None),
        check_vma=False,
    )
```

```python
import numpy as np
import jax
import jax.numpy as jnp
from jax import lax
from jax.experimental import pallas as pl
from jax.experimental.pallas import tpu as pltpu
from jax.sharding import PartitionSpec as P


def shifted(value, axis, steps):
    count = lax.axis_size(axis)
    initial, last = (max(0, -steps), min(count, count - steps))
    pairs = [(source, source + steps) for source in range(initial, last)]
    if not pairs:
        return jnp.zeros_like(value)
    return lax.ppermute(value, axis, pairs)


def gelu(v):
    c = np.float32(np.sqrt(2 / np.pi))
    return v * (0.5 * (1.0 + jnp.tanh(c * (v + 0.044715 * (v * v * v)))))


def conv_rows(src_ref, w_ref, stack, rows_out, emit):
    chunk = stack.shape[0]
    cols, cin = src_ref.shape[1], src_ref.shape[2]
    cout = w_ref.shape[3]
    r0 = 0
    while r0 < rows_out:
        n = min(chunk, rows_out - r0)
        m = n * cols
        for a in range(3):
            stack[0:n, :, a * cin : (a + 1) * cin] = src_ref[r0 + a : r0 + a + n]
        lhs = stack[0:n].reshape(m, 3 * cin)
        taps = [
            jnp.dot(lhs, w_ref[:, b].reshape(3 * cin, cout), preferred_element_type=jnp.float32)
            for b in range(3)
        ]
        col = lax.broadcasted_iota(jnp.int32, (n, cols, cout), 1).reshape(m, cout)
        left = pltpu.roll(taps[0], shift=1, axis=0)
        right = pltpu.roll(taps[2], shift=m - 1, axis=0)
        out = taps[1] + jnp.where(col == 0, 0.0, left) + jnp.where(col == cols - 1, 0.0, right)
        emit(r0, n, out.reshape(n, cols, cout))
        r0 += n


def layers_kernel(bounds_ref, above_ref, image_ref, below_ref, w1_ref, w2_ref, out_ref, xbuf,
                  first_buf, stack):
    halo = below_ref.shape[0]
    block = image_ref.shape[0]
    xbuf[0:halo] = above_ref[0:halo]
    xbuf[halo : halo + block] = image_ref[...]
    xbuf[halo + block :] = below_ref[0:halo]
    rows1 = block + 2 * halo - 2

    def emit_first(r0, n, value):
        value = gelu(value)
        row = lax.broadcasted_iota(jnp.int32, value.shape, 0) + r0
        inside = (row >= bounds_ref[0]) & (row < bounds_ref[1])
        first_buf[r0 : r0 + n] = jnp.where(inside, value, 0.0).astype(jnp.bfloat16)

    def emit_second(r0, n, value):
        out_ref[r0 : r0 + n] = gelu(value).astype(jnp.bfloat16)

    conv_rows(xbuf, w1_ref, stack, rows1, emit_first)
    conv_rows(first_buf, w2_ref, stack, rows1 - 2, emit_second)


def mix_kernel(coef_ref, fb_ref, rb_ref, own_ref, par_ref, ra_ref, fa_ref, routed_ref,
               above_ref, frame_ref, below_ref, w3_ref, out_ref, fbuf, mixed_buf, stack):
    block = frame_ref.shape[0]
    fbuf[0:1] = above_ref[...]
    fbuf[1 : block + 1] = frame_ref[...]
    fbuf[block + 1 :] = below_ref[...]
    f32 = jnp.float32
    step = stack.shape[0]
    for r0 in range(0, block + 2, step):
        rows = pl.ds(r0, min(step, block + 2 - r0))
        summed = (
            coef_ref[0] * fb_ref[rows].astype(f32)
            + coef_ref[1] * rb_ref[rows].astype(f32)
            + coef_ref[2] * own_ref[rows].astype(f32)
            + coef_ref[3] * par_ref[rows].astype(f32)
            + coef_ref[4] * ra_ref[rows].astype(f32)
            + coef_ref[5] * fa_ref[rows].astype(f32)
            + coef_ref[6] * routed_ref[rows].astype(f32)
        )
        mixed_buf[rows] = (summed * fbuf[rows].astype(f32)).astype(jnp.bfloat16)

    def emit(r0, n, value):
        out_ref[r0 : r0 + n] = value.astype(jnp.bfloat16)

    conv_rows(mixed_buf, w3_ref, stack, block, emit)


def vmem():
    return pl.BlockSpec(memory_space=pltpu.VMEM)


def smem():
    return pl.BlockSpec(memory_space=pltpu.SMEM)


CHUNK = 2


def layers(bounds, above, image, below, w1, w2):
    block, cols, c = image.shape
    halo = below.shape[0]
    rows = block + 2 * halo
    flops = 2 * 9 * c * c * cols * (2 * rows - 6)
    return pl.pallas_call(
        layers_kernel,
        out_shape=jax.ShapeDtypeStruct((rows - 4, cols, c), jnp.bfloat16),
        in_specs=[smem()] + [vmem()] * 5,
        out_specs=vmem(),
        scratch_shapes=[pltpu.VMEM((rows, cols, c), jnp.bfloat16),
                        pltpu.VMEM((rows - 2, cols, c), jnp.bfloat16),
                        pltpu.VMEM((CHUNK, cols, 3 * c), jnp.bfloat16)],
        cost_estimate=pl.CostEstimate(flops=flops, transcendentals=2 * rows * cols * c,
                                      bytes_accessed=4 * rows * cols * c + 4 * 9 * c * c),
    )(bounds, above, image, below, w1, w2)


def mix(coef, fb, rb, own, par, ra, fa, routed, above, frame, below, w3):
    block, cols, c = frame.shape
    flops = 2 * 9 * c * c * cols * block
    return pl.pallas_call(
        mix_kernel,
        out_shape=jax.ShapeDtypeStruct((block, cols, c), jnp.bfloat16),
        in_specs=[smem()] + [vmem()] * 11,
        out_specs=vmem(),
        scratch_shapes=[pltpu.VMEM((block + 2, cols, c), jnp.bfloat16),
                        pltpu.VMEM((block + 2, cols, c), jnp.bfloat16),
                        pltpu.VMEM((CHUNK, cols, 3 * c), jnp.bfloat16)],
        cost_estimate=pl.CostEstimate(flops=flops, transcendentals=0,
                                      bytes_accessed=18 * (block + 2) * cols * c + 2 * 9 * c * c),
    )(coef, fb, rb, own, par, ra, fa, routed, above, frame, below, w3)


def shards(
    event_slices,
    frame_features,
    exposure_start,
    exposure_end,
    intersection_us,
    conv_first,
    conv_second,
    conv_frame,
):
    image = event_slices[0]
    frame = frame_features[0]
    block = image.shape[0]
    height = block * lax.axis_size("rows")
    row0 = lax.axis_index("rows") * block

    image_above = shifted(image[block - 3 :], "rows", 1)
    image_below = shifted(image[:3], "rows", -1)
    frame_above = shifted(frame[block - 1 :], "rows", 1)
    frame_below = shifted(frame[:1], "rows", -1)

    count = lax.axis_size("tm")
    t = lax.axis_index("tm")
    intersection = intersection_us[0].astype(jnp.float32)
    window = intersection.shape[0]
    radius = (window - 1) // 2
    slice_index = t + jnp.arange(window, dtype=jnp.int32) - radius
    valid = (slice_index >= exposure_start[0]) & (slice_index <= exposure_end[0])
    weights = jnp.where(valid, intersection, jnp.float32(0.0))
    weights = weights / jnp.sum(weights)
    is_odd = (t % 2) == 1
    partner_weight = jnp.where(is_odd, weights[1], weights[3])
    routed_weight = jnp.where(is_odd, weights[4], weights[0])
    coef = jnp.concatenate([weights[:3], partner_weight[None], weights[3:], routed_weight[None]])
    bounds = jnp.stack([2 - row0, height - row0 + 2]).astype(jnp.int32)
    coef, bounds, image = lax.optimization_barrier((coef, bounds, image))

    second = layers(bounds, image_above, image, image_below, conv_first, conv_second)

    partner = lax.ppermute(second, "tm", [(i, i ^ 1) for i in range(count)])
    if count == 8:
        from_behind = lax.ppermute(second, "tm", [(0, 2), (1, 3), (3, 5), (4, 6), (5, 7)])
        from_ahead = lax.ppermute(second, "tm", [(2, 0), (3, 1), (4, 2), (6, 4), (7, 5)])
        hop = lax.ppermute(second, "tm", [(2, 6), (5, 1)])
        routed = lax.ppermute(hop, "tm", [(6, 4), (1, 3)])
    else:
        from_behind = shifted(second, "tm", 2)
        from_ahead = shifted(second, "tm", -2)
        routed = jnp.zeros_like(second)
    relay_behind = lax.ppermute(from_behind, "tm", [(i + 1, i) for i in range(2, count, 2)])
    relay_ahead = lax.ppermute(from_ahead, "tm", [(i, i + 1) for i in range(0, count - 2, 2)])
    result = mix(coef, from_behind, relay_behind, second, partner, relay_ahead, from_ahead, routed,
                 frame_above, frame, frame_below, conv_frame)
    return result[None]


def solution(mesh):
    return jax.shard_map(
        shards,
        mesh=mesh,
        in_specs=(
            P("tm", "rows", None, None),
            P("tm", "rows", None, None),
            P("tm"),
            P("tm"),
            P("tm", None),
            P(),
            P(),
            P(),
        ),
        out_specs=P("tm", "rows", None, None),
        check_vma=False,
    )
```

```python
import numpy as np
import jax
import jax.numpy as jnp
from jax import lax
from jax.experimental import pallas as pl
from jax.experimental.pallas import tpu as pltpu
from jax.sharding import PartitionSpec as P


def shifted(value, axis, steps):
    count = lax.axis_size(axis)
    initial, last = (max(0, -steps), min(count, count - steps))
    pairs = [(source, source + steps) for source in range(initial, last)]
    if not pairs:
        return jnp.zeros_like(value)
    return lax.ppermute(value, axis, pairs)


def gelu(v):
    c = np.float32(np.sqrt(2 / np.pi))
    return v * (0.5 * (1.0 + jnp.tanh(c * (v + 0.044715 * (v * v * v)))))


def conv_chunk(src_ref, w_ref, stack, r0, n, emit):
    cols, cin = src_ref.shape[1], src_ref.shape[2]
    cout = w_ref.shape[3]
    m = n * cols
    for a in range(3):
        stack[0:n, :, a * cin : (a + 1) * cin] = src_ref[r0 + a : r0 + a + n]
    lhs = stack[0:n].reshape(m, 3 * cin)
    taps = [
        jnp.dot(lhs, w_ref[:, b].reshape(3 * cin, cout), preferred_element_type=jnp.float32)
        for b in range(3)
    ]
    col = lax.broadcasted_iota(jnp.int32, (n, cols, cout), 1).reshape(m, cout)
    left = pltpu.roll(taps[0], shift=1, axis=0)
    right = pltpu.roll(taps[2], shift=m - 1, axis=0)
    out = taps[1] + jnp.where(col == 0, 0.0, left) + jnp.where(col == cols - 1, 0.0, right)
    emit(r0, n, out.reshape(n, cols, cout))


def conv_rows(src_ref, w_ref, stack, rows_out, emit):
    chunk = stack.shape[0]
    for r0 in range(0, rows_out, chunk):
        conv_chunk(src_ref, w_ref, stack, r0, min(chunk, rows_out - r0), emit)


def layers_kernel(bounds_ref, above_ref, image_ref, below_ref, w1_ref, w2_ref, out_ref, xbuf,
                  first_buf, stack):
    halo = below_ref.shape[0] - 1
    block = image_ref.shape[0]
    xbuf[0:halo] = above_ref[0:halo]
    xbuf[halo : halo + block] = image_ref[...]
    xbuf[halo + block :] = below_ref[0:halo]
    rows1 = block + 2 * halo - 2

    def emit_first(r0, n, value):
        value = gelu(value)
        row = lax.broadcasted_iota(jnp.int32, value.shape, 0) + r0
        inside = (row >= bounds_ref[0]) & (row < bounds_ref[1])
        first_buf[r0 : r0 + n] = jnp.where(inside, value, 0.0).astype(jnp.bfloat16)

    def emit_second(r0, n, value):
        out_ref[r0 : r0 + n] = gelu(value).astype(jnp.bfloat16)

    conv_rows(xbuf, w1_ref, stack, rows1, emit_first)
    conv_rows(first_buf, w2_ref, stack, rows1 - 2, emit_second)


def mix_kernel(coef_ref, fb_ref, rb_ref, own_ref, par_ref, ra_ref, fa_ref, routed_ref,
               above_ref, frame_ref, below_ref, w3_ref, out_ref, fbuf, mixed_buf, stack):
    halo = below_ref.shape[0] - 1
    block = frame_ref.shape[0]
    fbuf[0:1] = above_ref[halo : halo + 1]
    fbuf[1 : block + 1] = frame_ref[...]
    fbuf[block + 1 :] = below_ref[halo : halo + 1]
    f32 = jnp.float32
    step = stack.shape[0]

    def join(r0, n):
        rows = pl.ds(r0, n)
        summed = (
            coef_ref[0] * fb_ref[rows].astype(f32)
            + coef_ref[1] * rb_ref[rows].astype(f32)
            + coef_ref[2] * own_ref[rows].astype(f32)
            + coef_ref[3] * par_ref[rows].astype(f32)
            + coef_ref[4] * ra_ref[rows].astype(f32)
            + coef_ref[5] * fa_ref[rows].astype(f32)
            + coef_ref[6] * routed_ref[rows].astype(f32)
        )
        mixed_buf[rows] = (summed * fbuf[rows].astype(f32)).astype(jnp.bfloat16)

    def emit(r0, n, value):
        out_ref[r0 : r0 + n] = value.astype(jnp.bfloat16)

    join(0, 2)
    done = 2
    r0 = 0
    while r0 < block:
        n = min(step, block - r0)
        need = r0 + n + 2
        if need > done:
            join(done, need - done)
            done = need
        conv_chunk(mixed_buf, w3_ref, stack, r0, n, emit)
        r0 += n


def vmem():
    return pl.BlockSpec(memory_space=pltpu.VMEM)


def smem():
    return pl.BlockSpec(memory_space=pltpu.SMEM)


CHUNK = 2


def layers(bounds, above, image, below, w1, w2):
    block, cols, c = image.shape
    halo = below.shape[0] - 1
    rows = block + 2 * halo
    flops = 2 * 9 * c * c * cols * (2 * rows - 6)
    return pl.pallas_call(
        layers_kernel,
        out_shape=jax.ShapeDtypeStruct((rows - 4, cols, c), jnp.bfloat16),
        in_specs=[smem()] + [vmem()] * 5,
        out_specs=vmem(),
        scratch_shapes=[pltpu.VMEM((rows, cols, c), jnp.bfloat16),
                        pltpu.VMEM((rows - 2, cols, c), jnp.bfloat16),
                        pltpu.VMEM((CHUNK, cols, 3 * c), jnp.bfloat16)],
        cost_estimate=pl.CostEstimate(flops=flops, transcendentals=2 * rows * cols * c,
                                      bytes_accessed=4 * rows * cols * c + 4 * 9 * c * c),
    )(bounds, above, image, below, w1, w2)


def mix(coef, fb, rb, own, par, ra, fa, routed, above, frame, below, w3):
    block, cols, c = frame.shape
    flops = 2 * 9 * c * c * cols * block
    return pl.pallas_call(
        mix_kernel,
        out_shape=jax.ShapeDtypeStruct((block, cols, c), jnp.bfloat16),
        in_specs=[smem()] + [vmem()] * 11,
        out_specs=vmem(),
        scratch_shapes=[pltpu.VMEM((block + 2, cols, c), jnp.bfloat16),
                        pltpu.VMEM((block + 2, cols, c), jnp.bfloat16),
                        pltpu.VMEM((CHUNK, cols, 3 * c), jnp.bfloat16)],
        cost_estimate=pl.CostEstimate(flops=flops, transcendentals=0,
                                      bytes_accessed=18 * (block + 2) * cols * c + 2 * 9 * c * c),
    )(coef, fb, rb, own, par, ra, fa, routed, above, frame, below, w3)


def shards(
    event_slices,
    frame_features,
    exposure_start,
    exposure_end,
    intersection_us,
    conv_first,
    conv_second,
    conv_frame,
):
    image = event_slices[0]
    frame = frame_features[0]
    block = image.shape[0]
    height = block * lax.axis_size("rows")
    row0 = lax.axis_index("rows") * block

    down = jnp.concatenate([image[block - 3 :], frame[block - 1 :]], axis=0)
    up = jnp.concatenate([image[:3], frame[:1]], axis=0)
    from_above = shifted(down, "rows", 1)
    from_below = shifted(up, "rows", -1)

    count = lax.axis_size("tm")
    t = lax.axis_index("tm")
    intersection = intersection_us[0].astype(jnp.float32)
    window = intersection.shape[0]
    radius = (window - 1) // 2
    slice_index = t + jnp.arange(window, dtype=jnp.int32) - radius
    valid = (slice_index >= exposure_start[0]) & (slice_index <= exposure_end[0])
    weights = jnp.where(valid, intersection, jnp.float32(0.0))
    weights = weights / jnp.sum(weights)
    is_odd = (t % 2) == 1
    partner_weight = jnp.where(is_odd, weights[1], weights[3])
    routed_weight = jnp.where(is_odd, weights[4], weights[0])
    coef = jnp.concatenate([weights[:3], partner_weight[None], weights[3:], routed_weight[None]])
    bounds = jnp.stack([2 - row0, height - row0 + 2]).astype(jnp.int32)
    coef, bounds, image = lax.optimization_barrier((coef, bounds, image))

    second = layers(bounds, from_above, image, from_below, conv_first, conv_second)

    partner = lax.ppermute(second, "tm", [(i, i ^ 1) for i in range(count)])
    if count == 8:
        from_behind = lax.ppermute(second, "tm", [(0, 2), (1, 3), (3, 5), (4, 6), (5, 7)])
        from_ahead = lax.ppermute(second, "tm", [(2, 0), (3, 1), (4, 2), (6, 4), (7, 5)])
        hop = lax.ppermute(second, "tm", [(2, 6), (5, 1)])
        routed = lax.ppermute(hop, "tm", [(6, 4), (1, 3)])
    else:
        from_behind = shifted(second, "tm", 2)
        from_ahead = shifted(second, "tm", -2)
        routed = jnp.zeros_like(second)
    relay_behind = lax.ppermute(from_behind, "tm", [(i + 1, i) for i in range(2, count, 2)])
    relay_ahead = lax.ppermute(from_ahead, "tm", [(i, i + 1) for i in range(0, count - 2, 2)])
    result = mix(coef, from_behind, relay_behind, second, partner, relay_ahead, from_ahead, routed,
                 from_above, frame, from_below, conv_frame)
    return result[None]


def solution(mesh):
    return jax.shard_map(
        shards,
        mesh=mesh,
        in_specs=(
            P("tm", "rows", None, None),
            P("tm", "rows", None, None),
            P("tm"),
            P("tm"),
            P("tm", None),
            P(),
            P(),
            P(),
        ),
        out_specs=P("tm", "rows", None, None),
        check_vma=False,
    )
```

```python
import numpy as np
import jax
import jax.numpy as jnp
from jax import lax
from jax.experimental import pallas as pl
from jax.experimental.pallas import tpu as pltpu
from jax.sharding import PartitionSpec as P


def shifted(value, axis, steps):
    count = lax.axis_size(axis)
    initial, last = (max(0, -steps), min(count, count - steps))
    pairs = [(source, source + steps) for source in range(initial, last)]
    if not pairs:
        return jnp.zeros_like(value)
    return lax.ppermute(value, axis, pairs)


def gelu(v):
    c = np.float32(np.sqrt(2 / np.pi))
    return v * (0.5 * (1.0 + jnp.tanh(c * (v + 0.044715 * (v * v * v)))))


def conv_chunk(src_ref, w_ref, stack, r0, n, emit):
    cols, cin = src_ref.shape[1], src_ref.shape[2]
    cout = w_ref.shape[3]
    m = n * cols
    for a in range(3):
        stack[0:n, :, a * cin : (a + 1) * cin] = src_ref[r0 + a : r0 + a + n]
    lhs = stack[0:n].reshape(m, 3 * cin)
    taps = [
        jnp.dot(lhs, w_ref[:, b].reshape(3 * cin, cout), preferred_element_type=jnp.float32)
        for b in range(3)
    ]
    col = lax.broadcasted_iota(jnp.int32, (n, cols, cout), 1).reshape(m, cout)
    left = pltpu.roll(taps[0], shift=1, axis=0)
    right = pltpu.roll(taps[2], shift=m - 1, axis=0)
    out = taps[1] + jnp.where(col == 0, 0.0, left) + jnp.where(col == cols - 1, 0.0, right)
    emit(r0, n, out.reshape(n, cols, cout))


def conv_rows(src_ref, w_ref, stack, rows_out, emit):
    chunk = stack.shape[0]
    for r0 in range(0, rows_out, chunk):
        conv_chunk(src_ref, w_ref, stack, r0, min(chunk, rows_out - r0), emit)


def layers_kernel(bounds_ref, above_ref, image_ref, below_ref, w1_ref, w2_ref, out_ref, xbuf,
                  first_buf, stack):
    halo = below_ref.shape[0] - 1
    block = image_ref.shape[0]
    xbuf[0:halo] = above_ref[0:halo]
    xbuf[halo : halo + block] = image_ref[...]
    xbuf[halo + block :] = below_ref[0:halo]
    rows1 = block + 2 * halo - 2

    def emit_first(r0, n, value):
        value = gelu(value)
        row = lax.broadcasted_iota(jnp.int32, value.shape, 0) + r0
        inside = (row >= bounds_ref[0]) & (row < bounds_ref[1])
        first_buf[r0 : r0 + n] = jnp.where(inside, value, 0.0).astype(jnp.bfloat16)

    def emit_second(r0, n, value):
        out_ref[r0 : r0 + n] = gelu(value).astype(jnp.bfloat16)

    conv_rows(xbuf, w1_ref, stack, rows1, emit_first)
    conv_rows(first_buf, w2_ref, stack, rows1 - 2, emit_second)


def mix_kernel(coef_ref, fb_ref, rb_ref, own_ref, par_ref, ra_ref, fa_ref, routed_ref,
               above_ref, frame_ref, below_ref, w3_ref, out_ref, fbuf, mixed_buf, stack):
    halo = below_ref.shape[0] - 1
    block = frame_ref.shape[0]
    fbuf[0:1] = above_ref[halo : halo + 1]
    fbuf[1 : block + 1] = frame_ref[...]
    fbuf[block + 1 :] = below_ref[halo : halo + 1]
    f32 = jnp.float32
    step = stack.shape[0]

    def join(r0, n):
        rows = pl.ds(r0, n)
        bf = jnp.bfloat16
        summed = (
            coef_ref[0].astype(bf) * fb_ref[rows]
            + coef_ref[1].astype(bf) * rb_ref[rows]
            + coef_ref[2].astype(bf) * own_ref[rows]
            + coef_ref[3].astype(bf) * par_ref[rows]
            + coef_ref[4].astype(bf) * ra_ref[rows]
            + coef_ref[5].astype(bf) * fa_ref[rows]
            + coef_ref[6].astype(bf) * routed_ref[rows]
        )
        mixed_buf[rows] = summed * fbuf[rows]

    def emit(r0, n, value):
        out_ref[r0 : r0 + n] = value.astype(jnp.bfloat16)

    join(0, 2)
    done = 2
    r0 = 0
    while r0 < block:
        n = min(step, block - r0)
        need = r0 + n + 2
        if need > done:
            join(done, need - done)
            done = need
        conv_chunk(mixed_buf, w3_ref, stack, r0, n, emit)
        r0 += n


def vmem():
    return pl.BlockSpec(memory_space=pltpu.VMEM)


def smem():
    return pl.BlockSpec(memory_space=pltpu.SMEM)


CHUNK = 2


def layers(bounds, above, image, below, w1, w2):
    block, cols, c = image.shape
    halo = below.shape[0] - 1
    rows = block + 2 * halo
    flops = 2 * 9 * c * c * cols * (2 * rows - 6)
    return pl.pallas_call(
        layers_kernel,
        out_shape=jax.ShapeDtypeStruct((rows - 4, cols, c), jnp.bfloat16),
        in_specs=[smem()] + [vmem()] * 5,
        out_specs=vmem(),
        scratch_shapes=[pltpu.VMEM((rows, cols, c), jnp.bfloat16),
                        pltpu.VMEM((rows - 2, cols, c), jnp.bfloat16),
                        pltpu.VMEM((CHUNK, cols, 3 * c), jnp.bfloat16)],
        cost_estimate=pl.CostEstimate(flops=flops, transcendentals=2 * rows * cols * c,
                                      bytes_accessed=4 * rows * cols * c + 4 * 9 * c * c),
    )(bounds, above, image, below, w1, w2)


def mix(coef, fb, rb, own, par, ra, fa, routed, above, frame, below, w3):
    block, cols, c = frame.shape
    flops = 2 * 9 * c * c * cols * block
    return pl.pallas_call(
        mix_kernel,
        out_shape=jax.ShapeDtypeStruct((block, cols, c), jnp.bfloat16),
        in_specs=[smem()] + [vmem()] * 11,
        out_specs=vmem(),
        scratch_shapes=[pltpu.VMEM((block + 2, cols, c), jnp.bfloat16),
                        pltpu.VMEM((block + 2, cols, c), jnp.bfloat16),
                        pltpu.VMEM((CHUNK, cols, 3 * c), jnp.bfloat16)],
        cost_estimate=pl.CostEstimate(flops=flops, transcendentals=0,
                                      bytes_accessed=18 * (block + 2) * cols * c + 2 * 9 * c * c),
    )(coef, fb, rb, own, par, ra, fa, routed, above, frame, below, w3)


def shards(
    event_slices,
    frame_features,
    exposure_start,
    exposure_end,
    intersection_us,
    conv_first,
    conv_second,
    conv_frame,
):
    image = event_slices[0]
    frame = frame_features[0]
    block = image.shape[0]
    height = block * lax.axis_size("rows")
    row0 = lax.axis_index("rows") * block

    down = jnp.concatenate([image[block - 3 :], frame[block - 1 :]], axis=0)
    up = jnp.concatenate([image[:3], frame[:1]], axis=0)
    from_above = shifted(down, "rows", 1)
    from_below = shifted(up, "rows", -1)

    count = lax.axis_size("tm")
    t = lax.axis_index("tm")
    intersection = intersection_us[0].astype(jnp.float32)
    window = intersection.shape[0]
    radius = (window - 1) // 2
    slice_index = t + jnp.arange(window, dtype=jnp.int32) - radius
    valid = (slice_index >= exposure_start[0]) & (slice_index <= exposure_end[0])
    weights = jnp.where(valid, intersection, jnp.float32(0.0))
    weights = weights / jnp.sum(weights)
    is_odd = (t % 2) == 1
    partner_weight = jnp.where(is_odd, weights[1], weights[3])
    routed_weight = jnp.where(is_odd, weights[4], weights[0])
    coef = jnp.concatenate([weights[:3], partner_weight[None], weights[3:], routed_weight[None]])
    bounds = jnp.stack([2 - row0, height - row0 + 2]).astype(jnp.int32)
    coef, bounds, image = lax.optimization_barrier((coef, bounds, image))

    second = layers(bounds, from_above, image, from_below, conv_first, conv_second)

    partner = lax.ppermute(second, "tm", [(i, i ^ 1) for i in range(count)])
    if count == 8:
        from_behind = lax.ppermute(second, "tm", [(0, 2), (1, 3), (3, 5), (4, 6), (5, 7)])
        from_ahead = lax.ppermute(second, "tm", [(2, 0), (3, 1), (4, 2), (6, 4), (7, 5)])
        hop = lax.ppermute(second, "tm", [(2, 6), (5, 1)])
        routed = lax.ppermute(hop, "tm", [(6, 4), (1, 3)])
    else:
        from_behind = shifted(second, "tm", 2)
        from_ahead = shifted(second, "tm", -2)
        routed = jnp.zeros_like(second)
    relay_behind = lax.ppermute(from_behind, "tm", [(i + 1, i) for i in range(2, count, 2)])
    relay_ahead = lax.ppermute(from_ahead, "tm", [(i, i + 1) for i in range(0, count - 2, 2)])
    result = mix(coef, from_behind, relay_behind, second, partner, relay_ahead, from_ahead, routed,
                 from_above, frame, from_below, conv_frame)
    return result[None]


def solution(mesh):
    return jax.shard_map(
        shards,
        mesh=mesh,
        in_specs=(
            P("tm", "rows", None, None),
            P("tm", "rows", None, None),
            P("tm"),
            P("tm"),
            P("tm", None),
            P(),
            P(),
            P(),
        ),
        out_specs=P("tm", "rows", None, None),
        check_vma=False,
    )
```

```python
import numpy as np
import jax
import jax.numpy as jnp
from jax import lax
from jax.experimental import pallas as pl
from jax.experimental.pallas import tpu as pltpu
from jax.sharding import PartitionSpec as P


def shifted(value, axis, steps):
    count = lax.axis_size(axis)
    initial, last = (max(0, -steps), min(count, count - steps))
    pairs = [(source, source + steps) for source in range(initial, last)]
    if not pairs:
        return jnp.zeros_like(value)
    return lax.ppermute(value, axis, pairs)


def gelu(v):
    c = np.float32(np.sqrt(2 / np.pi))
    return v * (0.5 * (1.0 + jnp.tanh(c * (v + 0.044715 * (v * v * v)))))


def conv_chunk(src_ref, w_ref, stack, r0, n, emit):
    cols, cin = src_ref.shape[1], src_ref.shape[2]
    cout = w_ref.shape[3]
    m = n * cols
    for a in range(3):
        stack[0:n, :, a * cin : (a + 1) * cin] = src_ref[r0 + a : r0 + a + n]
    lhs = stack[0:n].reshape(m, 3 * cin)
    taps = [
        jnp.dot(lhs, w_ref[:, b].reshape(3 * cin, cout), preferred_element_type=jnp.float32)
        for b in range(3)
    ]
    col = lax.broadcasted_iota(jnp.int32, (n, cols, cout), 1).reshape(m, cout)
    left = pltpu.roll(taps[0], shift=1, axis=0)
    right = pltpu.roll(taps[2], shift=m - 1, axis=0)
    out = taps[1] + jnp.where(col == 0, 0.0, left) + jnp.where(col == cols - 1, 0.0, right)
    emit(r0, n, out.reshape(n, cols, cout))


def conv_rows(src_ref, w_ref, stack, rows_out, emit):
    chunk = stack.shape[0]
    for r0 in range(0, rows_out, chunk):
        conv_chunk(src_ref, w_ref, stack, r0, min(chunk, rows_out - r0), emit)


def layers_kernel(bounds_ref, above_ref, image_ref, below_ref, w1_ref, w2_ref, out_ref, xbuf,
                  first_buf, stack):
    halo = below_ref.shape[0] - 1
    block = image_ref.shape[0]
    xbuf[0:halo] = above_ref[0:halo]
    xbuf[halo : halo + block] = image_ref[...]
    xbuf[halo + block :] = below_ref[0:halo]
    rows1 = block + 2 * halo - 2

    def emit_first(r0, n, value):
        value = gelu(value)
        row = lax.broadcasted_iota(jnp.int32, value.shape, 0) + r0
        inside = (row >= bounds_ref[0]) & (row < bounds_ref[1])
        first_buf[r0 : r0 + n] = jnp.where(inside, value, 0.0).astype(jnp.bfloat16)

    def emit_second(r0, n, value):
        out_ref[r0 : r0 + n] = gelu(value).astype(jnp.bfloat16)

    conv_rows(xbuf, w1_ref, stack, rows1, emit_first)
    conv_rows(first_buf, w2_ref, stack, rows1 - 2, emit_second)


def mix_kernel(coef_ref, *refs):
    (fb_hbm, rb_hbm, own_hbm, par_hbm, ra_hbm, fa_hbm, routed_hbm, above_hbm, frame_hbm, below_hbm,
     w3_hbm, out_ref, fb_ref, rb_ref, own_ref, par_ref, ra_ref, fa_ref, routed_ref, fbuf, w3_ref,
     mixed_buf, stack, sems) = refs
    block = frame_hbm.shape[0]
    rows = block + 2
    split = rows // 2 + 1
    slices = [(fb_hbm, fb_ref), (rb_hbm, rb_ref), (own_hbm, own_ref), (par_hbm, par_ref),
              (ra_hbm, ra_ref), (fa_hbm, fa_ref), (routed_hbm, routed_ref)]
    first = [pltpu.make_async_copy(w3_hbm, w3_ref, sems.at[0])]
    for i, (src, dst) in enumerate(slices):
        first.append(pltpu.make_async_copy(src.at[0:split], dst.at[0:split], sems.at[1 + i]))
    halo = below_hbm.shape[0] - 1
    first.append(pltpu.make_async_copy(above_hbm.at[halo : halo + 1], fbuf.at[0:1], sems.at[8]))
    first.append(pltpu.make_async_copy(frame_hbm, fbuf.at[1 : block + 1], sems.at[9]))
    first.append(pltpu.make_async_copy(below_hbm.at[halo : halo + 1], fbuf.at[block + 1 :], sems.at[10]))
    second = [
        pltpu.make_async_copy(src.at[split:rows], dst.at[split:rows], sems.at[11 + i])
        for i, (src, dst) in enumerate(slices)
    ]
    for c in first + second:
        c.start()
    f32 = jnp.float32
    step = stack.shape[0]

    def join(r0, n):
        part = pl.ds(r0, n)
        summed = (
            coef_ref[0] * fb_ref[part].astype(f32)
            + coef_ref[1] * rb_ref[part].astype(f32)
            + coef_ref[2] * own_ref[part].astype(f32)
            + coef_ref[3] * par_ref[part].astype(f32)
            + coef_ref[4] * ra_ref[part].astype(f32)
            + coef_ref[5] * fa_ref[part].astype(f32)
            + coef_ref[6] * routed_ref[part].astype(f32)
        )
        mixed_buf[part] = (summed * fbuf[part].astype(f32)).astype(jnp.bfloat16)

    def emit(r0, n, value):
        out_ref[r0 : r0 + n] = value.astype(jnp.bfloat16)

    for c in first:
        c.wait()
    join(0, split)
    r0 = 0
    while r0 + step + 2 <= split:
        conv_chunk(mixed_buf, w3_ref, stack, r0, step, emit)
        r0 += step
    for c in second:
        c.wait()
    join(split, rows - split)
    while r0 < block:
        n = min(step, block - r0)
        conv_chunk(mixed_buf, w3_ref, stack, r0, n, emit)
        r0 += n


def vmem():
    return pl.BlockSpec(memory_space=pltpu.VMEM)


def smem():
    return pl.BlockSpec(memory_space=pltpu.SMEM)


CHUNK = 2


def layers(bounds, above, image, below, w1, w2):
    block, cols, c = image.shape
    halo = below.shape[0] - 1
    rows = block + 2 * halo
    flops = 2 * 9 * c * c * cols * (2 * rows - 6)
    return pl.pallas_call(
        layers_kernel,
        out_shape=jax.ShapeDtypeStruct((rows - 4, cols, c), jnp.bfloat16),
        in_specs=[smem()] + [vmem()] * 5,
        out_specs=vmem(),
        scratch_shapes=[pltpu.VMEM((rows, cols, c), jnp.bfloat16),
                        pltpu.VMEM((rows - 2, cols, c), jnp.bfloat16),
                        pltpu.VMEM((CHUNK, cols, 3 * c), jnp.bfloat16)],
        cost_estimate=pl.CostEstimate(flops=flops, transcendentals=2 * rows * cols * c,
                                      bytes_accessed=4 * rows * cols * c + 4 * 9 * c * c),
    )(bounds, above, image, below, w1, w2)


def mix(coef, fb, rb, own, par, ra, fa, routed, above, frame, below, w3):
    block, cols, c = frame.shape
    flops = 2 * 9 * c * c * cols * block
    hbm = pl.BlockSpec(memory_space=pl.ANY)
    slab = pltpu.VMEM((block + 2, cols, c), jnp.bfloat16)
    return pl.pallas_call(
        mix_kernel,
        out_shape=jax.ShapeDtypeStruct((block, cols, c), jnp.bfloat16),
        in_specs=[smem()] + [hbm] * 11,
        out_specs=vmem(),
        scratch_shapes=[slab] * 7 + [
            slab,
            pltpu.VMEM(w3.shape, w3.dtype),
            slab,
            pltpu.VMEM((CHUNK, cols, 3 * c), jnp.bfloat16),
            pltpu.SemaphoreType.DMA((18,)),
        ],
        cost_estimate=pl.CostEstimate(flops=flops, transcendentals=0,
                                      bytes_accessed=18 * (block + 2) * cols * c + 2 * 9 * c * c),
    )(coef, fb, rb, own, par, ra, fa, routed, above, frame, below, w3)


def shards(
    event_slices,
    frame_features,
    exposure_start,
    exposure_end,
    intersection_us,
    conv_first,
    conv_second,
    conv_frame,
):
    image = event_slices[0]
    frame = frame_features[0]
    block = image.shape[0]
    height = block * lax.axis_size("rows")
    row0 = lax.axis_index("rows") * block

    down = jnp.concatenate([image[block - 3 :], frame[block - 1 :]], axis=0)
    up = jnp.concatenate([image[:3], frame[:1]], axis=0)
    from_above = shifted(down, "rows", 1)
    from_below = shifted(up, "rows", -1)

    count = lax.axis_size("tm")
    t = lax.axis_index("tm")
    intersection = intersection_us[0].astype(jnp.float32)
    window = intersection.shape[0]
    radius = (window - 1) // 2
    slice_index = t + jnp.arange(window, dtype=jnp.int32) - radius
    valid = (slice_index >= exposure_start[0]) & (slice_index <= exposure_end[0])
    weights = jnp.where(valid, intersection, jnp.float32(0.0))
    weights = weights / jnp.sum(weights)
    is_odd = (t % 2) == 1
    partner_weight = jnp.where(is_odd, weights[1], weights[3])
    routed_weight = jnp.where(is_odd, weights[4], weights[0])
    coef = jnp.concatenate([weights[:3], partner_weight[None], weights[3:], routed_weight[None]])
    bounds = jnp.stack([2 - row0, height - row0 + 2]).astype(jnp.int32)
    coef, bounds, image = lax.optimization_barrier((coef, bounds, image))

    second = layers(bounds, from_above, image, from_below, conv_first, conv_second)

    partner = lax.ppermute(second, "tm", [(i, i ^ 1) for i in range(count)])
    if count == 8:
        from_behind = lax.ppermute(second, "tm", [(0, 2), (1, 3), (3, 5), (4, 6), (5, 7)])
        from_ahead = lax.ppermute(second, "tm", [(2, 0), (3, 1), (4, 2), (6, 4), (7, 5)])
        hop = lax.ppermute(second, "tm", [(2, 6), (5, 1)])
        routed = lax.ppermute(hop, "tm", [(6, 4), (1, 3)])
    else:
        from_behind = shifted(second, "tm", 2)
        from_ahead = shifted(second, "tm", -2)
        routed = jnp.zeros_like(second)
    relay_behind = lax.ppermute(from_behind, "tm", [(i + 1, i) for i in range(2, count, 2)])
    relay_ahead = lax.ppermute(from_ahead, "tm", [(i, i + 1) for i in range(0, count - 2, 2)])
    result = mix(coef, from_behind, relay_behind, second, partner, relay_ahead, from_ahead, routed,
                 from_above, frame, from_below, conv_frame)
    return result[None]


def solution(mesh):
    return jax.shard_map(
        shards,
        mesh=mesh,
        in_specs=(
            P("tm", "rows", None, None),
            P("tm", "rows", None, None),
            P("tm"),
            P("tm"),
            P("tm", None),
            P(),
            P(),
            P(),
        ),
        out_specs=P("tm", "rows", None, None),
        check_vma=False,
    )
```

```python
import numpy as np
import jax
import jax.numpy as jnp
from jax import lax
from jax.experimental import pallas as pl
from jax.experimental.pallas import tpu as pltpu
from jax.sharding import PartitionSpec as P


def shifted(value, axis, steps):
    count = lax.axis_size(axis)
    initial, last = (max(0, -steps), min(count, count - steps))
    pairs = [(source, source + steps) for source in range(initial, last)]
    if not pairs:
        return jnp.zeros_like(value)
    return lax.ppermute(value, axis, pairs)


def gelu(v):
    c = np.float32(np.sqrt(2 / np.pi))
    return v * (0.5 * (1.0 + jnp.tanh(c * (v + 0.044715 * (v * v * v)))))


def conv_chunk(src_ref, w_ref, stack, r0, n, emit):
    cols, cin = src_ref.shape[1], src_ref.shape[2]
    cout = w_ref.shape[3]
    m = n * cols
    for a in range(3):
        stack[0:n, :, a * cin : (a + 1) * cin] = src_ref[r0 + a : r0 + a + n]
    lhs = stack[0:n].reshape(m, 3 * cin)
    taps = [
        jnp.dot(lhs, w_ref[:, b].reshape(3 * cin, cout), preferred_element_type=jnp.float32)
        for b in range(3)
    ]
    col = lax.broadcasted_iota(jnp.int32, (n, cols, cout), 1).reshape(m, cout)
    left = pltpu.roll(taps[0], shift=1, axis=0)
    right = pltpu.roll(taps[2], shift=m - 1, axis=0)
    out = taps[1] + jnp.where(col == 0, 0.0, left) + jnp.where(col == cols - 1, 0.0, right)
    emit(r0, n, out.reshape(n, cols, cout))


def conv_rows(src_ref, w_ref, stack, rows_out, emit):
    chunk = stack.shape[0]
    for r0 in range(0, rows_out, chunk):
        conv_chunk(src_ref, w_ref, stack, r0, min(chunk, rows_out - r0), emit)


def layers_kernel(bounds_ref, above_ref, image_ref, below_ref, w1_ref, w2_ref, out_ref, xbuf,
                  first_buf, stack):
    halo = below_ref.shape[0] - 1
    block = image_ref.shape[0]
    xbuf[0:halo] = above_ref[0:halo]
    xbuf[halo : halo + block] = image_ref[...]
    xbuf[halo + block :] = below_ref[0:halo]
    rows1 = block + 2 * halo - 2

    def emit_first(r0, n, value):
        value = gelu(value)
        row = lax.broadcasted_iota(jnp.int32, value.shape, 0) + r0
        inside = (row >= bounds_ref[0]) & (row < bounds_ref[1])
        first_buf[r0 : r0 + n] = jnp.where(inside, value, 0.0).astype(jnp.bfloat16)

    def emit_second(r0, n, value):
        out_ref[r0 : r0 + n] = gelu(value).astype(jnp.bfloat16)

    conv_rows(xbuf, w1_ref, stack, rows1, emit_first)
    conv_rows(first_buf, w2_ref, stack, rows1 - 2, emit_second)


def mix_kernel(coef_ref, *refs):
    (fb_hbm, rb_hbm, own_hbm, par_hbm, ra_hbm, fa_hbm, routed_hbm, above_hbm, frame_hbm, below_hbm,
     w3_hbm, out_ref, fb_ref, rb_ref, own_ref, par_ref, ra_ref, fa_ref, routed_ref, fbuf, w3_ref,
     mixed_buf, stack, sems) = refs
    block = frame_hbm.shape[0]
    rows = block + 2
    split = rows // 2 + 1
    slices = [(fb_hbm, fb_ref), (rb_hbm, rb_ref), (own_hbm, own_ref), (par_hbm, par_ref),
              (ra_hbm, ra_ref), (fa_hbm, fa_ref), (routed_hbm, routed_ref)]
    received = [coef_ref[7 + i] > 0.5 for i in range(len(slices))]
    halo = below_hbm.shape[0] - 1
    fixed = [
        pltpu.make_async_copy(w3_hbm, w3_ref, sems.at[0]),
        pltpu.make_async_copy(above_hbm.at[halo : halo + 1], fbuf.at[0:1], sems.at[8]),
        pltpu.make_async_copy(frame_hbm, fbuf.at[1 : block + 1], sems.at[9]),
        pltpu.make_async_copy(below_hbm.at[halo : halo + 1], fbuf.at[block + 1 :], sems.at[10]),
    ]
    first = [pltpu.make_async_copy(src.at[0:split], dst.at[0:split], sems.at[1 + i])
             for i, (src, dst) in enumerate(slices)]
    second = [pltpu.make_async_copy(src.at[split:rows], dst.at[split:rows], sems.at[11 + i])
              for i, (src, dst) in enumerate(slices)]
    for c in fixed:
        c.start()
    for group in (first, second):
        for flag, c in zip(received, group):
            pl.when(flag)(c.start)
    for flag, (src, dst) in zip(received, slices):
        @pl.when(jnp.logical_not(flag))
        def _():
            dst[...] = jnp.zeros(dst.shape, dst.dtype)
    f32 = jnp.float32
    step = stack.shape[0]

    def join(r0, n):
        part = pl.ds(r0, n)
        summed = (
            coef_ref[0] * fb_ref[part].astype(f32)
            + coef_ref[1] * rb_ref[part].astype(f32)
            + coef_ref[2] * own_ref[part].astype(f32)
            + coef_ref[3] * par_ref[part].astype(f32)
            + coef_ref[4] * ra_ref[part].astype(f32)
            + coef_ref[5] * fa_ref[part].astype(f32)
            + coef_ref[6] * routed_ref[part].astype(f32)
        )
        mixed_buf[part] = (summed * fbuf[part].astype(f32)).astype(jnp.bfloat16)

    def emit(r0, n, value):
        out_ref[r0 : r0 + n] = value.astype(jnp.bfloat16)

    for c in fixed:
        c.wait()
    for flag, c in zip(received, first):
        pl.when(flag)(c.wait)
    join(0, split)
    r0 = 0
    while r0 + step + 2 <= split:
        conv_chunk(mixed_buf, w3_ref, stack, r0, step, emit)
        r0 += step
    for flag, c in zip(received, second):
        pl.when(flag)(c.wait)
    join(split, rows - split)
    while r0 < block:
        n = min(step, block - r0)
        conv_chunk(mixed_buf, w3_ref, stack, r0, n, emit)
        r0 += n


def vmem():
    return pl.BlockSpec(memory_space=pltpu.VMEM)


def smem():
    return pl.BlockSpec(memory_space=pltpu.SMEM)


CHUNK = 2


def layers(bounds, above, image, below, w1, w2):
    block, cols, c = image.shape
    halo = below.shape[0] - 1
    rows = block + 2 * halo
    flops = 2 * 9 * c * c * cols * (2 * rows - 6)
    return pl.pallas_call(
        layers_kernel,
        out_shape=jax.ShapeDtypeStruct((rows - 4, cols, c), jnp.bfloat16),
        in_specs=[smem()] + [vmem()] * 5,
        out_specs=vmem(),
        scratch_shapes=[pltpu.VMEM((rows, cols, c), jnp.bfloat16),
                        pltpu.VMEM((rows - 2, cols, c), jnp.bfloat16),
                        pltpu.VMEM((CHUNK, cols, 3 * c), jnp.bfloat16)],
        cost_estimate=pl.CostEstimate(flops=flops, transcendentals=2 * rows * cols * c,
                                      bytes_accessed=4 * rows * cols * c + 4 * 9 * c * c),
    )(bounds, above, image, below, w1, w2)


def mix(coef, fb, rb, own, par, ra, fa, routed, above, frame, below, w3):
    block, cols, c = frame.shape
    flops = 2 * 9 * c * c * cols * block
    hbm = pl.BlockSpec(memory_space=pl.ANY)
    slab = pltpu.VMEM((block + 2, cols, c), jnp.bfloat16)
    return pl.pallas_call(
        mix_kernel,
        out_shape=jax.ShapeDtypeStruct((block, cols, c), jnp.bfloat16),
        in_specs=[smem()] + [hbm] * 11,
        out_specs=vmem(),
        scratch_shapes=[slab] * 7 + [
            slab,
            pltpu.VMEM(w3.shape, w3.dtype),
            slab,
            pltpu.VMEM((CHUNK, cols, 3 * c), jnp.bfloat16),
            pltpu.SemaphoreType.DMA((18,)),
        ],
        cost_estimate=pl.CostEstimate(flops=flops, transcendentals=0,
                                      bytes_accessed=18 * (block + 2) * cols * c + 2 * 9 * c * c),
    )(coef, fb, rb, own, par, ra, fa, routed, above, frame, below, w3)


def shards(
    event_slices,
    frame_features,
    exposure_start,
    exposure_end,
    intersection_us,
    conv_first,
    conv_second,
    conv_frame,
):
    image = event_slices[0]
    frame = frame_features[0]
    block = image.shape[0]
    height = block * lax.axis_size("rows")
    row0 = lax.axis_index("rows") * block

    down = jnp.concatenate([image[block - 3 :], frame[block - 1 :]], axis=0)
    up = jnp.concatenate([image[:3], frame[:1]], axis=0)
    from_above = shifted(down, "rows", 1)
    from_below = shifted(up, "rows", -1)

    count = lax.axis_size("tm")
    t = lax.axis_index("tm")
    intersection = intersection_us[0].astype(jnp.float32)
    window = intersection.shape[0]
    radius = (window - 1) // 2
    slice_index = t + jnp.arange(window, dtype=jnp.int32) - radius
    valid = (slice_index >= exposure_start[0]) & (slice_index <= exposure_end[0])
    weights = jnp.where(valid, intersection, jnp.float32(0.0))
    weights = weights / jnp.sum(weights)
    is_odd = (t % 2) == 1
    partner_weight = jnp.where(is_odd, weights[1], weights[3])
    routed_weight = jnp.where(is_odd, weights[4], weights[0])
    coef = jnp.concatenate([weights[:3], partner_weight[None], weights[3:], routed_weight[None]])
    bounds = jnp.stack([2 - row0, height - row0 + 2]).astype(jnp.int32)
    coef, bounds, image = lax.optimization_barrier((coef, bounds, image))

    second = layers(bounds, from_above, image, from_below, conv_first, conv_second)

    partner = lax.ppermute(second, "tm", [(i, i ^ 1) for i in range(count)])
    if count == 8:
        behind_pairs = [(0, 2), (1, 3), (3, 5), (4, 6), (5, 7)]
        ahead_pairs = [(2, 0), (3, 1), (4, 2), (6, 4), (7, 5)]
        routed_pairs = [(6, 4), (1, 3)]
        hop = lax.ppermute(second, "tm", [(2, 6), (5, 1)])
        routed = lax.ppermute(hop, "tm", routed_pairs)
    else:
        behind_pairs = [(i, i + 2) for i in range(count - 2)]
        ahead_pairs = [(i + 2, i) for i in range(count - 2)]
        routed_pairs = []
        routed = jnp.zeros_like(second)
    from_behind = lax.ppermute(second, "tm", behind_pairs)
    from_ahead = lax.ppermute(second, "tm", ahead_pairs)
    behind_relays = [(i + 1, i) for i in range(2, count, 2)]
    ahead_relays = [(i, i + 1) for i in range(0, count - 2, 2)]
    relay_behind = lax.ppermute(from_behind, "tm", behind_relays)
    relay_ahead = lax.ppermute(from_ahead, "tm", ahead_relays)
    every = [(i, i) for i in range(count)]
    table = np.zeros((count, 7), np.float32)
    for column, pairs in enumerate([behind_pairs, behind_relays, every, every, ahead_relays, ahead_pairs,
                                    routed_pairs]):
        for _, target in pairs:
            table[target, column] = 1.0
    coef = jnp.concatenate([coef, jnp.asarray(table)[t]])
    result = mix(coef, from_behind, relay_behind, second, partner, relay_ahead, from_ahead, routed,
                 from_above, frame, from_below, conv_frame)
    return result[None]


def solution(mesh):
    return jax.shard_map(
        shards,
        mesh=mesh,
        in_specs=(
            P("tm", "rows", None, None),
            P("tm", "rows", None, None),
            P("tm"),
            P("tm"),
            P("tm", None),
            P(),
            P(),
            P(),
        ),
        out_specs=P("tm", "rows", None, None),
        check_vma=False,
    )
```

```python
import numpy as np
import jax
import jax.numpy as jnp
from jax import lax
from jax.experimental import pallas as pl
from jax.experimental.pallas import tpu as pltpu
from jax.sharding import PartitionSpec as P


def shifted(value, axis, steps):
    count = lax.axis_size(axis)
    initial, last = (max(0, -steps), min(count, count - steps))
    pairs = [(source, source + steps) for source in range(initial, last)]
    if not pairs:
        return jnp.zeros_like(value)
    return lax.ppermute(value, axis, pairs)


def gelu(v):
    c = np.float32(np.sqrt(2 / np.pi))
    return v * (0.5 * (1.0 + jnp.tanh(c * (v + 0.044715 * (v * v * v)))))


def conv_rows(src_ref, w_ref, stack, rows_out, emit):
    chunk = stack.shape[0]
    cols, cin = src_ref.shape[1], src_ref.shape[2]
    cout = w_ref.shape[3]
    r0 = 0
    while r0 < rows_out:
        n = min(chunk, rows_out - r0)
        m = n * cols
        for a in range(3):
            stack[0:n, :, a * cin : (a + 1) * cin] = src_ref[r0 + a : r0 + a + n]
        lhs = stack[0:n].reshape(m, 3 * cin)
        taps = [
            jnp.dot(lhs, w_ref[:, b].reshape(3 * cin, cout), preferred_element_type=jnp.float32)
            for b in range(3)
        ]
        col = lax.broadcasted_iota(jnp.int32, (n, cols, cout), 1).reshape(m, cout)
        left = pltpu.roll(taps[0], shift=1, axis=0)
        right = pltpu.roll(taps[2], shift=m - 1, axis=0)
        out = taps[1] + jnp.where(col == 0, 0.0, left) + jnp.where(col == cols - 1, 0.0, right)
        emit(r0, n, out.reshape(n, cols, cout))
        r0 += n


def layers_kernel(bounds_ref, above_ref, image_ref, below_ref, w1_ref, w2_ref, out_ref, xbuf,
                  first_buf, stack):
    halo = below_ref.shape[0]
    block = image_ref.shape[0]
    xbuf[0:halo] = above_ref[0:halo]
    xbuf[halo : halo + block] = image_ref[...]
    xbuf[halo + block :] = below_ref[0:halo]
    rows1 = block + 2 * halo - 2

    def emit_first(r0, n, value):
        value = gelu(value)
        row = lax.broadcasted_iota(jnp.int32, value.shape, 0) + r0
        inside = (row >= bounds_ref[0]) & (row < bounds_ref[1])
        first_buf[r0 : r0 + n] = jnp.where(inside, value, 0.0).astype(jnp.bfloat16)

    def emit_second(r0, n, value):
        out_ref[r0 : r0 + n] = gelu(value).astype(jnp.bfloat16)

    conv_rows(xbuf, w1_ref, stack, rows1, emit_first)
    conv_rows(first_buf, w2_ref, stack, rows1 - 2, emit_second)


def join_kernel(coef_ref, fb_ref, rb_ref, own_ref, par_ref, ra_ref, fa_ref, routed_ref, frame_ref,
                mixed_ref, top_ref, bottom_ref):
    f32 = jnp.float32
    block = frame_ref.shape[0]
    for r0 in range(0, block, 2):
        rows = pl.ds(r0, 2)
        summed = (
            coef_ref[0] * fb_ref[rows].astype(f32)
            + coef_ref[1] * rb_ref[rows].astype(f32)
            + coef_ref[2] * own_ref[rows].astype(f32)
            + coef_ref[3] * par_ref[rows].astype(f32)
            + coef_ref[4] * ra_ref[rows].astype(f32)
            + coef_ref[5] * fa_ref[rows].astype(f32)
            + coef_ref[6] * routed_ref[rows].astype(f32)
        )
        mixed_ref[rows] = (summed * frame_ref[rows].astype(f32)).astype(jnp.bfloat16)
    top_ref[...] = mixed_ref[0:1]
    bottom_ref[...] = mixed_ref[block - 1 :]


def interior_kernel(mixed_ref, w3_ref, out_ref, stack):
    def emit(r0, n, value):
        out_ref[r0 : r0 + n] = value.astype(jnp.bfloat16)

    conv_rows(mixed_ref, w3_ref, stack, mixed_ref.shape[0] - 2, emit)


def edges_kernel(above_ref, mixed_ref, below_ref, inner_ref, w3_ref, out_ref, ext, stack):
    block = mixed_ref.shape[0]

    def emit_at(row):
        def emit(r0, n, value):
            out_ref[row : row + 1] = value.astype(jnp.bfloat16)
        return emit

    ext[0:1] = above_ref[...]
    ext[1:3] = mixed_ref[0:2]
    conv_rows(ext, w3_ref, stack, 1, emit_at(0))
    ext[0:2] = mixed_ref[block - 2 :]
    ext[2:3] = below_ref[...]
    conv_rows(ext, w3_ref, stack, 1, emit_at(block - 1))
    out_ref[1 : block - 1] = inner_ref[...]


def vmem():
    return pl.BlockSpec(memory_space=pltpu.VMEM)


def smem():
    return pl.BlockSpec(memory_space=pltpu.SMEM)


CHUNK = 2


def layers(bounds, above, image, below, w1, w2):
    block, cols, c = image.shape
    halo = below.shape[0]
    rows = block + 2 * halo
    flops = 2 * 9 * c * c * cols * (2 * rows - 6)
    return pl.pallas_call(
        layers_kernel,
        out_shape=jax.ShapeDtypeStruct((rows - 4, cols, c), jnp.bfloat16),
        in_specs=[smem()] + [vmem()] * 5,
        out_specs=vmem(),
        scratch_shapes=[pltpu.VMEM((rows, cols, c), jnp.bfloat16),
                        pltpu.VMEM((rows - 2, cols, c), jnp.bfloat16),
                        pltpu.VMEM((CHUNK, cols, 3 * c), jnp.bfloat16)],
        cost_estimate=pl.CostEstimate(flops=flops, transcendentals=2 * rows * cols * c,
                                      bytes_accessed=4 * rows * cols * c + 4 * 9 * c * c),
    )(bounds, above, image, below, w1, w2)


def join(coef, fb, rb, own, par, ra, fa, routed, frame):
    block, cols, c = frame.shape
    row = jax.ShapeDtypeStruct((1, cols, c), jnp.bfloat16)
    return pl.pallas_call(
        join_kernel,
        out_shape=(jax.ShapeDtypeStruct((block, cols, c), jnp.bfloat16), row, row),
        in_specs=[smem()] + [vmem()] * 8,
        out_specs=(vmem(), vmem(), vmem()),
        cost_estimate=pl.CostEstimate(flops=16 * block * cols * c, transcendentals=0,
                                      bytes_accessed=18 * block * cols * c),
    )(coef, fb, rb, own, par, ra, fa, routed, frame)


def frame_conv(mixed, from_above, from_below, w3):
    block, cols, c = mixed.shape
    inner = pl.pallas_call(
        interior_kernel,
        out_shape=jax.ShapeDtypeStruct((block - 2, cols, c), jnp.bfloat16),
        in_specs=[vmem()] * 2,
        out_specs=vmem(),
        scratch_shapes=[pltpu.VMEM((CHUNK, cols, 3 * c), jnp.bfloat16)],
        cost_estimate=pl.CostEstimate(flops=2 * 9 * c * c * cols * (block - 2), transcendentals=0,
                                      bytes_accessed=4 * block * cols * c + 2 * 9 * c * c),
    )(mixed, w3)
    return pl.pallas_call(
        edges_kernel,
        out_shape=jax.ShapeDtypeStruct((block, cols, c), jnp.bfloat16),
        in_specs=[vmem()] * 5,
        out_specs=vmem(),
        scratch_shapes=[pltpu.VMEM((3, cols, c), jnp.bfloat16),
                        pltpu.VMEM((1, cols, 3 * c), jnp.bfloat16)],
        cost_estimate=pl.CostEstimate(flops=2 * 9 * c * c * cols * 2, transcendentals=0,
                                      bytes_accessed=4 * block * cols * c + 2 * 9 * c * c),
    )(from_above, mixed, from_below, inner, w3)


def shards(
    event_slices,
    frame_features,
    exposure_start,
    exposure_end,
    intersection_us,
    conv_first,
    conv_second,
    conv_frame,
):
    image = event_slices[0]
    frame = frame_features[0]
    block = image.shape[0]
    height = block * lax.axis_size("rows")
    row0 = lax.axis_index("rows") * block

    from_above = shifted(image[block - 2 :], "rows", 1)
    from_below = shifted(image[:2], "rows", -1)

    count = lax.axis_size("tm")
    t = lax.axis_index("tm")
    intersection = intersection_us[0].astype(jnp.float32)
    window = intersection.shape[0]
    radius = (window - 1) // 2
    slice_index = t + jnp.arange(window, dtype=jnp.int32) - radius
    valid = (slice_index >= exposure_start[0]) & (slice_index <= exposure_end[0])
    weights = jnp.where(valid, intersection, jnp.float32(0.0))
    weights = weights / jnp.sum(weights)
    is_odd = (t % 2) == 1
    partner_weight = jnp.where(is_odd, weights[1], weights[3])
    routed_weight = jnp.where(is_odd, weights[4], weights[0])
    coef = jnp.concatenate([weights[:3], partner_weight[None], weights[3:], routed_weight[None]])
    bounds = jnp.stack([1 - row0, height - row0 + 1]).astype(jnp.int32)
    coef, bounds, image = lax.optimization_barrier((coef, bounds, image))

    second = layers(bounds, from_above, image, from_below, conv_first, conv_second)

    partner = lax.ppermute(second, "tm", [(i, i ^ 1) for i in range(count)])
    if count == 8:
        from_behind = lax.ppermute(second, "tm", [(0, 2), (1, 3), (3, 5), (4, 6), (5, 7)])
        from_ahead = lax.ppermute(second, "tm", [(2, 0), (3, 1), (4, 2), (6, 4), (7, 5)])
        hop = lax.ppermute(second, "tm", [(2, 6), (5, 1)])
        routed = lax.ppermute(hop, "tm", [(6, 4), (1, 3)])
    else:
        from_behind = shifted(second, "tm", 2)
        from_ahead = shifted(second, "tm", -2)
        routed = jnp.zeros_like(second)
    relay_behind = lax.ppermute(from_behind, "tm", [(i + 1, i) for i in range(2, count, 2)])
    relay_ahead = lax.ppermute(from_ahead, "tm", [(i, i + 1) for i in range(0, count - 2, 2)])
    mixed, top, bottom = join(coef, from_behind, relay_behind, second, partner, relay_ahead,
                              from_ahead, routed, frame)
    mixed_above = shifted(bottom, "rows", 1)
    mixed_below = shifted(top, "rows", -1)
    result = frame_conv(mixed, mixed_above, mixed_below, conv_frame)
    return result[None]


def solution(mesh):
    return jax.shard_map(
        shards,
        mesh=mesh,
        in_specs=(
            P("tm", "rows", None, None),
            P("tm", "rows", None, None),
            P("tm"),
            P("tm"),
            P("tm", None),
            P(),
            P(),
            P(),
        ),
        out_specs=P("tm", "rows", None, None),
        check_vma=False,
    )
```

```python
import numpy as np
import jax
import jax.numpy as jnp
from jax import lax
from jax.experimental import pallas as pl
from jax.experimental.pallas import tpu as pltpu
from jax.sharding import PartitionSpec as P


def shifted(value, axis, steps):
    count = lax.axis_size(axis)
    initial, last = (max(0, -steps), min(count, count - steps))
    pairs = [(source, source + steps) for source in range(initial, last)]
    if not pairs:
        return jnp.zeros_like(value)
    return lax.ppermute(value, axis, pairs)


def gelu(v):
    c = np.float32(np.sqrt(2 / np.pi))
    return v * (0.5 * (1.0 + jnp.tanh(c * (v + 0.044715 * (v * v * v)))))


def conv_rows(src_ref, w_ref, stack, rows_out, emit):
    chunk = stack.shape[0]
    cols, cin = src_ref.shape[1], src_ref.shape[2]
    cout = w_ref.shape[3]
    r0 = 0
    while r0 < rows_out:
        n = min(chunk, rows_out - r0)
        m = n * cols
        for a in range(3):
            stack[0:n, :, a * cin : (a + 1) * cin] = src_ref[r0 + a : r0 + a + n]
        lhs = stack[0:n].reshape(m, 3 * cin)
        taps = [
            jnp.dot(lhs, w_ref[:, b].reshape(3 * cin, cout), preferred_element_type=jnp.float32)
            for b in range(3)
        ]
        col = lax.broadcasted_iota(jnp.int32, (n, cols, cout), 1).reshape(m, cout)
        left = pltpu.roll(taps[0], shift=1, axis=0)
        right = pltpu.roll(taps[2], shift=m - 1, axis=0)
        out = taps[1] + jnp.where(col == 0, 0.0, left) + jnp.where(col == cols - 1, 0.0, right)
        emit(r0, n, out.reshape(n, cols, cout))
        r0 += n


def layers_kernel(bounds_ref, above_ref, image_ref, below_ref, w1_ref, w2_ref, out_ref, xbuf,
                  first_buf, stack):
    halo = below_ref.shape[0] - 1
    block = image_ref.shape[0]
    xbuf[0:halo] = above_ref[0:halo]
    xbuf[halo : halo + block] = image_ref[...]
    xbuf[halo + block :] = below_ref[0:halo]
    rows1 = block + 2 * halo - 2

    def emit_first(r0, n, value):
        value = gelu(value)
        row = lax.broadcasted_iota(jnp.int32, value.shape, 0) + r0
        inside = (row >= bounds_ref[0]) & (row < bounds_ref[1])
        first_buf[r0 : r0 + n] = jnp.where(inside, value, 0.0).astype(jnp.bfloat16)

    def emit_second(r0, n, value):
        out_ref[r0 : r0 + n] = gelu(value).astype(jnp.bfloat16)

    conv_rows(xbuf, w1_ref, stack, rows1, emit_first)
    conv_rows(first_buf, w2_ref, stack, rows1 - 2, emit_second)


def mix_kernel(coef_ref, fb_ref, fbo_ref, rb_ref, own_ref, par_ref, ra_ref, fa_ref, routed_ref,
               above_ref, frame_ref, below_ref, w3_ref, out_ref, fbuf, mixed_buf, stack):
    halo = below_ref.shape[0] - 1
    block = frame_ref.shape[0]
    fbuf[0:1] = above_ref[halo : halo + 1]
    fbuf[1 : block + 1] = frame_ref[...]
    fbuf[block + 1 :] = below_ref[halo : halo + 1]
    f32 = jnp.float32
    step = stack.shape[0]
    for r0 in range(0, block + 2, step):
        rows = pl.ds(r0, min(step, block + 2 - r0))
        summed = (
            coef_ref[0] * (fb_ref[rows].astype(f32) + fbo_ref[rows].astype(f32))
            + coef_ref[1] * rb_ref[rows].astype(f32)
            + coef_ref[2] * own_ref[rows].astype(f32)
            + coef_ref[3] * par_ref[rows].astype(f32)
            + coef_ref[4] * ra_ref[rows].astype(f32)
            + coef_ref[5] * fa_ref[rows].astype(f32)
            + coef_ref[6] * routed_ref[rows].astype(f32)
        )
        mixed_buf[rows] = (summed * fbuf[rows].astype(f32)).astype(jnp.bfloat16)

    def emit(r0, n, value):
        out_ref[r0 : r0 + n] = value.astype(jnp.bfloat16)

    conv_rows(mixed_buf, w3_ref, stack, block, emit)


def vmem():
    return pl.BlockSpec(memory_space=pltpu.VMEM)


def smem():
    return pl.BlockSpec(memory_space=pltpu.SMEM)


CHUNK = 2


def layers(bounds, above, image, below, w1, w2):
    block, cols, c = image.shape
    halo = below.shape[0] - 1
    rows = block + 2 * halo
    flops = 2 * 9 * c * c * cols * (2 * rows - 6)
    return pl.pallas_call(
        layers_kernel,
        out_shape=jax.ShapeDtypeStruct((rows - 4, cols, c), jnp.bfloat16),
        in_specs=[smem()] + [vmem()] * 5,
        out_specs=vmem(),
        scratch_shapes=[pltpu.VMEM((rows, cols, c), jnp.bfloat16),
                        pltpu.VMEM((rows - 2, cols, c), jnp.bfloat16),
                        pltpu.VMEM((CHUNK, cols, 3 * c), jnp.bfloat16)],
        cost_estimate=pl.CostEstimate(flops=flops, transcendentals=2 * rows * cols * c,
                                      bytes_accessed=4 * rows * cols * c + 4 * 9 * c * c),
    )(bounds, above, image, below, w1, w2)


def mix(coef, fb, fbo, rb, own, par, ra, fa, routed, above, frame, below, w3):
    block, cols, c = frame.shape
    flops = 2 * 9 * c * c * cols * block
    return pl.pallas_call(
        mix_kernel,
        out_shape=jax.ShapeDtypeStruct((block, cols, c), jnp.bfloat16),
        in_specs=[smem()] + [vmem()] * 12,
        out_specs=vmem(),
        scratch_shapes=[pltpu.VMEM((block + 2, cols, c), jnp.bfloat16),
                        pltpu.VMEM((block + 2, cols, c), jnp.bfloat16),
                        pltpu.VMEM((CHUNK, cols, 3 * c), jnp.bfloat16)],
        cost_estimate=pl.CostEstimate(flops=flops, transcendentals=0,
                                      bytes_accessed=18 * (block + 2) * cols * c + 2 * 9 * c * c),
    )(coef, fb, fbo, rb, own, par, ra, fa, routed, above, frame, below, w3)


def shards(
    event_slices,
    frame_features,
    exposure_start,
    exposure_end,
    intersection_us,
    conv_first,
    conv_second,
    conv_frame,
):
    image = event_slices[0]
    frame = frame_features[0]
    block = image.shape[0]
    height = block * lax.axis_size("rows")
    row0 = lax.axis_index("rows") * block

    down = jnp.concatenate([image[block - 3 :], frame[block - 1 :]], axis=0)
    up = jnp.concatenate([image[:3], frame[:1]], axis=0)
    from_above = shifted(down, "rows", 1)
    from_below = shifted(up, "rows", -1)

    count = lax.axis_size("tm")
    t = lax.axis_index("tm")
    intersection = intersection_us[0].astype(jnp.float32)
    window = intersection.shape[0]
    radius = (window - 1) // 2
    slice_index = t + jnp.arange(window, dtype=jnp.int32) - radius
    valid = (slice_index >= exposure_start[0]) & (slice_index <= exposure_end[0])
    weights = jnp.where(valid, intersection, jnp.float32(0.0))
    weights = weights / jnp.sum(weights)
    is_odd = (t % 2) == 1
    partner_weight = jnp.where(is_odd, weights[1], weights[3])
    routed_weight = jnp.where(is_odd, weights[4], weights[0])
    coef = jnp.concatenate([weights[:3], partner_weight[None], weights[3:], routed_weight[None]])
    bounds = jnp.stack([2 - row0, height - row0 + 2]).astype(jnp.int32)
    coef, bounds, image = lax.optimization_barrier((coef, bounds, image))

    second = layers(bounds, from_above, image, from_below, conv_first, conv_second)

    partner = lax.ppermute(second, "tm", [(i, i ^ 1) for i in range(count)])
    if count == 8:
        behind_pairs = [(0, 2), (1, 3), (3, 5), (4, 6), (5, 7)]
        from_ahead = lax.ppermute(second, "tm", [(2, 0), (3, 1), (4, 2), (6, 4), (7, 5)])
        hop = lax.ppermute(second, "tm", [(2, 6), (5, 1)])
        routed = lax.ppermute(hop, "tm", [(6, 4), (1, 3)])
    else:
        behind_pairs = [(i, i + 2) for i in range(count - 2)]
        from_ahead = shifted(second, "tm", -2)
        routed = jnp.zeros_like(second)
    behind_even = lax.ppermute(second, "tm", [(a, b) for a, b in behind_pairs if b % 2 == 0])
    behind_odd = lax.ppermute(second, "tm", [(a, b) for a, b in behind_pairs if b % 2 == 1])
    relay_behind = lax.ppermute(behind_odd, "tm", [(i + 1, i) for i in range(2, count, 2)])
    relay_ahead = lax.ppermute(from_ahead, "tm", [(i, i + 1) for i in range(0, count - 2, 2)])
    result = mix(coef, behind_even, behind_odd, relay_behind, second, partner, relay_ahead, from_ahead,
                 routed, from_above, frame, from_below, conv_frame)
    return result[None]


def solution(mesh):
    return jax.shard_map(
        shards,
        mesh=mesh,
        in_specs=(
            P("tm", "rows", None, None),
            P("tm", "rows", None, None),
            P("tm"),
            P("tm"),
            P("tm", None),
            P(),
            P(),
            P(),
        ),
        out_specs=P("tm", "rows", None, None),
        check_vma=False,
    )
```

```python
import numpy as np
import jax
import jax.numpy as jnp
from jax import lax
from jax.experimental import pallas as pl
from jax.experimental.pallas import tpu as pltpu
from jax.sharding import PartitionSpec as P


def shifted(value, axis, steps):
    count = lax.axis_size(axis)
    initial, last = (max(0, -steps), min(count, count - steps))
    pairs = [(source, source + steps) for source in range(initial, last)]
    if not pairs:
        return jnp.zeros_like(value)
    return lax.ppermute(value, axis, pairs)


def gelu(v):
    c = np.float32(np.sqrt(2 / np.pi))
    return v * (0.5 * (1.0 + jnp.tanh(c * (v + 0.044715 * (v * v * v)))))


def conv_rows(src_ref, w_ref, stack, rows_out, emit):
    chunk = stack.shape[0]
    cols, cin = src_ref.shape[1], src_ref.shape[2]
    cout = w_ref.shape[3]
    r0 = 0
    while r0 < rows_out:
        n = min(chunk, rows_out - r0)
        m = n * cols
        for a in range(3):
            stack[0:n, :, a * cin : (a + 1) * cin] = src_ref[r0 + a : r0 + a + n]
        lhs = stack[0:n].reshape(m, 3 * cin)
        taps = [
            jnp.dot(lhs, w_ref[:, b].reshape(3 * cin, cout), preferred_element_type=jnp.float32)
            for b in range(3)
        ]
        col = lax.broadcasted_iota(jnp.int32, (n, cols, cout), 1).reshape(m, cout)
        left = pltpu.roll(taps[0], shift=1, axis=0)
        right = pltpu.roll(taps[2], shift=m - 1, axis=0)
        out = taps[1] + jnp.where(col == 0, 0.0, left) + jnp.where(col == cols - 1, 0.0, right)
        emit(r0, n, out.reshape(n, cols, cout))
        r0 += n


def layers_kernel(bounds_ref, above_ref, image_ref, below_ref, w1_ref, w2_ref, out_ref, xbuf,
                  first_buf, stack):
    halo = below_ref.shape[0] - 1
    block = image_ref.shape[0]
    xbuf[0:halo] = above_ref[0:halo]
    xbuf[halo : halo + block] = image_ref[...]
    xbuf[halo + block :] = below_ref[0:halo]
    rows1 = block + 2 * halo - 2

    def emit_first(r0, n, value):
        value = gelu(value)
        row = lax.broadcasted_iota(jnp.int32, value.shape, 0) + r0
        inside = (row >= bounds_ref[0]) & (row < bounds_ref[1])
        first_buf[r0 : r0 + n] = jnp.where(inside, value, 0.0).astype(jnp.bfloat16)

    def emit_second(r0, n, value):
        out_ref[r0 : r0 + n] = gelu(value).astype(jnp.bfloat16)

    conv_rows(xbuf, w1_ref, stack, rows1, emit_first)
    conv_rows(first_buf, w2_ref, stack, rows1 - 2, emit_second)


def mix_kernel(coef_ref, fb_ref, fbo_ref, rb_ref, own_ref, par_ref, ra_ref, fa_ref, fao_ref, routed_ref,
               above_ref, frame_ref, below_ref, w3_ref, out_ref, fbuf, mixed_buf, stack):
    halo = below_ref.shape[0] - 1
    block = frame_ref.shape[0]
    fbuf[0:1] = above_ref[halo : halo + 1]
    fbuf[1 : block + 1] = frame_ref[...]
    fbuf[block + 1 :] = below_ref[halo : halo + 1]
    f32 = jnp.float32
    step = stack.shape[0]
    for r0 in range(0, block + 2, step):
        rows = pl.ds(r0, min(step, block + 2 - r0))
        summed = (
            coef_ref[0] * (fb_ref[rows].astype(f32) + fbo_ref[rows].astype(f32))
            + coef_ref[1] * rb_ref[rows].astype(f32)
            + coef_ref[2] * own_ref[rows].astype(f32)
            + coef_ref[3] * par_ref[rows].astype(f32)
            + coef_ref[4] * ra_ref[rows].astype(f32)
            + coef_ref[5] * (fa_ref[rows].astype(f32) + fao_ref[rows].astype(f32))
            + coef_ref[6] * routed_ref[rows].astype(f32)
        )
        mixed_buf[rows] = (summed * fbuf[rows].astype(f32)).astype(jnp.bfloat16)

    def emit(r0, n, value):
        out_ref[r0 : r0 + n] = value.astype(jnp.bfloat16)

    conv_rows(mixed_buf, w3_ref, stack, block, emit)


def vmem():
    return pl.BlockSpec(memory_space=pltpu.VMEM)


def smem():
    return pl.BlockSpec(memory_space=pltpu.SMEM)


CHUNK = 2


def layers(bounds, above, image, below, w1, w2):
    block, cols, c = image.shape
    halo = below.shape[0] - 1
    rows = block + 2 * halo
    flops = 2 * 9 * c * c * cols * (2 * rows - 6)
    return pl.pallas_call(
        layers_kernel,
        out_shape=jax.ShapeDtypeStruct((rows - 4, cols, c), jnp.bfloat16),
        in_specs=[smem()] + [vmem()] * 5,
        out_specs=vmem(),
        scratch_shapes=[pltpu.VMEM((rows, cols, c), jnp.bfloat16),
                        pltpu.VMEM((rows - 2, cols, c), jnp.bfloat16),
                        pltpu.VMEM((CHUNK, cols, 3 * c), jnp.bfloat16)],
        cost_estimate=pl.CostEstimate(flops=flops, transcendentals=2 * rows * cols * c,
                                      bytes_accessed=4 * rows * cols * c + 4 * 9 * c * c),
    )(bounds, above, image, below, w1, w2)


def mix(coef, fb, fbo, rb, own, par, ra, fa, fao, routed, above, frame, below, w3):
    block, cols, c = frame.shape
    flops = 2 * 9 * c * c * cols * block
    return pl.pallas_call(
        mix_kernel,
        out_shape=jax.ShapeDtypeStruct((block, cols, c), jnp.bfloat16),
        in_specs=[smem()] + [vmem()] * 13,
        out_specs=vmem(),
        scratch_shapes=[pltpu.VMEM((block + 2, cols, c), jnp.bfloat16),
                        pltpu.VMEM((block + 2, cols, c), jnp.bfloat16),
                        pltpu.VMEM((CHUNK, cols, 3 * c), jnp.bfloat16)],
        cost_estimate=pl.CostEstimate(flops=flops, transcendentals=0,
                                      bytes_accessed=18 * (block + 2) * cols * c + 2 * 9 * c * c),
    )(coef, fb, fbo, rb, own, par, ra, fa, fao, routed, above, frame, below, w3)


def shards(
    event_slices,
    frame_features,
    exposure_start,
    exposure_end,
    intersection_us,
    conv_first,
    conv_second,
    conv_frame,
):
    image = event_slices[0]
    frame = frame_features[0]
    block = image.shape[0]
    height = block * lax.axis_size("rows")
    row0 = lax.axis_index("rows") * block

    down = jnp.concatenate([image[block - 3 :], frame[block - 1 :]], axis=0)
    up = jnp.concatenate([image[:3], frame[:1]], axis=0)
    from_above = shifted(down, "rows", 1)
    from_below = shifted(up, "rows", -1)

    count = lax.axis_size("tm")
    t = lax.axis_index("tm")
    intersection = intersection_us[0].astype(jnp.float32)
    window = intersection.shape[0]
    radius = (window - 1) // 2
    slice_index = t + jnp.arange(window, dtype=jnp.int32) - radius
    valid = (slice_index >= exposure_start[0]) & (slice_index <= exposure_end[0])
    weights = jnp.where(valid, intersection, jnp.float32(0.0))
    weights = weights / jnp.sum(weights)
    is_odd = (t % 2) == 1
    partner_weight = jnp.where(is_odd, weights[1], weights[3])
    routed_weight = jnp.where(is_odd, weights[4], weights[0])
    coef = jnp.concatenate([weights[:3], partner_weight[None], weights[3:], routed_weight[None]])
    bounds = jnp.stack([2 - row0, height - row0 + 2]).astype(jnp.int32)
    coef, bounds, image = lax.optimization_barrier((coef, bounds, image))

    second = layers(bounds, from_above, image, from_below, conv_first, conv_second)

    partner = lax.ppermute(second, "tm", [(i, i ^ 1) for i in range(count)])
    if count == 8:
        behind_pairs = [(0, 2), (1, 3), (3, 5), (4, 6), (5, 7)]
        ahead_pairs = [(2, 0), (3, 1), (4, 2), (6, 4), (7, 5)]
        hop = lax.ppermute(second, "tm", [(2, 6), (5, 1)])
        routed = lax.ppermute(hop, "tm", [(6, 4), (1, 3)])
    else:
        behind_pairs = [(i, i + 2) for i in range(count - 2)]
        ahead_pairs = [(i + 2, i) for i in range(count - 2)]
        routed = jnp.zeros_like(second)
    behind_even = lax.ppermute(second, "tm", [(a, b) for a, b in behind_pairs if b % 2 == 0])
    behind_odd = lax.ppermute(second, "tm", [(a, b) for a, b in behind_pairs if b % 2 == 1])
    relay_behind = lax.ppermute(behind_odd, "tm", [(i + 1, i) for i in range(2, count, 2)])
    ahead_even = lax.ppermute(second, "tm", [(a, b) for a, b in ahead_pairs if b % 2 == 0])
    ahead_odd = lax.ppermute(second, "tm", [(a, b) for a, b in ahead_pairs if b % 2 == 1])
    relay_ahead = lax.ppermute(ahead_even, "tm", [(i, i + 1) for i in range(0, count - 2, 2)])
    result = mix(coef, behind_even, behind_odd, relay_behind, second, partner, relay_ahead, ahead_even,
                 ahead_odd, routed, from_above, frame, from_below, conv_frame)
    return result[None]


def solution(mesh):
    return jax.shard_map(
        shards,
        mesh=mesh,
        in_specs=(
            P("tm", "rows", None, None),
            P("tm", "rows", None, None),
            P("tm"),
            P("tm"),
            P("tm", None),
            P(),
            P(),
            P(),
        ),
        out_specs=P("tm", "rows", None, None),
        check_vma=False,
    )
```

```python
import numpy as np
import jax
import jax.numpy as jnp
from jax import lax
from jax.experimental import pallas as pl
from jax.experimental.pallas import tpu as pltpu
from jax.sharding import PartitionSpec as P


def shifted(value, axis, steps):
    count = lax.axis_size(axis)
    initial, last = (max(0, -steps), min(count, count - steps))
    pairs = [(source, source + steps) for source in range(initial, last)]
    if not pairs:
        return jnp.zeros_like(value)
    return lax.ppermute(value, axis, pairs)


def gelu(v):
    c = np.float32(np.sqrt(2 / np.pi))
    k = np.float32(np.sqrt(2 / np.pi) * 0.044715)
    h = 0.5 * v
    return h + h * jnp.tanh(v * (c + k * (v * v)))


def conv_rows(src_ref, w_ref, stack, rows_out, emit):
    chunk = stack.shape[0]
    cols, cin = src_ref.shape[1], src_ref.shape[2]
    cout = w_ref.shape[3]
    r0 = 0
    while r0 < rows_out:
        n = min(chunk, rows_out - r0)
        m = n * cols
        for a in range(3):
            stack[0:n, :, a * cin : (a + 1) * cin] = src_ref[r0 + a : r0 + a + n]
        lhs = stack[0:n].reshape(m, 3 * cin)
        taps = [
            jnp.dot(lhs, w_ref[:, b].reshape(3 * cin, cout), preferred_element_type=jnp.float32)
            for b in range(3)
        ]
        col = lax.broadcasted_iota(jnp.int32, (n, cols, cout), 1).reshape(m, cout)
        left = pltpu.roll(taps[0], shift=1, axis=0)
        right = pltpu.roll(taps[2], shift=m - 1, axis=0)
        out = taps[1] + jnp.where(col == 0, 0.0, left) + jnp.where(col == cols - 1, 0.0, right)
        emit(r0, n, out.reshape(n, cols, cout))
        r0 += n


def layers_kernel(bounds_ref, above_ref, image_ref, below_ref, w1_ref, w2_ref, out_ref, xbuf,
                  first_buf, stack):
    halo = below_ref.shape[0] - 1
    block = image_ref.shape[0]
    xbuf[0:halo] = above_ref[0:halo]
    xbuf[halo : halo + block] = image_ref[...]
    xbuf[halo + block :] = below_ref[0:halo]
    rows1 = block + 2 * halo - 2

    def emit_first(r0, n, value):
        value = gelu(value)
        row = lax.broadcasted_iota(jnp.int32, value.shape, 0) + r0
        inside = (row >= bounds_ref[0]) & (row < bounds_ref[1])
        first_buf[r0 : r0 + n] = jnp.where(inside, value, 0.0).astype(jnp.bfloat16)

    def emit_second(r0, n, value):
        out_ref[r0 : r0 + n] = gelu(value).astype(jnp.bfloat16)

    conv_rows(xbuf, w1_ref, stack, rows1, emit_first)
    conv_rows(first_buf, w2_ref, stack, rows1 - 2, emit_second)


def mix_kernel(coef_ref, fb_ref, fbo_ref, rb_ref, own_ref, par_ref, ra_ref, fa_ref, routed_ref,
               above_ref, frame_ref, below_ref, w3_ref, out_ref, fbuf, mixed_buf, stack):
    halo = below_ref.shape[0] - 1
    block = frame_ref.shape[0]
    fbuf[0:1] = above_ref[halo : halo + 1]
    fbuf[1 : block + 1] = frame_ref[...]
    fbuf[block + 1 :] = below_ref[halo : halo + 1]
    f32 = jnp.float32
    step = stack.shape[0]
    for r0 in range(0, block + 2, step):
        rows = pl.ds(r0, min(step, block + 2 - r0))
        summed = (
            coef_ref[0] * (fb_ref[rows].astype(f32) + fbo_ref[rows].astype(f32))
            + coef_ref[1] * rb_ref[rows].astype(f32)
            + coef_ref[2] * own_ref[rows].astype(f32)
            + coef_ref[3] * par_ref[rows].astype(f32)
            + coef_ref[4] * ra_ref[rows].astype(f32)
            + coef_ref[5] * fa_ref[rows].astype(f32)
            + coef_ref[6] * routed_ref[rows].astype(f32)
        )
        mixed_buf[rows] = (summed * fbuf[rows].astype(f32)).astype(jnp.bfloat16)

    def emit(r0, n, value):
        out_ref[r0 : r0 + n] = value.astype(jnp.bfloat16)

    conv_rows(mixed_buf, w3_ref, stack, block, emit)


def vmem():
    return pl.BlockSpec(memory_space=pltpu.VMEM)


def smem():
    return pl.BlockSpec(memory_space=pltpu.SMEM)


CHUNK = 2


def layers(bounds, above, image, below, w1, w2):
    block, cols, c = image.shape
    halo = below.shape[0] - 1
    rows = block + 2 * halo
    flops = 2 * 9 * c * c * cols * (2 * rows - 6)
    return pl.pallas_call(
        layers_kernel,
        out_shape=jax.ShapeDtypeStruct((rows - 4, cols, c), jnp.bfloat16),
        in_specs=[smem()] + [vmem()] * 5,
        out_specs=vmem(),
        scratch_shapes=[pltpu.VMEM((rows, cols, c), jnp.bfloat16),
                        pltpu.VMEM((rows - 2, cols, c), jnp.bfloat16),
                        pltpu.VMEM((CHUNK, cols, 3 * c), jnp.bfloat16)],
        cost_estimate=pl.CostEstimate(flops=flops, transcendentals=2 * rows * cols * c,
                                      bytes_accessed=4 * rows * cols * c + 4 * 9 * c * c),
    )(bounds, above, image, below, w1, w2)


def mix(coef, fb, fbo, rb, own, par, ra, fa, routed, above, frame, below, w3):
    block, cols, c = frame.shape
    flops = 2 * 9 * c * c * cols * block
    return pl.pallas_call(
        mix_kernel,
        out_shape=jax.ShapeDtypeStruct((block, cols, c), jnp.bfloat16),
        in_specs=[smem()] + [vmem()] * 12,
        out_specs=vmem(),
        scratch_shapes=[pltpu.VMEM((block + 2, cols, c), jnp.bfloat16),
                        pltpu.VMEM((block + 2, cols, c), jnp.bfloat16),
                        pltpu.VMEM((CHUNK, cols, 3 * c), jnp.bfloat16)],
        cost_estimate=pl.CostEstimate(flops=flops, transcendentals=0,
                                      bytes_accessed=18 * (block + 2) * cols * c + 2 * 9 * c * c),
    )(coef, fb, fbo, rb, own, par, ra, fa, routed, above, frame, below, w3)


def shards(
    event_slices,
    frame_features,
    exposure_start,
    exposure_end,
    intersection_us,
    conv_first,
    conv_second,
    conv_frame,
):
    image = event_slices[0]
    frame = frame_features[0]
    block = image.shape[0]
    height = block * lax.axis_size("rows")
    row0 = lax.axis_index("rows") * block

    down = jnp.concatenate([image[block - 3 :], frame[block - 1 :]], axis=0)
    up = jnp.concatenate([image[:3], frame[:1]], axis=0)
    from_above = shifted(down, "rows", 1)
    from_below = shifted(up, "rows", -1)

    count = lax.axis_size("tm")
    t = lax.axis_index("tm")
    intersection = intersection_us[0].astype(jnp.float32)
    window = intersection.shape[0]
    radius = (window - 1) // 2
    slice_index = t + jnp.arange(window, dtype=jnp.int32) - radius
    valid = (slice_index >= exposure_start[0]) & (slice_index <= exposure_end[0])
    weights = jnp.where(valid, intersection, jnp.float32(0.0))
    weights = weights / jnp.sum(weights)
    is_odd = (t % 2) == 1
    partner_weight = jnp.where(is_odd, weights[1], weights[3])
    routed_weight = jnp.where(is_odd, weights[4], weights[0])
    coef = jnp.concatenate([weights[:3], partner_weight[None], weights[3:], routed_weight[None]])
    bounds = jnp.stack([2 - row0, height - row0 + 2]).astype(jnp.int32)
    coef, bounds, image = lax.optimization_barrier((coef, bounds, image))

    second = layers(bounds, from_above, image, from_below, conv_first, conv_second)

    partner = lax.ppermute(second, "tm", [(i, i ^ 1) for i in range(count)])
    if count == 8:
        behind_pairs = [(0, 2), (1, 3), (3, 5), (4, 6), (5, 7)]
        from_ahead = lax.ppermute(second, "tm", [(2, 0), (3, 1), (4, 2), (6, 4), (7, 5)])
        hop = lax.ppermute(second, "tm", [(2, 6), (5, 1)])
        routed = lax.ppermute(hop, "tm", [(6, 4), (1, 3)])
    else:
        behind_pairs = [(i, i + 2) for i in range(count - 2)]
        from_ahead = shifted(second, "tm", -2)
        routed = jnp.zeros_like(second)
    behind_even = lax.ppermute(second, "tm", [(a, b) for a, b in behind_pairs if b % 2 == 0])
    behind_odd = lax.ppermute(second, "tm", [(a, b) for a, b in behind_pairs if b % 2 == 1])
    relay_behind = lax.ppermute(behind_odd, "tm", [(i + 1, i) for i in range(2, count, 2)])
    relay_ahead = lax.ppermute(from_ahead, "tm", [(i, i + 1) for i in range(0, count - 2, 2)])
    result = mix(coef, behind_even, behind_odd, relay_behind, second, partner, relay_ahead, from_ahead,
                 routed, from_above, frame, from_below, conv_frame)
    return result[None]


def solution(mesh):
    return jax.shard_map(
        shards,
        mesh=mesh,
        in_specs=(
            P("tm", "rows", None, None),
            P("tm", "rows", None, None),
            P("tm"),
            P("tm"),
            P("tm", None),
            P(),
            P(),
            P(),
        ),
        out_specs=P("tm", "rows", None, None),
        check_vma=False,
    )
```

```python
import numpy as np
import jax
import jax.numpy as jnp
from jax import lax
from jax.experimental import pallas as pl
from jax.experimental.pallas import tpu as pltpu
from jax.sharding import PartitionSpec as P


def shifted(value, axis, steps):
    count = lax.axis_size(axis)
    initial, last = (max(0, -steps), min(count, count - steps))
    pairs = [(source, source + steps) for source in range(initial, last)]
    if not pairs:
        return jnp.zeros_like(value)
    return lax.ppermute(value, axis, pairs)


def gelu(v):
    c = np.float32(np.sqrt(2 / np.pi))
    k = np.float32(np.sqrt(2 / np.pi) * 0.044715)
    h = 0.5 * v
    return h + h * jnp.tanh(v * (c + k * (v * v)))


def conv_rows(src_ref, w_ref, stack, rows_out, emit):
    chunk = stack.shape[0]
    cols, cin = src_ref.shape[1], src_ref.shape[2]
    cout = w_ref.shape[3]
    r0 = 0
    while r0 < rows_out:
        n = min(chunk, rows_out - r0)
        m = n * cols
        for a in range(3):
            stack[0:n, :, a * cin : (a + 1) * cin] = src_ref[r0 + a : r0 + a + n]
        lhs = stack[0:n].reshape(m, 3 * cin)
        taps = [
            jnp.dot(lhs, w_ref[:, b].reshape(3 * cin, cout), preferred_element_type=jnp.float32)
            for b in range(3)
        ]
        col = lax.broadcasted_iota(jnp.int32, (n, cols, cout), 1).reshape(m, cout)
        left = pltpu.roll(taps[0], shift=1, axis=0)
        right = pltpu.roll(taps[2], shift=m - 1, axis=0)
        out = taps[1] + jnp.where(col == 0, 0.0, left) + jnp.where(col == cols - 1, 0.0, right)
        emit(r0, n, out.reshape(n, cols, cout))
        r0 += n


def layers_kernel(bounds_ref, above_ref, image_ref, below_ref, w1_ref, w2_ref, out_ref, xbuf,
                  first_buf, stack):
    halo = below_ref.shape[0] - 1
    block = image_ref.shape[0]
    xbuf[0:halo] = above_ref[0:halo]
    xbuf[halo : halo + block] = image_ref[...]
    xbuf[halo + block :] = below_ref[0:halo]
    rows1 = block + 2 * halo - 2

    def emit_first(r0, n, value):
        value = gelu(value)
        row = lax.broadcasted_iota(jnp.int32, value.shape, 0) + r0
        inside = (row >= bounds_ref[0]) & (row < bounds_ref[1])
        first_buf[r0 : r0 + n] = jnp.where(inside, value, 0.0).astype(jnp.bfloat16)

    def emit_second(r0, n, value):
        out_ref[r0 : r0 + n] = gelu(value).astype(jnp.bfloat16)

    conv_rows(xbuf, w1_ref, stack, rows1, emit_first)
    conv_rows(first_buf, w2_ref, stack, rows1 - 2, emit_second)


def mix_kernel(coef_ref, fb_ref, fbo_ref, rb_ref, own_ref, par_ref, ra_ref, fa_ref, routed_ref,
               above_ref, frame_ref, below_ref, w3_ref, out_ref, fbuf, mixed_buf, stack):
    halo = below_ref.shape[0] - 1
    block = frame_ref.shape[0]
    fbuf[0:1] = above_ref[halo : halo + 1]
    fbuf[1 : block + 1] = frame_ref[...]
    fbuf[block + 1 :] = below_ref[halo : halo + 1]
    f32 = jnp.float32
    step = stack.shape[0]
    for r0 in range(0, block + 2, step):
        rows = pl.ds(r0, min(step, block + 2 - r0))
        summed = (
            coef_ref[0] * (fb_ref[rows].astype(f32) + fbo_ref[rows].astype(f32))
            + coef_ref[1] * rb_ref[rows].astype(f32)
            + coef_ref[2] * own_ref[rows].astype(f32)
            + coef_ref[3] * par_ref[rows].astype(f32)
            + coef_ref[4] * ra_ref[rows].astype(f32)
            + coef_ref[5] * fa_ref[rows].astype(f32)
            + coef_ref[6] * routed_ref[rows].astype(f32)
        )
        mixed_buf[rows] = (summed * fbuf[rows].astype(f32)).astype(jnp.bfloat16)

    def emit(r0, n, value):
        out_ref[r0 : r0 + n] = value.astype(jnp.bfloat16)

    conv_rows(mixed_buf, w3_ref, stack, block, emit)


def vmem():
    return pl.BlockSpec(memory_space=pltpu.VMEM)


def smem():
    return pl.BlockSpec(memory_space=pltpu.SMEM)


CHUNK = 2


def layers(bounds, above, image, below, w1, w2):
    block, cols, c = image.shape
    halo = below.shape[0] - 1
    rows = block + 2 * halo
    flops = 2 * 9 * c * c * cols * (2 * rows - 6)
    return pl.pallas_call(
        layers_kernel,
        out_shape=jax.ShapeDtypeStruct((rows - 4, cols, c), jnp.bfloat16),
        in_specs=[smem()] + [vmem()] * 5,
        out_specs=vmem(),
        scratch_shapes=[pltpu.VMEM((rows, cols, c), jnp.bfloat16),
                        pltpu.VMEM((rows - 2, cols, c), jnp.bfloat16),
                        pltpu.VMEM((CHUNK, cols, 3 * c), jnp.bfloat16)],
        cost_estimate=pl.CostEstimate(flops=flops, transcendentals=2 * rows * cols * c,
                                      bytes_accessed=4 * rows * cols * c + 4 * 9 * c * c),
    )(bounds, above, image, below, w1, w2)


def mix(coef, fb, fbo, rb, own, par, ra, fa, routed, above, frame, below, w3):
    block, cols, c = frame.shape
    flops = 2 * 9 * c * c * cols * block
    return pl.pallas_call(
        mix_kernel,
        out_shape=jax.ShapeDtypeStruct((block, cols, c), jnp.bfloat16),
        in_specs=[smem()] + [vmem()] * 12,
        out_specs=vmem(),
        scratch_shapes=[pltpu.VMEM((block + 2, cols, c), jnp.bfloat16),
                        pltpu.VMEM((block + 2, cols, c), jnp.bfloat16),
                        pltpu.VMEM((2 * CHUNK, cols, 3 * c), jnp.bfloat16)],
        cost_estimate=pl.CostEstimate(flops=flops, transcendentals=0,
                                      bytes_accessed=18 * (block + 2) * cols * c + 2 * 9 * c * c),
    )(coef, fb, fbo, rb, own, par, ra, fa, routed, above, frame, below, w3)


def shards(
    event_slices,
    frame_features,
    exposure_start,
    exposure_end,
    intersection_us,
    conv_first,
    conv_second,
    conv_frame,
):
    image = event_slices[0]
    frame = frame_features[0]
    block = image.shape[0]
    height = block * lax.axis_size("rows")
    row0 = lax.axis_index("rows") * block

    down = jnp.concatenate([image[block - 3 :], frame[block - 1 :]], axis=0)
    up = jnp.concatenate([image[:3], frame[:1]], axis=0)
    from_above = shifted(down, "rows", 1)
    from_below = shifted(up, "rows", -1)

    count = lax.axis_size("tm")
    t = lax.axis_index("tm")
    intersection = intersection_us[0].astype(jnp.float32)
    window = intersection.shape[0]
    radius = (window - 1) // 2
    slice_index = t + jnp.arange(window, dtype=jnp.int32) - radius
    valid = (slice_index >= exposure_start[0]) & (slice_index <= exposure_end[0])
    weights = jnp.where(valid, intersection, jnp.float32(0.0))
    weights = weights / jnp.sum(weights)
    is_odd = (t % 2) == 1
    partner_weight = jnp.where(is_odd, weights[1], weights[3])
    routed_weight = jnp.where(is_odd, weights[4], weights[0])
    coef = jnp.concatenate([weights[:3], partner_weight[None], weights[3:], routed_weight[None]])
    bounds = jnp.stack([2 - row0, height - row0 + 2]).astype(jnp.int32)
    coef, bounds, image = lax.optimization_barrier((coef, bounds, image))

    second = layers(bounds, from_above, image, from_below, conv_first, conv_second)

    partner = lax.ppermute(second, "tm", [(i, i ^ 1) for i in range(count)])
    if count == 8:
        behind_pairs = [(0, 2), (1, 3), (3, 5), (4, 6), (5, 7)]
        from_ahead = lax.ppermute(second, "tm", [(2, 0), (3, 1), (4, 2), (6, 4), (7, 5)])
        hop = lax.ppermute(second, "tm", [(2, 6), (5, 1)])
        routed = lax.ppermute(hop, "tm", [(6, 4), (1, 3)])
    else:
        behind_pairs = [(i, i + 2) for i in range(count - 2)]
        from_ahead = shifted(second, "tm", -2)
        routed = jnp.zeros_like(second)
    behind_even = lax.ppermute(second, "tm", [(a, b) for a, b in behind_pairs if b % 2 == 0])
    behind_odd = lax.ppermute(second, "tm", [(a, b) for a, b in behind_pairs if b % 2 == 1])
    relay_behind = lax.ppermute(behind_odd, "tm", [(i + 1, i) for i in range(2, count, 2)])
    relay_ahead = lax.ppermute(from_ahead, "tm", [(i, i + 1) for i in range(0, count - 2, 2)])
    result = mix(coef, behind_even, behind_odd, relay_behind, second, partner, relay_ahead, from_ahead,
                 routed, from_above, frame, from_below, conv_frame)
    return result[None]


def solution(mesh):
    return jax.shard_map(
        shards,
        mesh=mesh,
        in_specs=(
            P("tm", "rows", None, None),
            P("tm", "rows", None, None),
            P("tm"),
            P("tm"),
            P("tm", None),
            P(),
            P(),
            P(),
        ),
        out_specs=P("tm", "rows", None, None),
        check_vma=False,
    )
```

```python
import numpy as np
import jax
import jax.numpy as jnp
from jax import lax
from jax.experimental import pallas as pl
from jax.experimental.pallas import tpu as pltpu
from jax.sharding import PartitionSpec as P


def shifted(value, axis, steps):
    count = lax.axis_size(axis)
    initial, last = (max(0, -steps), min(count, count - steps))
    pairs = [(source, source + steps) for source in range(initial, last)]
    if not pairs:
        return jnp.zeros_like(value)
    return lax.ppermute(value, axis, pairs)


def gelu(v):
    c = np.float32(np.sqrt(2 / np.pi))
    k = np.float32(np.sqrt(2 / np.pi) * 0.044715)
    h = 0.5 * v
    return h + h * jnp.tanh(v * (c + k * (v * v)))


def conv_rows(src_ref, w_ref, stack, rows_out, emit):
    chunk = stack.shape[0]
    cols, cin = src_ref.shape[1], src_ref.shape[2]
    cout = w_ref.shape[3]
    r0 = 0
    while r0 < rows_out:
        n = min(chunk, rows_out - r0)
        m = n * cols
        for a in range(3):
            stack[0:n, :, a * cin : (a + 1) * cin] = src_ref[r0 + a : r0 + a + n]
        lhs = stack[0:n].reshape(m, 3 * cin)
        taps = [
            jnp.dot(lhs, w_ref[:, b].reshape(3 * cin, cout), preferred_element_type=jnp.float32)
            for b in range(3)
        ]
        col = lax.broadcasted_iota(jnp.int32, (n, cols, cout), 1).reshape(m, cout)
        left = pltpu.roll(taps[0], shift=1, axis=0)
        right = pltpu.roll(taps[2], shift=m - 1, axis=0)
        out = taps[1] + jnp.where(col == 0, 0.0, left) + jnp.where(col == cols - 1, 0.0, right)
        emit(r0, n, out.reshape(n, cols, cout))
        r0 += n


def layers_kernel(bounds_ref, above_ref, image_ref, below_ref, w1_ref, w2_ref, out_ref, xbuf,
                  first_buf, stack):
    halo = below_ref.shape[0] - 1
    block = image_ref.shape[0]
    xbuf[0:halo] = above_ref[0:halo]
    xbuf[halo : halo + block] = image_ref[...]
    xbuf[halo + block :] = below_ref[0:halo]
    rows1 = block + 2 * halo - 2

    def emit_first(r0, n, value):
        value = gelu(value)
        row = lax.broadcasted_iota(jnp.int32, value.shape, 0) + r0
        inside = (row >= bounds_ref[0]) & (row < bounds_ref[1])
        first_buf[r0 : r0 + n] = jnp.where(inside, value, 0.0).astype(jnp.bfloat16)

    def emit_second(r0, n, value):
        out_ref[r0 : r0 + n] = gelu(value).astype(jnp.bfloat16)

    conv_rows(xbuf, w1_ref, stack, rows1, emit_first)
    conv_rows(first_buf, w2_ref, stack, rows1 - 2, emit_second)


def mix_kernel(coef_ref, fb_ref, fbo_ref, rb_ref, own_ref, par_ref, ra_ref, fa_ref, routed_ref,
               above_ref, frame_ref, below_ref, w3_ref, out_ref, fbuf, mixed_buf, stack):
    halo = below_ref.shape[0] - 1
    block = frame_ref.shape[0]
    fbuf[0:1] = above_ref[halo : halo + 1]
    fbuf[1 : block + 1] = frame_ref[...]
    fbuf[block + 1 :] = below_ref[halo : halo + 1]
    f32 = jnp.float32
    step = stack.shape[0]
    for r0 in range(0, block + 2, step):
        rows = pl.ds(r0, min(step, block + 2 - r0))
        summed = (
            coef_ref[7] * fb_ref[rows].astype(f32)
            + coef_ref[0] * fbo_ref[rows].astype(f32)
            + coef_ref[1] * rb_ref[rows].astype(f32)
            + coef_ref[2] * own_ref[rows].astype(f32)
            + coef_ref[3] * par_ref[rows].astype(f32)
            + coef_ref[4] * ra_ref[rows].astype(f32)
            + coef_ref[5] * fa_ref[rows].astype(f32)
            + coef_ref[6] * routed_ref[rows].astype(f32)
        )
        mixed_buf[rows] = (summed * fbuf[rows].astype(f32)).astype(jnp.bfloat16)

    def emit(r0, n, value):
        out_ref[r0 : r0 + n] = value.astype(jnp.bfloat16)

    conv_rows(mixed_buf, w3_ref, stack, block, emit)


def vmem():
    return pl.BlockSpec(memory_space=pltpu.VMEM)


def smem():
    return pl.BlockSpec(memory_space=pltpu.SMEM)


CHUNK = 2


def layers(bounds, above, image, below, w1, w2):
    block, cols, c = image.shape
    halo = below.shape[0] - 1
    rows = block + 2 * halo
    flops = 2 * 9 * c * c * cols * (2 * rows - 6)
    return pl.pallas_call(
        layers_kernel,
        out_shape=jax.ShapeDtypeStruct((rows - 4, cols, c), jnp.bfloat16),
        in_specs=[smem()] + [vmem()] * 5,
        out_specs=vmem(),
        scratch_shapes=[pltpu.VMEM((rows, cols, c), jnp.bfloat16),
                        pltpu.VMEM((rows - 2, cols, c), jnp.bfloat16),
                        pltpu.VMEM((CHUNK, cols, 3 * c), jnp.bfloat16)],
        cost_estimate=pl.CostEstimate(flops=flops, transcendentals=2 * rows * cols * c,
                                      bytes_accessed=4 * rows * cols * c + 4 * 9 * c * c),
    )(bounds, above, image, below, w1, w2)


def mix(coef, fb, fbo, rb, own, par, ra, fa, routed, above, frame, below, w3):
    block, cols, c = frame.shape
    flops = 2 * 9 * c * c * cols * block
    return pl.pallas_call(
        mix_kernel,
        out_shape=jax.ShapeDtypeStruct((block, cols, c), jnp.bfloat16),
        in_specs=[smem()] + [vmem()] * 12,
        out_specs=vmem(),
        scratch_shapes=[pltpu.VMEM((block + 2, cols, c), jnp.bfloat16),
                        pltpu.VMEM((block + 2, cols, c), jnp.bfloat16),
                        pltpu.VMEM((CHUNK, cols, 3 * c), jnp.bfloat16)],
        cost_estimate=pl.CostEstimate(flops=flops, transcendentals=0,
                                      bytes_accessed=18 * (block + 2) * cols * c + 2 * 9 * c * c),
    )(coef, fb, fbo, rb, own, par, ra, fa, routed, above, frame, below, w3)


def shards(
    event_slices,
    frame_features,
    exposure_start,
    exposure_end,
    intersection_us,
    conv_first,
    conv_second,
    conv_frame,
):
    image = event_slices[0]
    frame = frame_features[0]
    block = image.shape[0]
    height = block * lax.axis_size("rows")
    row0 = lax.axis_index("rows") * block

    down = jnp.concatenate([image[block - 3 :], frame[block - 1 :]], axis=0)
    up = jnp.concatenate([image[:3], frame[:1]], axis=0)
    from_above = shifted(down, "rows", 1)
    from_below = shifted(up, "rows", -1)

    count = lax.axis_size("tm")
    t = lax.axis_index("tm")
    intersection = intersection_us[0].astype(jnp.float32)
    window = intersection.shape[0]
    radius = (window - 1) // 2
    slice_index = t + jnp.arange(window, dtype=jnp.int32) - radius
    valid = (slice_index >= exposure_start[0]) & (slice_index <= exposure_end[0])
    weights = jnp.where(valid, intersection, jnp.float32(0.0))
    weights = weights / jnp.sum(weights)
    is_odd = (t % 2) == 1
    partner_weight = jnp.where(is_odd, weights[1], weights[3])
    routed_weight = jnp.where(is_odd, weights[4], weights[0])
    mixed_weight = jnp.where(is_odd, weights[4], weights[0])
    coef = jnp.concatenate([weights[:3], partner_weight[None], weights[3:], routed_weight[None],
                            mixed_weight[None]])
    bounds = jnp.stack([2 - row0, height - row0 + 2]).astype(jnp.int32)
    coef, bounds, image = lax.optimization_barrier((coef, bounds, image))

    second = layers(bounds, from_above, image, from_below, conv_first, conv_second)

    partner = lax.ppermute(second, "tm", [(i, i ^ 1) for i in range(count)])
    if count == 8:
        behind_pairs = [(0, 2), (1, 3), (3, 5), (4, 6), (5, 7)]
        ahead_pairs = [(2, 0), (3, 1), (4, 2), (6, 4), (7, 5)]
        hop = lax.ppermute(second, "tm", [(2, 6), (5, 1)])
        routed = lax.ppermute(hop, "tm", [(6, 4), (1, 3)])
    else:
        behind_pairs = [(i, i + 2) for i in range(count - 2)]
        ahead_pairs = [(i + 2, i) for i in range(count - 2)]
        routed = jnp.zeros_like(second)
    behind_even = lax.ppermute(second, "tm", [(a, b) for a, b in behind_pairs if b % 2 == 0]
                               + [(a, b) for a, b in ahead_pairs if b % 2 == 1])
    from_ahead = lax.ppermute(second, "tm", [(a, b) for a, b in ahead_pairs if b % 2 == 0])
    behind_odd = lax.ppermute(second, "tm", [(a, b) for a, b in behind_pairs if b % 2 == 1])
    relay_behind = lax.ppermute(behind_odd, "tm", [(i + 1, i) for i in range(2, count, 2)])
    relay_ahead = lax.ppermute(from_ahead, "tm", [(i, i + 1) for i in range(0, count - 2, 2)])
    result = mix(coef, behind_even, behind_odd, relay_behind, second, partner, relay_ahead, from_ahead,
                 routed, from_above, frame, from_below, conv_frame)
    return result[None]


def solution(mesh):
    return jax.shard_map(
        shards,
        mesh=mesh,
        in_specs=(
            P("tm", "rows", None, None),
            P("tm", "rows", None, None),
            P("tm"),
            P("tm"),
            P("tm", None),
            P(),
            P(),
            P(),
        ),
        out_specs=P("tm", "rows", None, None),
        check_vma=False,
    )
```

```python
import numpy as np
import jax
import jax.numpy as jnp
from jax import lax
from jax.experimental import pallas as pl
from jax.experimental.pallas import tpu as pltpu
from jax.sharding import PartitionSpec as P


def shifted(value, axis, steps):
    count = lax.axis_size(axis)
    initial, last = (max(0, -steps), min(count, count - steps))
    pairs = [(source, source + steps) for source in range(initial, last)]
    if not pairs:
        return jnp.zeros_like(value)
    return lax.ppermute(value, axis, pairs)


def gelu(v):
    c = np.float32(np.sqrt(2 / np.pi))
    k = np.float32(np.sqrt(2 / np.pi) * 0.044715)
    h = 0.5 * v
    return h + h * jnp.tanh(v * (c + k * (v * v)))


def conv_rows(src_ref, w_ref, stack, rows_out, emit):
    chunk = stack.shape[0]
    cols, cin = src_ref.shape[1], src_ref.shape[2]
    cout = w_ref.shape[3]
    r0 = 0
    while r0 < rows_out:
        n = min(chunk, rows_out - r0)
        m = n * cols
        for a in range(3):
            stack[0:n, :, a * cin : (a + 1) * cin] = src_ref[r0 + a : r0 + a + n]
        lhs = stack[0:n].reshape(m, 3 * cin)
        taps = [
            jnp.dot(lhs, w_ref[:, b].reshape(3 * cin, cout), preferred_element_type=jnp.float32)
            for b in range(3)
        ]
        col = lax.broadcasted_iota(jnp.int32, (n, cols, cout), 1).reshape(m, cout)
        left = pltpu.roll(taps[0], shift=1, axis=0)
        right = pltpu.roll(taps[2], shift=m - 1, axis=0)
        out = taps[1] + jnp.where(col == 0, 0.0, left) + jnp.where(col == cols - 1, 0.0, right)
        emit(r0, n, out.reshape(n, cols, cout))
        r0 += n


def layers_kernel(bounds_ref, above_ref, image_ref, below_ref, w1_ref, w2_ref, out_ref, xbuf,
                  first_buf, stack):
    halo = below_ref.shape[0] - 1
    block = image_ref.shape[0]
    xbuf[0:halo] = above_ref[0:halo]
    xbuf[halo : halo + block] = image_ref[...]
    xbuf[halo + block :] = below_ref[0:halo]
    rows1 = block + 2 * halo - 2

    def emit_first(r0, n, value):
        value = gelu(value)
        row = lax.broadcasted_iota(jnp.int32, value.shape, 0) + r0
        inside = (row >= bounds_ref[0]) & (row < bounds_ref[1])
        first_buf[r0 : r0 + n] = jnp.where(inside, value, 0.0).astype(jnp.bfloat16)

    def emit_second(r0, n, value):
        out_ref[r0 : r0 + n] = gelu(value).astype(jnp.bfloat16)

    conv_rows(xbuf, w1_ref, stack, rows1, emit_first)
    conv_rows(first_buf, w2_ref, stack, rows1 - 2, emit_second)


def mix_kernel(coef_ref, fb_ref, fbo_ref, rb_ref, own_ref, par_ref, ra_ref, fa_ref, routed_ref,
               above_ref, frame_ref, below_ref, w3_ref, out_ref, fbuf, mixed_buf, stack):
    halo = below_ref.shape[0] - 1
    block = frame_ref.shape[0]
    fbuf[0:1] = above_ref[halo : halo + 1]
    fbuf[1 : block + 1] = frame_ref[...]
    fbuf[block + 1 :] = below_ref[halo : halo + 1]
    f32 = jnp.float32
    step = stack.shape[0]
    for r0 in range(0, block + 2, step):
        rows = pl.ds(r0, min(step, block + 2 - r0))
        summed = (
            coef_ref[0] * (fb_ref[rows] + fbo_ref[rows]).astype(f32)
            + coef_ref[7] * (rb_ref[rows] + ra_ref[rows]).astype(f32)
            + coef_ref[2] * own_ref[rows].astype(f32)
            + coef_ref[3] * par_ref[rows].astype(f32)
            + coef_ref[5] * fa_ref[rows].astype(f32)
            + coef_ref[6] * routed_ref[rows].astype(f32)
        )
        mixed_buf[rows] = (summed * fbuf[rows].astype(f32)).astype(jnp.bfloat16)

    def emit(r0, n, value):
        out_ref[r0 : r0 + n] = value.astype(jnp.bfloat16)

    conv_rows(mixed_buf, w3_ref, stack, block, emit)


def vmem():
    return pl.BlockSpec(memory_space=pltpu.VMEM)


def smem():
    return pl.BlockSpec(memory_space=pltpu.SMEM)


CHUNK = 2


def layers(bounds, above, image, below, w1, w2):
    block, cols, c = image.shape
    halo = below.shape[0] - 1
    rows = block + 2 * halo
    flops = 2 * 9 * c * c * cols * (2 * rows - 6)
    return pl.pallas_call(
        layers_kernel,
        out_shape=jax.ShapeDtypeStruct((rows - 4, cols, c), jnp.bfloat16),
        in_specs=[smem()] + [vmem()] * 5,
        out_specs=vmem(),
        scratch_shapes=[pltpu.VMEM((rows, cols, c), jnp.bfloat16),
                        pltpu.VMEM((rows - 2, cols, c), jnp.bfloat16),
                        pltpu.VMEM((CHUNK, cols, 3 * c), jnp.bfloat16)],
        cost_estimate=pl.CostEstimate(flops=flops, transcendentals=2 * rows * cols * c,
                                      bytes_accessed=4 * rows * cols * c + 4 * 9 * c * c),
    )(bounds, above, image, below, w1, w2)


def mix(coef, fb, fbo, rb, own, par, ra, fa, routed, above, frame, below, w3):
    block, cols, c = frame.shape
    flops = 2 * 9 * c * c * cols * block
    return pl.pallas_call(
        mix_kernel,
        out_shape=jax.ShapeDtypeStruct((block, cols, c), jnp.bfloat16),
        in_specs=[smem()] + [vmem()] * 12,
        out_specs=vmem(),
        scratch_shapes=[pltpu.VMEM((block + 2, cols, c), jnp.bfloat16),
                        pltpu.VMEM((block + 2, cols, c), jnp.bfloat16),
                        pltpu.VMEM((CHUNK, cols, 3 * c), jnp.bfloat16)],
        cost_estimate=pl.CostEstimate(flops=flops, transcendentals=0,
                                      bytes_accessed=18 * (block + 2) * cols * c + 2 * 9 * c * c),
    )(coef, fb, fbo, rb, own, par, ra, fa, routed, above, frame, below, w3)


def shards(
    event_slices,
    frame_features,
    exposure_start,
    exposure_end,
    intersection_us,
    conv_first,
    conv_second,
    conv_frame,
):
    image = event_slices[0]
    frame = frame_features[0]
    block = image.shape[0]
    height = block * lax.axis_size("rows")
    row0 = lax.axis_index("rows") * block

    down = jnp.concatenate([image[block - 3 :], frame[block - 1 :]], axis=0)
    up = jnp.concatenate([image[:3], frame[:1]], axis=0)
    from_above = shifted(down, "rows", 1)
    from_below = shifted(up, "rows", -1)

    count = lax.axis_size("tm")
    t = lax.axis_index("tm")
    intersection = intersection_us[0].astype(jnp.float32)
    window = intersection.shape[0]
    radius = (window - 1) // 2
    slice_index = t + jnp.arange(window, dtype=jnp.int32) - radius
    valid = (slice_index >= exposure_start[0]) & (slice_index <= exposure_end[0])
    weights = jnp.where(valid, intersection, jnp.float32(0.0))
    weights = weights / jnp.sum(weights)
    is_odd = (t % 2) == 1
    partner_weight = jnp.where(is_odd, weights[1], weights[3])
    routed_weight = jnp.where(is_odd, weights[4], weights[0])
    relay_weight = jnp.where(is_odd, weights[3], weights[1])
    coef = jnp.concatenate([weights[:3], partner_weight[None], weights[3:], routed_weight[None],
                            relay_weight[None]])
    bounds = jnp.stack([2 - row0, height - row0 + 2]).astype(jnp.int32)
    coef, bounds, image = lax.optimization_barrier((coef, bounds, image))

    second = layers(bounds, from_above, image, from_below, conv_first, conv_second)

    partner = lax.ppermute(second, "tm", [(i, i ^ 1) for i in range(count)])
    if count == 8:
        behind_pairs = [(0, 2), (1, 3), (3, 5), (4, 6), (5, 7)]
        from_ahead = lax.ppermute(second, "tm", [(2, 0), (3, 1), (4, 2), (6, 4), (7, 5)])
        hop = lax.ppermute(second, "tm", [(2, 6), (5, 1)])
        routed = lax.ppermute(hop, "tm", [(6, 4), (1, 3)])
    else:
        behind_pairs = [(i, i + 2) for i in range(count - 2)]
        from_ahead = shifted(second, "tm", -2)
        routed = jnp.zeros_like(second)
    behind_even = lax.ppermute(second, "tm", [(a, b) for a, b in behind_pairs if b % 2 == 0])
    behind_odd = lax.ppermute(second, "tm", [(a, b) for a, b in behind_pairs if b % 2 == 1])
    relay_behind = lax.ppermute(behind_odd, "tm", [(i + 1, i) for i in range(2, count, 2)])
    relay_ahead = lax.ppermute(from_ahead, "tm", [(i, i + 1) for i in range(0, count - 2, 2)])
    result = mix(coef, behind_even, behind_odd, relay_behind, second, partner, relay_ahead, from_ahead,
                 routed, from_above, frame, from_below, conv_frame)
    return result[None]


def solution(mesh):
    return jax.shard_map(
        shards,
        mesh=mesh,
        in_specs=(
            P("tm", "rows", None, None),
            P("tm", "rows", None, None),
            P("tm"),
            P("tm"),
            P("tm", None),
            P(),
            P(),
            P(),
        ),
        out_specs=P("tm", "rows", None, None),
        check_vma=False,
    )
```

```python
import numpy as np
import jax
import jax.numpy as jnp
from jax import lax
from jax.experimental import pallas as pl
from jax.experimental.pallas import tpu as pltpu
from jax.sharding import PartitionSpec as P


def shifted(value, axis, steps):
    count = lax.axis_size(axis)
    initial, last = (max(0, -steps), min(count, count - steps))
    pairs = [(source, source + steps) for source in range(initial, last)]
    if not pairs:
        return jnp.zeros_like(value)
    return lax.ppermute(value, axis, pairs)


def gelu(v):
    c = np.float32(np.sqrt(2 / np.pi))
    k = np.float32(np.sqrt(2 / np.pi) * 0.044715)
    h = 0.5 * v
    return h + h * jnp.tanh(v * (c + k * (v * v)))


def conv_rows(src_ref, w_ref, stack, rows_out, emit):
    chunk = stack.shape[0]
    cols, cin = src_ref.shape[1], src_ref.shape[2]
    cout = w_ref.shape[3]
    r0 = 0
    while r0 < rows_out:
        n = min(chunk, rows_out - r0)
        m = n * cols
        for a in range(3):
            stack[0:n, :, a * cin : (a + 1) * cin] = src_ref[r0 + a : r0 + a + n]
        lhs = stack[0:n].reshape(m, 3 * cin)
        taps = [
            jnp.dot(lhs, w_ref[:, b].reshape(3 * cin, cout), preferred_element_type=jnp.float32)
            for b in range(3)
        ]
        col = lax.broadcasted_iota(jnp.int32, (n, cols, cout), 1).reshape(m, cout)
        left = pltpu.roll(taps[0], shift=1, axis=0)
        right = pltpu.roll(taps[2], shift=m - 1, axis=0)
        out = taps[1] + jnp.where(col == 0, 0.0, left) + jnp.where(col == cols - 1, 0.0, right)
        emit(r0, n, out.reshape(n, cols, cout))
        r0 += n


def layers_kernel(bounds_ref, above_hbm, image_hbm, below_hbm, w1_ref, w2_ref, out_ref, xbuf,
                  first_buf, stack, sems):
    halo = below_hbm.shape[0] - 1
    block = image_hbm.shape[0]
    copies = [
        pltpu.make_async_copy(above_hbm.at[0:halo], xbuf.at[0:halo], sems.at[0]),
        pltpu.make_async_copy(image_hbm, xbuf.at[halo : halo + block], sems.at[1]),
        pltpu.make_async_copy(below_hbm.at[0:halo], xbuf.at[halo + block :], sems.at[2]),
    ]
    for c in copies:
        c.start()
    for c in copies:
        c.wait()
    rows1 = block + 2 * halo - 2

    def emit_first(r0, n, value):
        value = gelu(value)
        row = lax.broadcasted_iota(jnp.int32, value.shape, 0) + r0
        inside = (row >= bounds_ref[0]) & (row < bounds_ref[1])
        first_buf[r0 : r0 + n] = jnp.where(inside, value, 0.0).astype(jnp.bfloat16)

    def emit_second(r0, n, value):
        out_ref[r0 : r0 + n] = gelu(value).astype(jnp.bfloat16)

    conv_rows(xbuf, w1_ref, stack, rows1, emit_first)
    conv_rows(first_buf, w2_ref, stack, rows1 - 2, emit_second)


def mix_kernel(coef_ref, fb_ref, fbo_ref, rb_ref, own_ref, par_ref, ra_ref, fa_ref, routed_ref,
               above_ref, frame_ref, below_ref, w3_ref, out_ref, fbuf, mixed_buf, stack):
    halo = below_ref.shape[0] - 1
    block = frame_ref.shape[0]
    fbuf[0:1] = above_ref[halo : halo + 1]
    fbuf[1 : block + 1] = frame_ref[...]
    fbuf[block + 1 :] = below_ref[halo : halo + 1]
    f32 = jnp.float32
    step = stack.shape[0]
    for r0 in range(0, block + 2, step):
        rows = pl.ds(r0, min(step, block + 2 - r0))
        summed = (
            coef_ref[0] * (fb_ref[rows].astype(f32) + fbo_ref[rows].astype(f32))
            + coef_ref[1] * rb_ref[rows].astype(f32)
            + coef_ref[2] * own_ref[rows].astype(f32)
            + coef_ref[3] * par_ref[rows].astype(f32)
            + coef_ref[4] * ra_ref[rows].astype(f32)
            + coef_ref[5] * fa_ref[rows].astype(f32)
            + coef_ref[6] * routed_ref[rows].astype(f32)
        )
        mixed_buf[rows] = (summed * fbuf[rows].astype(f32)).astype(jnp.bfloat16)

    def emit(r0, n, value):
        out_ref[r0 : r0 + n] = value.astype(jnp.bfloat16)

    conv_rows(mixed_buf, w3_ref, stack, block, emit)


def vmem():
    return pl.BlockSpec(memory_space=pltpu.VMEM)


def smem():
    return pl.BlockSpec(memory_space=pltpu.SMEM)


CHUNK = 2


def layers(bounds, above, image, below, w1, w2):
    block, cols, c = image.shape
    halo = below.shape[0] - 1
    rows = block + 2 * halo
    flops = 2 * 9 * c * c * cols * (2 * rows - 6)
    return pl.pallas_call(
        layers_kernel,
        out_shape=jax.ShapeDtypeStruct((rows - 4, cols, c), jnp.bfloat16),
        in_specs=[smem()] + [pl.BlockSpec(memory_space=pl.ANY)] * 3 + [vmem()] * 2,
        out_specs=vmem(),
        scratch_shapes=[pltpu.VMEM((rows, cols, c), jnp.bfloat16),
                        pltpu.VMEM((rows - 2, cols, c), jnp.bfloat16),
                        pltpu.VMEM((CHUNK, cols, 3 * c), jnp.bfloat16),
                        pltpu.SemaphoreType.DMA((3,))],
        cost_estimate=pl.CostEstimate(flops=flops, transcendentals=2 * rows * cols * c,
                                      bytes_accessed=4 * rows * cols * c + 4 * 9 * c * c),
    )(bounds, above, image, below, w1, w2)


def mix(coef, fb, fbo, rb, own, par, ra, fa, routed, above, frame, below, w3):
    block, cols, c = frame.shape
    flops = 2 * 9 * c * c * cols * block
    return pl.pallas_call(
        mix_kernel,
        out_shape=jax.ShapeDtypeStruct((block, cols, c), jnp.bfloat16),
        in_specs=[smem()] + [vmem()] * 12,
        out_specs=vmem(),
        scratch_shapes=[pltpu.VMEM((block + 2, cols, c), jnp.bfloat16),
                        pltpu.VMEM((block + 2, cols, c), jnp.bfloat16),
                        pltpu.VMEM((CHUNK, cols, 3 * c), jnp.bfloat16)],
        cost_estimate=pl.CostEstimate(flops=flops, transcendentals=0,
                                      bytes_accessed=18 * (block + 2) * cols * c + 2 * 9 * c * c),
    )(coef, fb, fbo, rb, own, par, ra, fa, routed, above, frame, below, w3)


def shards(
    event_slices,
    frame_features,
    exposure_start,
    exposure_end,
    intersection_us,
    conv_first,
    conv_second,
    conv_frame,
):
    image = event_slices[0]
    frame = frame_features[0]
    block = image.shape[0]
    height = block * lax.axis_size("rows")
    row0 = lax.axis_index("rows") * block

    down = jnp.concatenate([image[block - 3 :], frame[block - 1 :]], axis=0)
    up = jnp.concatenate([image[:3], frame[:1]], axis=0)
    from_above = shifted(down, "rows", 1)
    from_below = shifted(up, "rows", -1)

    count = lax.axis_size("tm")
    t = lax.axis_index("tm")
    intersection = intersection_us[0].astype(jnp.float32)
    window = intersection.shape[0]
    radius = (window - 1) // 2
    slice_index = t + jnp.arange(window, dtype=jnp.int32) - radius
    valid = (slice_index >= exposure_start[0]) & (slice_index <= exposure_end[0])
    weights = jnp.where(valid, intersection, jnp.float32(0.0))
    weights = weights / jnp.sum(weights)
    is_odd = (t % 2) == 1
    partner_weight = jnp.where(is_odd, weights[1], weights[3])
    routed_weight = jnp.where(is_odd, weights[4], weights[0])
    coef = jnp.concatenate([weights[:3], partner_weight[None], weights[3:], routed_weight[None]])
    bounds = jnp.stack([2 - row0, height - row0 + 2]).astype(jnp.int32)
    coef, bounds, image = lax.optimization_barrier((coef, bounds, image))

    second = layers(bounds, from_above, image, from_below, conv_first, conv_second)

    partner = lax.ppermute(second, "tm", [(i, i ^ 1) for i in range(count)])
    if count == 8:
        behind_pairs = [(0, 2), (1, 3), (3, 5), (4, 6), (5, 7)]
        from_ahead = lax.ppermute(second, "tm", [(2, 0), (3, 1), (4, 2), (6, 4), (7, 5)])
        hop = lax.ppermute(second, "tm", [(2, 6), (5, 1)])
        routed = lax.ppermute(hop, "tm", [(6, 4), (1, 3)])
    else:
        behind_pairs = [(i, i + 2) for i in range(count - 2)]
        from_ahead = shifted(second, "tm", -2)
        routed = jnp.zeros_like(second)
    behind_even = lax.ppermute(second, "tm", [(a, b) for a, b in behind_pairs if b % 2 == 0])
    behind_odd = lax.ppermute(second, "tm", [(a, b) for a, b in behind_pairs if b % 2 == 1])
    relay_behind = lax.ppermute(behind_odd, "tm", [(i + 1, i) for i in range(2, count, 2)])
    relay_ahead = lax.ppermute(from_ahead, "tm", [(i, i + 1) for i in range(0, count - 2, 2)])
    result = mix(coef, behind_even, behind_odd, relay_behind, second, partner, relay_ahead, from_ahead,
                 routed, from_above, frame, from_below, conv_frame)
    return result[None]


def solution(mesh):
    return jax.shard_map(
        shards,
        mesh=mesh,
        in_specs=(
            P("tm", "rows", None, None),
            P("tm", "rows", None, None),
            P("tm"),
            P("tm"),
            P("tm", None),
            P(),
            P(),
            P(),
        ),
        out_specs=P("tm", "rows", None, None),
        check_vma=False,
    )
```

```python
import numpy as np
import jax
import jax.numpy as jnp
from jax import lax
from jax.experimental import pallas as pl
from jax.experimental.pallas import tpu as pltpu
from jax.sharding import PartitionSpec as P


def shifted(value, axis, steps):
    count = lax.axis_size(axis)
    initial, last = (max(0, -steps), min(count, count - steps))
    pairs = [(source, source + steps) for source in range(initial, last)]
    if not pairs:
        return jnp.zeros_like(value)
    return lax.ppermute(value, axis, pairs)


def gelu(v):
    c = np.float32(np.sqrt(2 / np.pi))
    k = np.float32(np.sqrt(2 / np.pi) * 0.044715)
    h = 0.5 * v
    return h + h * jnp.tanh(v * (c + k * (v * v)))


def conv_rows(src_ref, w_ref, stack, rows_out, emit):
    chunk = stack.shape[0]
    cols, cin = src_ref.shape[1], src_ref.shape[2]
    cout = w_ref.shape[3]
    r0 = 0
    while r0 < rows_out:
        n = min(chunk, rows_out - r0)
        m = n * cols
        for a in range(3):
            stack[0:n, :, a * cin : (a + 1) * cin] = src_ref[r0 + a : r0 + a + n]
        lhs = stack[0:n].reshape(m, 3 * cin)
        taps = [
            jnp.dot(lhs, w_ref[:, b].reshape(3 * cin, cout), preferred_element_type=jnp.float32)
            for b in range(3)
        ]
        col = lax.broadcasted_iota(jnp.int32, (n, cols, cout), 1).reshape(m, cout)
        left = pltpu.roll(taps[0], shift=1, axis=0)
        right = pltpu.roll(taps[2], shift=m - 1, axis=0)
        out = taps[1] + jnp.where(col == 0, 0.0, left) + jnp.where(col == cols - 1, 0.0, right)
        emit(r0, n, out.reshape(n, cols, cout))
        r0 += n


def layers_kernel(bounds_ref, above_ref, image_ref, below_ref, w1_ref, w2_ref, out_ref, xbuf,
                  first_buf, stack):
    halo = below_ref.shape[0] - 1
    block = image_ref.shape[0]
    xbuf[0:halo] = above_ref[0:halo]
    xbuf[halo : halo + block] = image_ref[...]
    xbuf[halo + block :] = below_ref[0:halo]
    rows1 = block + 2 * halo - 2

    def emit_first(r0, n, value):
        value = gelu(value)
        row = lax.broadcasted_iota(jnp.int32, value.shape, 0) + r0
        inside = (row >= bounds_ref[0]) & (row < bounds_ref[1])
        first_buf[r0 : r0 + n] = jnp.where(inside, value, 0.0).astype(jnp.bfloat16)

    def emit_second(r0, n, value):
        out_ref[r0 : r0 + n] = gelu(value).astype(jnp.bfloat16)

    conv_rows(xbuf, w1_ref, stack, rows1, emit_first)
    conv_rows(first_buf, w2_ref, stack, rows1 - 2, emit_second)


def mix_kernel(coef_ref, fb_ref, fbo_ref, rb_ref, own_ref, par_ref, ra_ref, fa_ref, routed_ref,
               above_ref, frame_ref, below_ref, w3_ref, out_ref, fbuf, mixed_buf, stack):
    halo = below_ref.shape[0] - 1
    block = frame_ref.shape[0]
    fbuf[0:1] = above_ref[halo : halo + 1]
    fbuf[1 : block + 1] = frame_ref[...]
    fbuf[block + 1 :] = below_ref[halo : halo + 1]
    f32 = jnp.float32
    step = stack.shape[0]
    for r0 in range(0, block + 2, step):
        rows = pl.ds(r0, min(step, block + 2 - r0))
        summed = (
            coef_ref[0] * (fb_ref[rows].astype(f32) + fbo_ref[rows].astype(f32))
            + coef_ref[1] * rb_ref[rows].astype(f32)
            + coef_ref[2] * own_ref[rows].astype(f32)
            + coef_ref[3] * par_ref[rows].astype(f32)
            + coef_ref[4] * ra_ref[rows].astype(f32)
            + coef_ref[5] * fa_ref[rows].astype(f32)
            + coef_ref[6] * routed_ref[rows].astype(f32)
        )
        mixed_buf[rows] = (summed * fbuf[rows].astype(f32)).astype(jnp.bfloat16)

    def emit(r0, n, value):
        out_ref[r0 : r0 + n] = value.astype(jnp.bfloat16)

    conv_rows(mixed_buf, w3_ref, stack, block, emit)


def vmem():
    return pl.BlockSpec(memory_space=pltpu.VMEM)


def smem():
    return pl.BlockSpec(memory_space=pltpu.SMEM)


CHUNK = 2


def layers(bounds, above, image, below, w1, w2):
    block, cols, c = image.shape
    halo = below.shape[0] - 1
    rows = block + 2 * halo
    flops = 2 * 9 * c * c * cols * (2 * rows - 6)
    return pl.pallas_call(
        layers_kernel,
        out_shape=jax.ShapeDtypeStruct((rows - 4, cols, c), jnp.bfloat16),
        in_specs=[smem()] + [vmem()] * 5,
        out_specs=vmem(),
        scratch_shapes=[pltpu.VMEM((rows, cols, c), jnp.bfloat16),
                        pltpu.VMEM((rows - 2, cols, c), jnp.bfloat16),
                        pltpu.VMEM((1, cols, 3 * c), jnp.bfloat16)],
        cost_estimate=pl.CostEstimate(flops=flops, transcendentals=2 * rows * cols * c,
                                      bytes_accessed=4 * rows * cols * c + 4 * 9 * c * c),
    )(bounds, above, image, below, w1, w2)


def mix(coef, fb, fbo, rb, own, par, ra, fa, routed, above, frame, below, w3):
    block, cols, c = frame.shape
    flops = 2 * 9 * c * c * cols * block
    return pl.pallas_call(
        mix_kernel,
        out_shape=jax.ShapeDtypeStruct((block, cols, c), jnp.bfloat16),
        in_specs=[smem()] + [vmem()] * 12,
        out_specs=vmem(),
        scratch_shapes=[pltpu.VMEM((block + 2, cols, c), jnp.bfloat16),
                        pltpu.VMEM((block + 2, cols, c), jnp.bfloat16),
                        pltpu.VMEM((CHUNK, cols, 3 * c), jnp.bfloat16)],
        cost_estimate=pl.CostEstimate(flops=flops, transcendentals=0,
                                      bytes_accessed=18 * (block + 2) * cols * c + 2 * 9 * c * c),
    )(coef, fb, fbo, rb, own, par, ra, fa, routed, above, frame, below, w3)


def shards(
    event_slices,
    frame_features,
    exposure_start,
    exposure_end,
    intersection_us,
    conv_first,
    conv_second,
    conv_frame,
):
    image = event_slices[0]
    frame = frame_features[0]
    block = image.shape[0]
    height = block * lax.axis_size("rows")
    row0 = lax.axis_index("rows") * block

    down = jnp.concatenate([image[block - 3 :], frame[block - 1 :]], axis=0)
    up = jnp.concatenate([image[:3], frame[:1]], axis=0)
    from_above = shifted(down, "rows", 1)
    from_below = shifted(up, "rows", -1)

    count = lax.axis_size("tm")
    t = lax.axis_index("tm")
    intersection = intersection_us[0].astype(jnp.float32)
    window = intersection.shape[0]
    radius = (window - 1) // 2
    slice_index = t + jnp.arange(window, dtype=jnp.int32) - radius
    valid = (slice_index >= exposure_start[0]) & (slice_index <= exposure_end[0])
    weights = jnp.where(valid, intersection, jnp.float32(0.0))
    weights = weights / jnp.sum(weights)
    is_odd = (t % 2) == 1
    partner_weight = jnp.where(is_odd, weights[1], weights[3])
    routed_weight = jnp.where(is_odd, weights[4], weights[0])
    coef = jnp.concatenate([weights[:3], partner_weight[None], weights[3:], routed_weight[None]])
    bounds = jnp.stack([2 - row0, height - row0 + 2]).astype(jnp.int32)
    coef, bounds, image = lax.optimization_barrier((coef, bounds, image))

    second = layers(bounds, from_above, image, from_below, conv_first, conv_second)

    partner = lax.ppermute(second, "tm", [(i, i ^ 1) for i in range(count)])
    if count == 8:
        behind_pairs = [(0, 2), (1, 3), (3, 5), (4, 6), (5, 7)]
        from_ahead = lax.ppermute(second, "tm", [(2, 0), (3, 1), (4, 2), (6, 4), (7, 5)])
        hop = lax.ppermute(second, "tm", [(2, 6), (5, 1)])
        routed = lax.ppermute(hop, "tm", [(6, 4), (1, 3)])
    else:
        behind_pairs = [(i, i + 2) for i in range(count - 2)]
        from_ahead = shifted(second, "tm", -2)
        routed = jnp.zeros_like(second)
    behind_even = lax.ppermute(second, "tm", [(a, b) for a, b in behind_pairs if b % 2 == 0])
    behind_odd = lax.ppermute(second, "tm", [(a, b) for a, b in behind_pairs if b % 2 == 1])
    relay_behind = lax.ppermute(behind_odd, "tm", [(i + 1, i) for i in range(2, count, 2)])
    relay_ahead = lax.ppermute(from_ahead, "tm", [(i, i + 1) for i in range(0, count - 2, 2)])
    result = mix(coef, behind_even, behind_odd, relay_behind, second, partner, relay_ahead, from_ahead,
                 routed, from_above, frame, from_below, conv_frame)
    return result[None]


def solution(mesh):
    return jax.shard_map(
        shards,
        mesh=mesh,
        in_specs=(
            P("tm", "rows", None, None),
            P("tm", "rows", None, None),
            P("tm"),
            P("tm"),
            P("tm", None),
            P(),
            P(),
            P(),
        ),
        out_specs=P("tm", "rows", None, None),
        check_vma=False,
    )
```

```python
import numpy as np
import jax
import jax.numpy as jnp
from jax import lax
from jax.experimental import pallas as pl
from jax.experimental.pallas import tpu as pltpu
from jax.sharding import PartitionSpec as P


def shifted(value, axis, steps):
    count = lax.axis_size(axis)
    initial, last = (max(0, -steps), min(count, count - steps))
    pairs = [(source, source + steps) for source in range(initial, last)]
    if not pairs:
        return jnp.zeros_like(value)
    return lax.ppermute(value, axis, pairs)


def gelu(v):
    c = np.float32(np.sqrt(2 / np.pi))
    k = np.float32(np.sqrt(2 / np.pi) * 0.044715)
    h = 0.5 * v
    return h + h * jnp.tanh(v * (c + k * (v * v)))


def conv_rows(src_ref, w_ref, stack, rows_out, emit):
    chunk = stack.shape[0]
    cols, cin = src_ref.shape[1], src_ref.shape[2]
    cout = w_ref.shape[3]
    r0 = 0
    while r0 < rows_out:
        n = min(chunk, rows_out - r0)
        m = n * cols
        for a in range(3):
            stack[0:n, :, a * cin : (a + 1) * cin] = src_ref[r0 + a : r0 + a + n]
        lhs = stack[0:n].reshape(m, 3 * cin)
        taps = [
            jnp.dot(lhs, w_ref[:, b].reshape(3 * cin, cout), preferred_element_type=jnp.float32)
            for b in range(3)
        ]
        col = lax.broadcasted_iota(jnp.int32, (n, cols, cout), 1).reshape(m, cout)
        left = pltpu.roll(taps[0], shift=1, axis=0)
        right = pltpu.roll(taps[2], shift=m - 1, axis=0)
        out = taps[1] + jnp.where(col == 0, 0.0, left) + jnp.where(col == cols - 1, 0.0, right)
        emit(r0, n, out.reshape(n, cols, cout))
        r0 += n


def layers_kernel(bounds_ref, above_ref, image_ref, below_ref, w1_ref, w2_ref, out_ref, xbuf,
                  first_buf, stack):
    halo = below_ref.shape[0] - 1
    block = image_ref.shape[0]
    xbuf[0:halo] = above_ref[0:halo]
    xbuf[halo : halo + block] = image_ref[...]
    xbuf[halo + block :] = below_ref[0:halo]
    rows1 = block + 2 * halo - 2

    def emit_first(r0, n, value):
        value = gelu(value)
        row = lax.broadcasted_iota(jnp.int32, value.shape, 0) + r0
        inside = (row >= bounds_ref[0]) & (row < bounds_ref[1])
        first_buf[r0 : r0 + n] = jnp.where(inside, value, 0.0).astype(jnp.bfloat16)

    def emit_second(r0, n, value):
        out_ref[r0 : r0 + n] = gelu(value).astype(jnp.bfloat16)

    conv_rows(xbuf, w1_ref, stack, rows1, emit_first)
    conv_rows(first_buf, w2_ref, stack, rows1 - 2, emit_second)


def mix_kernel(coef_ref, fb_ref, fbo_ref, rb_ref, own_ref, par_ref, ra_ref, fa_ref, routed_ref,
               above_ref, frame_ref, below_ref, w3_ref, out_ref, fbuf, mixed_buf, stack):
    halo = below_ref.shape[0] - 1
    block = frame_ref.shape[0]
    fbuf[0:1] = above_ref[halo : halo + 1]
    fbuf[1 : block + 1] = frame_ref[...]
    fbuf[block + 1 :] = below_ref[halo : halo + 1]
    f32 = jnp.float32
    step = stack.shape[0]
    for r0 in range(0, block + 2, step):
        rows = pl.ds(r0, min(step, block + 2 - r0))
        summed = (
            coef_ref[0] * (fb_ref[rows].astype(f32) + fbo_ref[rows].astype(f32))
            + coef_ref[1] * rb_ref[rows].astype(f32)
            + coef_ref[2] * own_ref[rows].astype(f32)
            + coef_ref[3] * par_ref[rows].astype(f32)
            + coef_ref[4] * ra_ref[rows].astype(f32)
            + coef_ref[5] * fa_ref[rows].astype(f32)
            + coef_ref[6] * routed_ref[rows].astype(f32)
        )
        mixed_buf[rows] = (summed * fbuf[rows].astype(f32)).astype(jnp.bfloat16)

    def emit(r0, n, value):
        out_ref[r0 : r0 + n] = value.astype(jnp.bfloat16)

    conv_rows(mixed_buf, w3_ref, stack, block, emit)


def vmem():
    return pl.BlockSpec(memory_space=pltpu.VMEM)


def smem():
    return pl.BlockSpec(memory_space=pltpu.SMEM)


CHUNK = 2


def layers(bounds, above, image, below, w1, w2):
    block, cols, c = image.shape
    halo = below.shape[0] - 1
    rows = block + 2 * halo
    flops = 2 * 9 * c * c * cols * (2 * rows - 6)
    return pl.pallas_call(
        layers_kernel,
        out_shape=jax.ShapeDtypeStruct((rows - 4, cols, c), jnp.bfloat16),
        in_specs=[smem()] + [vmem()] * 5,
        out_specs=vmem(),
        scratch_shapes=[pltpu.VMEM((rows, cols, c), jnp.bfloat16),
                        pltpu.VMEM((rows - 2, cols, c), jnp.bfloat16),
                        pltpu.VMEM((CHUNK, cols, 3 * c), jnp.bfloat16)],
        cost_estimate=pl.CostEstimate(flops=flops, transcendentals=2 * rows * cols * c,
                                      bytes_accessed=4 * rows * cols * c + 4 * 9 * c * c),
    )(bounds, above, image, below, w1, w2)


def mix(coef, fb, fbo, rb, own, par, ra, fa, routed, above, frame, below, w3):
    block, cols, c = frame.shape
    flops = 2 * 9 * c * c * cols * block
    return pl.pallas_call(
        mix_kernel,
        out_shape=jax.ShapeDtypeStruct((block, cols, c), jnp.bfloat16),
        in_specs=[smem()] + [vmem()] * 12,
        out_specs=vmem(),
        scratch_shapes=[pltpu.VMEM((block + 2, cols, c), jnp.bfloat16),
                        pltpu.VMEM((block + 2, cols, c), jnp.bfloat16),
                        pltpu.VMEM((1, cols, 3 * c), jnp.bfloat16)],
        cost_estimate=pl.CostEstimate(flops=flops, transcendentals=0,
                                      bytes_accessed=18 * (block + 2) * cols * c + 2 * 9 * c * c),
    )(coef, fb, fbo, rb, own, par, ra, fa, routed, above, frame, below, w3)


def shards(
    event_slices,
    frame_features,
    exposure_start,
    exposure_end,
    intersection_us,
    conv_first,
    conv_second,
    conv_frame,
):
    image = event_slices[0]
    frame = frame_features[0]
    block = image.shape[0]
    height = block * lax.axis_size("rows")
    row0 = lax.axis_index("rows") * block

    down = jnp.concatenate([image[block - 3 :], frame[block - 1 :]], axis=0)
    up = jnp.concatenate([image[:3], frame[:1]], axis=0)
    from_above = shifted(down, "rows", 1)
    from_below = shifted(up, "rows", -1)

    count = lax.axis_size("tm")
    t = lax.axis_index("tm")
    intersection = intersection_us[0].astype(jnp.float32)
    window = intersection.shape[0]
    radius = (window - 1) // 2
    slice_index = t + jnp.arange(window, dtype=jnp.int32) - radius
    valid = (slice_index >= exposure_start[0]) & (slice_index <= exposure_end[0])
    weights = jnp.where(valid, intersection, jnp.float32(0.0))
    weights = weights / jnp.sum(weights)
    is_odd = (t % 2) == 1
    partner_weight = jnp.where(is_odd, weights[1], weights[3])
    routed_weight = jnp.where(is_odd, weights[4], weights[0])
    coef = jnp.concatenate([weights[:3], partner_weight[None], weights[3:], routed_weight[None]])
    bounds = jnp.stack([2 - row0, height - row0 + 2]).astype(jnp.int32)
    coef, bounds, image = lax.optimization_barrier((coef, bounds, image))

    second = layers(bounds, from_above, image, from_below, conv_first, conv_second)

    partner = lax.ppermute(second, "tm", [(i, i ^ 1) for i in range(count)])
    if count == 8:
        behind_pairs = [(0, 2), (1, 3), (3, 5), (4, 6), (5, 7)]
        from_ahead = lax.ppermute(second, "tm", [(2, 0), (3, 1), (4, 2), (6, 4), (7, 5)])
        hop = lax.ppermute(second, "tm", [(2, 6), (5, 1)])
        routed = lax.ppermute(hop, "tm", [(6, 4), (1, 3)])
    else:
        behind_pairs = [(i, i + 2) for i in range(count - 2)]
        from_ahead = shifted(second, "tm", -2)
        routed = jnp.zeros_like(second)
    behind_even = lax.ppermute(second, "tm", [(a, b) for a, b in behind_pairs if b % 2 == 0])
    behind_odd = lax.ppermute(second, "tm", [(a, b) for a, b in behind_pairs if b % 2 == 1])
    relay_behind = lax.ppermute(behind_odd, "tm", [(i + 1, i) for i in range(2, count, 2)])
    relay_ahead = lax.ppermute(from_ahead, "tm", [(i, i + 1) for i in range(0, count - 2, 2)])
    result = mix(coef, behind_even, behind_odd, relay_behind, second, partner, relay_ahead, from_ahead,
                 routed, from_above, frame, from_below, conv_frame)
    return result[None]


def solution(mesh):
    return jax.shard_map(
        shards,
        mesh=mesh,
        in_specs=(
            P("tm", "rows", None, None),
            P("tm", "rows", None, None),
            P("tm"),
            P("tm"),
            P("tm", None),
            P(),
            P(),
            P(),
        ),
        out_specs=P("tm", "rows", None, None),
        check_vma=False,
    )
```
